256 devices in a mesh: sx: 8 (over z_hi, x), sy: 4 (over z_lo), af: 8 (over y, core).
Axes of the slice: x: 4, y: 4, z: 8 (z_hi: 2, z_lo: 4; z = z_hi * 4 + z_lo), core: 2. Of those that a mesh axis runs over, the one named last changes fastest.
Arguments:
- volume: bfloat16 [8, 48, 48, 48, 128], P('af', 'sx', 'sy'), may hold values from -6 to 6
- kernel: bfloat16 [3, 3, 3, 128, 256], P(None, None, None, 'sx', ('sy', 'af')), may hold values from -0.109375 to 0.109375
- cotangent: bfloat16 [8, 256, 24, 576], P('sx', ('sy', 'af')), may hold values from -6 to 6
Outputs:
- features: bfloat16 [8, 256, 24, 576], P('sx', ('sy', 'af'))
- volume_grad: bfloat16 [8, 48, 48, 48, 128], P('af', 'sx', 'sy')
- kernel_grad: float32 [3, 3, 3, 128, 256], P(None, None, None, 'sx', ('sy', 'af'))
The draws below stay inside these ranges and needn't reach their ends.
All inputs are finite; a program needn't handle non-finite values.
Results may differ from the reference program's by a relative error of at most 0.0025.
Values may be sent and summed in bfloat16 or wider, within the bound.
A program may use at most 64 MiB of HBM per device.

```python
import jax
import jax.numpy as jnp
from jax import lax

GRID = 48
CIN = 128
COUT = 256
SAMPLES = 8
OUTG = 24


def level_of(stream_key, extent, shards, low, largest):
    level, own = 1.0, jax.random.fold_in(stream_key, 6)
    for position, shards_of in shards:
        draws = jnp.exp(jax.random.uniform(jax.random.fold_in(own, position), (shards_of,), jnp.float32, low / len(shards), largest / len(shards)))
        level = level * jnp.repeat(draws, extent[position] // shards_of).reshape([-1 if axis == position else 1 for axis in range(len(extent))])
    return level


def noise(own_key, shape, deviation, bound, shards=(), kind=jnp.bfloat16):
    level = level_of(own_key, shape, shards, -0.22, 0.18) if shards else 1.0
    result = jax.random.normal(own_key, shape, jnp.float32) * deviation * level
    return jnp.minimum(jnp.maximum(result, -bound), bound).astype(kind)


def setup_inputs(seed: int = 0) -> dict:
    splits = jax.random.split(jax.random.key(seed), 4)
    return {
        "volume": noise(splits[0], (SAMPLES, GRID, GRID, GRID, CIN), 1.0, 6.0, ((0, 8), (1, 8), (2, 4))),
        "kernel": noise(splits[1], (3, 3, 3, CIN, COUT), (27 * CIN) ** -0.5, 0.109375, ((3, 8), (4, 32))),
        "cotangent": noise(splits[2], (SAMPLES, COUT, OUTG, OUTG * OUTG), 1.0, 6.0, ((0, 8), (1, 32))),
    }


def convolve(volume_f, kernel_f):
    return lax.conv_general_dilated(volume_f, kernel_f, (2, 2, 2), ((1, 1), (1, 1), (1, 1)), dimension_numbers=('NDHWC', 'DHWIO', 'NDHWC'), precision=lax.Precision.HIGHEST)

def reference(volume, kernel, cotangent):
    volume_f = volume.astype(jnp.float32)
    kernel_f = kernel.astype(jnp.float32)
    conv, pullback = jax.vjp(convolve, volume_f, kernel_f)
    samples = volume.shape[0]
    edge = conv.shape[1]
    features = conv.astype(jnp.bfloat16).transpose(0, 4, 1, 2, 3).reshape(samples, COUT, edge, edge * edge)
    grad_out = cotangent.astype(jnp.float32).reshape(samples, COUT, edge, edge, edge).transpose(0, 2, 3, 4, 1)
    volume_grad, kernel_grad = pullback(grad_out)
    return (features, volume_grad.astype(jnp.bfloat16), kernel_grad.astype(jnp.float32))
```

```python
import jax
import jax.numpy as jnp
from jax import lax
from jax.sharding import PartitionSpec as P


def from_behind(value, axis, steps):
    count = lax.axis_size(axis)
    leading, last = (max(0, -steps), min(count, count - steps))
    return lax.ppermute(value, axis, [(source, source + steps) for source in range(leading, last)])


def strided_patch(extended, tap_d, tap_h, tap_w, depth, height, width):
    return extended[
        :,
        tap_d : tap_d + 2 * depth : 2,
        tap_h : tap_h + 2 * height : 2,
        tap_w : tap_w + 2 * width : 2,
        :,
    ]


def parity_view(extended):
    samples, d_ext, h_ext, w_ext, channels = extended.shape
    pads = [(0, 0)] + [(0, n % 2) for n in (d_ext, h_ext, w_ext)] + [(0, 0)]
    even = jnp.pad(extended, pads)
    _, d2, h2, w2, _ = even.shape
    split = even.reshape(samples, d2 // 2, 2, h2 // 2, 2, w2 // 2, 2, channels)
    return split.transpose(2, 4, 6, 0, 1, 3, 5, 7)


def im2col(classes, depth, height, width):
    patches = []
    for tap_d in range(3):
        for tap_h in range(3):
            for tap_w in range(3):
                cls = classes[tap_d % 2, tap_h % 2, tap_w % 2]
                od, oh, ow = tap_d // 2, tap_h // 2, tap_w // 2
                patches.append(cls[:, od : od + depth, oh : oh + height, ow : ow + width, :])
    return jnp.concatenate(patches, axis=-1)


def weave(even_part, odd_part, axis):
    stacked = jnp.stack([even_part, odd_part], axis=axis + 1)
    shape = list(even_part.shape)
    shape[axis] = shape[axis] * 2
    return stacked.reshape(shape)


def spread_back(grad_space, kernel_full):
    samples, depth, height, width, filters = grad_space.shape
    channels = kernel_full.shape[3]
    grad_flat = grad_space.reshape(-1, filters)
    classes = {}
    for tap_d in range(3):
        for tap_h in range(3):
            for tap_w in range(3):
                term = lax.dot_general(
                    grad_flat,
                    kernel_full[tap_d, tap_h, tap_w],
                    (((1,), (1,)), ((), ())),
                    preferred_element_type=jnp.float32,
                )
                term = term.reshape(samples, depth, height, width, channels)
                pads = [(0, 0)]
                for tap in (tap_d, tap_h, tap_w):
                    pads.append((1, 0) if tap == 2 else (0, 1))
                pads.append((0, 0))
                term = jnp.pad(term, pads)
                key_name = (tap_d % 2, tap_h % 2, tap_w % 2)
                classes[key_name] = classes[key_name] + term if key_name in classes else term
    planes = []
    for parity_d in range(2):
        rows_h = []
        for parity_h in range(2):
            rows_h.append(weave(classes[parity_d, parity_h, 0], classes[parity_d, parity_h, 1], 3))
        planes.append(weave(rows_h[0], rows_h[1], 2))
    whole = weave(planes[0], planes[1], 1)
    return whole[:, : 2 * depth + 1, : 2 * height + 1, : 2 * width + 1, :]


def on_device(volume, kernel, cotangent):
    samples = volume.shape[0]
    depth = volume.shape[1] // 2
    height = volume.shape[2] // 2
    width = volume.shape[3] // 2
    n_sy = lax.axis_size("sy")
    n_af = lax.axis_size("af")
    kernel_part = lax.all_gather(kernel, ("sy", "af"), axis=4, tiled=True)
    kernel_full = lax.all_gather(kernel_part, "sx", axis=3, tiled=True)
    filters = kernel_full.shape[4]
    per_dev = filters // (n_sy * n_af)
    below = from_behind(volume[:, -1:], "sx", 1)
    extended = jnp.concatenate([below, volume], axis=1)
    beside = from_behind(extended[:, :, -1:], "sy", 1)
    extended = jnp.concatenate([beside, extended], axis=2)
    extended = jnp.pad(extended, ((0, 0), (0, 0), (0, 0), (1, 0), (0, 0)))
    rows = samples * depth * height * width
    classes = parity_view(extended)
    cols = im2col(classes, depth, height, width).reshape(rows, -1)
    kernel_mat = kernel_full.reshape(-1, filters)
    total = jnp.dot(cols, kernel_mat, preferred_element_type=jnp.float32)
    conv_space = total.astype(jnp.bfloat16).reshape(
        samples, depth, height, width, n_sy, n_af, per_dev
    )
    by_sample = lax.all_to_all(conv_space, "af", split_axis=5, concat_axis=0, tiled=True)
    gathered = lax.all_to_all(
        lax.all_to_all(by_sample, "sx", split_axis=0, concat_axis=1, tiled=True),
        "sy",
        split_axis=4,
        concat_axis=2,
        tiled=True,
    )
    own_samples = gathered.shape[0]
    edge_d = gathered.shape[1]
    edge_h = gathered.shape[2]
    features = (
        gathered.reshape(own_samples, edge_d, edge_h, width, per_dev)
        .transpose(0, 4, 1, 2, 3)
        .reshape(own_samples, per_dev, edge_d, edge_h * width)
    )
    grad_after = (
        cotangent.reshape(own_samples, per_dev, edge_d, edge_h, width)
        .transpose(0, 2, 3, 4, 1)
        .reshape(own_samples, edge_d, edge_h, width, 1, 1, per_dev)
    )
    grad_region = lax.all_to_all(
        lax.all_to_all(grad_after, "sx", split_axis=1, concat_axis=0, tiled=True),
        "sy",
        split_axis=2,
        concat_axis=4,
        tiled=True,
    )
    grad_back = lax.all_to_all(grad_region, "af", split_axis=0, concat_axis=5, tiled=True)
    grad_space = grad_back.reshape(samples, depth, height, width, filters)
    grad_flat = grad_space.reshape(rows, filters)
    kernel_terms = lax.dot_general(
        cols, grad_flat, (((0,), (0,)), ((), ())), preferred_element_type=jnp.float32
    )
    n_sx = lax.axis_size("sx")
    channels = kernel_full.shape[3]
    taps = kernel_terms.reshape(27, channels, n_sy * n_af, per_dev).transpose(2, 0, 1, 3)
    by_filter = lax.all_to_all(taps, ("sy", "af"), 0, 0, tiled=True).sum(axis=0)
    own_ch = channels // n_sx
    by_filter = by_filter.reshape(27, n_sx, own_ch, per_dev).transpose(1, 0, 2, 3)
    kernel_grad = lax.all_to_all(by_filter, "sx", 0, 0, tiled=True).sum(axis=0)
    kernel_grad = kernel_grad.reshape(3, 3, 3, own_ch, per_dev)
    partial_grad = spread_back(grad_space, kernel_full)
    from_above = from_behind(partial_grad[:, 0:1], "sx", -1)
    own_depth = partial_grad[:, 1:]
    own_depth = jnp.concatenate([own_depth[:, :-1], own_depth[:, -1:] + from_above], axis=1)
    from_right = from_behind(own_depth[:, :, 0:1].astype(jnp.bfloat16), "sy", -1).astype(
        jnp.float32
    )
    own_height = own_depth[:, :, 1:]
    own_height = jnp.concatenate(
        [own_height[:, :, :-1], own_height[:, :, -1:] + from_right], axis=2
    )
    volume_grad = own_height[:, :, :, 1:]
    return (features, volume_grad.astype(jnp.bfloat16), kernel_grad)


def solution(mesh):
    return jax.shard_map(
        on_device,
        mesh=mesh,
        in_specs=(
            P("af", "sx", "sy", None, None),
            P(None, None, None, "sx", ("sy", "af")),
            P("sx", ("sy", "af"), None, None),
        ),
        out_specs=(
            P("sx", ("sy", "af"), None, None),
            P("af", "sx", "sy", None, None),
            P(None, None, None, "sx", ("sy", "af")),
        ),
        check_vma=False,
    )
```

```python
import jax
import jax.numpy as jnp
from jax import lax
from jax.sharding import PartitionSpec as P


def from_behind(value, axis, steps):
    count = lax.axis_size(axis)
    leading, last = (max(0, -steps), min(count, count - steps))
    return lax.ppermute(value, axis, [(source, source + steps) for source in range(leading, last)])


def strided_patch(extended, tap_d, tap_h, tap_w, depth, height, width):
    return extended[
        :,
        tap_d : tap_d + 2 * depth : 2,
        tap_h : tap_h + 2 * height : 2,
        tap_w : tap_w + 2 * width : 2,
        :,
    ]


def parity_view(extended):
    samples, d_ext, h_ext, w_ext, channels = extended.shape
    pads = [(0, 0)] + [(0, n % 2) for n in (d_ext, h_ext, w_ext)] + [(0, 0)]
    even = jnp.pad(extended, pads)
    _, d2, h2, w2, _ = even.shape
    split = even.reshape(samples, d2 // 2, 2, h2 // 2, 2, w2 // 2, 2, channels)
    return split.transpose(2, 4, 6, 0, 1, 3, 5, 7)


def im2col(classes, depth, height, width):
    patches = []
    for tap_d in range(3):
        for tap_h in range(3):
            for tap_w in range(3):
                cls = classes[tap_d % 2, tap_h % 2, tap_w % 2]
                od, oh, ow = tap_d // 2, tap_h // 2, tap_w // 2
                patches.append(cls[:, od : od + depth, oh : oh + height, ow : ow + width, :])
    return jnp.concatenate(patches, axis=-1)


def weave(even_part, odd_part, axis):
    stacked = jnp.stack([even_part, odd_part], axis=axis + 1)
    shape = list(even_part.shape)
    shape[axis] = shape[axis] * 2
    return stacked.reshape(shape)


def spread_back(grad_space, kernel_full):
    samples, depth, height, width, filters = grad_space.shape
    channels = kernel_full.shape[3]
    grad_flat = grad_space.reshape(-1, filters)
    classes = {}
    for tap_d in range(3):
        for tap_h in range(3):
            for tap_w in range(3):
                term = lax.dot_general(
                    grad_flat,
                    kernel_full[tap_d, tap_h, tap_w],
                    (((1,), (1,)), ((), ())),
                    preferred_element_type=jnp.float32,
                )
                term = term.reshape(samples, depth, height, width, channels)
                pads = [(0, 0)]
                for tap in (tap_d, tap_h, tap_w):
                    pads.append((1, 0) if tap == 2 else (0, 1))
                pads.append((0, 0))
                term = jnp.pad(term, pads)
                key_name = (tap_d % 2, tap_h % 2, tap_w % 2)
                classes[key_name] = classes[key_name] + term if key_name in classes else term
    planes = []
    for parity_d in range(2):
        rows_h = []
        for parity_h in range(2):
            rows_h.append(weave(classes[parity_d, parity_h, 0], classes[parity_d, parity_h, 1], 3))
        planes.append(weave(rows_h[0], rows_h[1], 2))
    whole = weave(planes[0], planes[1], 1)
    return whole[:, : 2 * depth + 1, : 2 * height + 1, : 2 * width + 1, :]


def on_device(volume, kernel, cotangent):
    samples = volume.shape[0]
    depth = volume.shape[1] // 2
    height = volume.shape[2] // 2
    width = volume.shape[3] // 2
    n_sy = lax.axis_size("sy")
    n_af = lax.axis_size("af")
    kernel_part = lax.all_gather(kernel, ("sy", "af"), axis=4, tiled=True)
    kernel_full = lax.all_gather(kernel_part, "sx", axis=3, tiled=True)
    filters = kernel_full.shape[4]
    per_dev = filters // (n_sy * n_af)
    below = from_behind(volume[:, -1:], "sx", 1)
    extended = jnp.concatenate([below, volume], axis=1)
    beside = from_behind(extended[:, :, -1:], "sy", 1)
    extended = jnp.concatenate([beside, extended], axis=2)
    extended = jnp.pad(extended, ((0, 0), (0, 0), (0, 0), (1, 0), (0, 0)))
    rows = samples * depth * height * width
    classes = parity_view(extended)
    cols = im2col(classes, depth, height, width).reshape(rows, -1)
    kernel_mat = kernel_full.reshape(-1, filters)
    total = jnp.dot(cols, kernel_mat, preferred_element_type=jnp.float32)
    n_sx = lax.axis_size("sx")
    conv_space = total.astype(jnp.bfloat16).reshape(depth, height, width, n_sy, n_af, per_dev)
    by_af = lax.all_to_all(conv_space.transpose(4, 3, 0, 1, 2, 5), "af", 0, 0, tiled=True)
    by_region = by_af.reshape(n_sx * n_sy, depth, height, width, per_dev)
    gathered = lax.all_to_all(by_region, ("sx", "sy"), 0, 0, tiled=True)
    own_samples = cotangent.shape[0]
    features = (
        gathered.reshape(n_sx, n_sy, depth, height, width, per_dev)
        .transpose(5, 0, 2, 1, 3, 4)
        .reshape(cotangent.shape)
    )
    grad_blocks = (
        cotangent.reshape(per_dev, n_sx, depth, n_sy, height, width)
        .transpose(1, 3, 2, 4, 5, 0)
        .reshape(n_sx * n_sy, depth, height, width, per_dev)
    )
    grad_region = lax.all_to_all(grad_blocks, ("sx", "sy"), 0, 0, tiled=True)
    grad_region = grad_region.reshape(n_sx * own_samples, n_sy, depth, height, width, per_dev)
    grad_back = lax.all_to_all(grad_region, "af", 0, 0, tiled=True)
    grad_back = grad_back.transpose(2, 3, 4, 1, 0, 5)
    grad_space = grad_back.reshape(samples, depth, height, width, filters)
    grad_flat = grad_space.reshape(rows, filters)
    kernel_terms = lax.dot_general(
        cols, grad_flat, (((0,), (0,)), ((), ())), preferred_element_type=jnp.float32
    )
    channels = kernel_full.shape[3]
    taps = kernel_terms.reshape(27, channels, n_sy * n_af, per_dev).transpose(2, 0, 1, 3)
    by_filter = lax.all_to_all(taps, ("sy", "af"), 0, 0, tiled=True).sum(axis=0)
    own_ch = channels // n_sx
    by_filter = by_filter.reshape(27, n_sx, own_ch, per_dev).transpose(1, 0, 2, 3)
    kernel_grad = lax.all_to_all(by_filter, "sx", 0, 0, tiled=True).sum(axis=0)
    kernel_grad = kernel_grad.reshape(3, 3, 3, own_ch, per_dev)
    partial_grad = spread_back(grad_space, kernel_full)
    from_above = from_behind(partial_grad[:, 0:1], "sx", -1)
    own_depth = partial_grad[:, 1:]
    own_depth = jnp.concatenate([own_depth[:, :-1], own_depth[:, -1:] + from_above], axis=1)
    from_right = from_behind(own_depth[:, :, 0:1].astype(jnp.bfloat16), "sy", -1).astype(
        jnp.float32
    )
    own_height = own_depth[:, :, 1:]
    own_height = jnp.concatenate(
        [own_height[:, :, :-1], own_height[:, :, -1:] + from_right], axis=2
    )
    volume_grad = own_height[:, :, :, 1:]
    return (features, volume_grad.astype(jnp.bfloat16), kernel_grad)


def solution(mesh):
    return jax.shard_map(
        on_device,
        mesh=mesh,
        in_specs=(
            P("af", "sx", "sy", None, None),
            P(None, None, None, "sx", ("sy", "af")),
            P("sx", ("sy", "af"), None, None),
        ),
        out_specs=(
            P("sx", ("sy", "af"), None, None),
            P("af", "sx", "sy", None, None),
            P(None, None, None, "sx", ("sy", "af")),
        ),
        check_vma=False,
    )
```

```python
import functools

import jax
import jax.numpy as jnp
from jax import lax
from jax.experimental import pallas as pl
from jax.experimental.pallas import tpu as pltpu
from jax.sharding import PartitionSpec as P


def _gather_body(n_sy, n_af, block_ref, out_ref, send_sem, recv_sem):
    group = n_sy * n_af
    sx = lax.axis_index("sx")
    me = lax.axis_index("sy") * n_af + lax.axis_index("af")
    barrier = pltpu.get_barrier_semaphore()
    for step in range(1, group):
        peer = lax.rem(me + step, group)
        pl.semaphore_signal(
            barrier,
            inc=1,
            device_id=(sx, peer // n_af, lax.rem(peer, n_af)),
            device_id_type=pl.DeviceIdType.MESH,
        )
    pl.semaphore_wait(barrier, group - 1)
    copies = []
    for step in range(1, group):
        peer = lax.rem(me + step, group)
        copy = pltpu.make_async_remote_copy(
            src_ref=block_ref,
            dst_ref=out_ref.at[me],
            send_sem=send_sem.at[step - 1],
            recv_sem=recv_sem.at[step - 1],
            device_id=(sx, peer // n_af, lax.rem(peer, n_af)),
            device_id_type=pl.DeviceIdType.MESH,
        )
        copy.start()
        copies.append(copy)
    out_ref[me] = block_ref[...]
    for copy in copies:
        copy.wait_send()
    for step in range(1, group):
        source = lax.rem(me + group - step, group)
        incoming = pltpu.make_async_remote_copy(
            src_ref=block_ref,
            dst_ref=out_ref.at[source],
            send_sem=send_sem.at[step - 1],
            recv_sem=recv_sem.at[step - 1],
            device_id=(sx, source // n_af, lax.rem(source, n_af)),
            device_id_type=pl.DeviceIdType.MESH,
        )
        incoming.wait_recv()


def gather_filters(kernel):
    n_sy = lax.axis_size("sy")
    n_af = lax.axis_size("af")
    group = n_sy * n_af
    taps, channels, per_dev = kernel.shape[0] * kernel.shape[1] * kernel.shape[2], kernel.shape[3], kernel.shape[4]
    block = kernel.reshape(-1, 128)
    gathered = pl.pallas_call(
        functools.partial(_gather_body, n_sy, n_af),
        out_shape=jax.ShapeDtypeStruct((group,) + block.shape, block.dtype),
        in_specs=[pl.BlockSpec(memory_space=pltpu.VMEM)],
        out_specs=pl.BlockSpec(memory_space=pltpu.VMEM),
        scratch_shapes=[
            pltpu.SemaphoreType.DMA((group - 1,)),
            pltpu.SemaphoreType.DMA((group - 1,)),
        ],
        compiler_params=pltpu.CompilerParams(collective_id=0, has_side_effects=True),
    )(block)
    gathered = gathered.reshape(group, taps, channels, per_dev).transpose(1, 2, 0, 3)
    return gathered.reshape(kernel.shape[:4] + (group * per_dev,))


def from_behind(value, axis, steps):
    count = lax.axis_size(axis)
    leading, last = (max(0, -steps), min(count, count - steps))
    return lax.ppermute(value, axis, [(source, source + steps) for source in range(leading, last)])


def strided_patch(extended, tap_d, tap_h, tap_w, depth, height, width):
    return extended[
        :,
        tap_d : tap_d + 2 * depth : 2,
        tap_h : tap_h + 2 * height : 2,
        tap_w : tap_w + 2 * width : 2,
        :,
    ]


def parity_view(extended):
    samples, d_ext, h_ext, w_ext, channels = extended.shape
    pads = [(0, 0)] + [(0, n % 2) for n in (d_ext, h_ext, w_ext)] + [(0, 0)]
    even = jnp.pad(extended, pads)
    _, d2, h2, w2, _ = even.shape
    split = even.reshape(samples, d2 // 2, 2, h2 // 2, 2, w2 // 2, 2, channels)
    return split.transpose(2, 4, 6, 0, 1, 3, 5, 7)


def im2col(classes, depth, height, width):
    patches = []
    for tap_d in range(3):
        for tap_h in range(3):
            for tap_w in range(3):
                cls = classes[tap_d % 2, tap_h % 2, tap_w % 2]
                od, oh, ow = tap_d // 2, tap_h // 2, tap_w // 2
                patches.append(cls[:, od : od + depth, oh : oh + height, ow : ow + width, :])
    return jnp.concatenate(patches, axis=-1)


def weave(even_part, odd_part, axis):
    stacked = jnp.stack([even_part, odd_part], axis=axis + 1)
    shape = list(even_part.shape)
    shape[axis] = shape[axis] * 2
    return stacked.reshape(shape)


def spread_back(grad_space, kernel_full):
    samples, depth, height, width, filters = grad_space.shape
    channels = kernel_full.shape[3]
    grad_flat = grad_space.reshape(-1, filters)
    classes = {}
    for tap_d in range(3):
        for tap_h in range(3):
            for tap_w in range(3):
                term = lax.dot_general(
                    grad_flat,
                    kernel_full[tap_d, tap_h, tap_w],
                    (((1,), (1,)), ((), ())),
                    preferred_element_type=jnp.float32,
                )
                term = term.reshape(samples, depth, height, width, channels)
                pads = [(0, 0)]
                for tap in (tap_d, tap_h, tap_w):
                    pads.append((1, 0) if tap == 2 else (0, 1))
                pads.append((0, 0))
                term = jnp.pad(term, pads)
                key_name = (tap_d % 2, tap_h % 2, tap_w % 2)
                classes[key_name] = classes[key_name] + term if key_name in classes else term
    planes = []
    for parity_d in range(2):
        rows_h = []
        for parity_h in range(2):
            rows_h.append(weave(classes[parity_d, parity_h, 0], classes[parity_d, parity_h, 1], 3))
        planes.append(weave(rows_h[0], rows_h[1], 2))
    whole = weave(planes[0], planes[1], 1)
    return whole[:, : 2 * depth + 1, : 2 * height + 1, : 2 * width + 1, :]


def on_device(volume, kernel, cotangent):
    samples = volume.shape[0]
    depth = volume.shape[1] // 2
    height = volume.shape[2] // 2
    width = volume.shape[3] // 2
    n_sy = lax.axis_size("sy")
    n_af = lax.axis_size("af")
    kernel_part = gather_filters(kernel)
    kernel_full = lax.all_gather(kernel_part, "sx", axis=3, tiled=True)
    filters = kernel_full.shape[4]
    per_dev = filters // (n_sy * n_af)
    below = from_behind(volume[:, -1:], "sx", 1)
    extended = jnp.concatenate([below, volume], axis=1)
    beside = from_behind(extended[:, :, -1:], "sy", 1)
    extended = jnp.concatenate([beside, extended], axis=2)
    extended = jnp.pad(extended, ((0, 0), (0, 0), (0, 0), (1, 0), (0, 0)))
    rows = samples * depth * height * width
    classes = parity_view(extended)
    cols = im2col(classes, depth, height, width).reshape(rows, -1)
    kernel_mat = kernel_full.reshape(-1, filters)
    total = jnp.dot(cols, kernel_mat, preferred_element_type=jnp.float32)
    n_sx = lax.axis_size("sx")
    conv_space = total.astype(jnp.bfloat16).reshape(depth, height, width, n_sy, n_af, per_dev)
    by_af = lax.all_to_all(conv_space.transpose(4, 3, 0, 1, 2, 5), "af", 0, 0, tiled=True)
    by_region = by_af.reshape(n_sx * n_sy, depth, height, width, per_dev)
    gathered = lax.all_to_all(by_region, ("sx", "sy"), 0, 0, tiled=True)
    own_samples = cotangent.shape[0]
    features = (
        gathered.reshape(n_sx, n_sy, depth, height, width, per_dev)
        .transpose(5, 0, 2, 1, 3, 4)
        .reshape(cotangent.shape)
    )
    grad_blocks = (
        cotangent.reshape(per_dev, n_sx, depth, n_sy, height, width)
        .transpose(1, 3, 2, 4, 5, 0)
        .reshape(n_sx * n_sy, depth, height, width, per_dev)
    )
    grad_region = lax.all_to_all(grad_blocks, ("sx", "sy"), 0, 0, tiled=True)
    grad_region = grad_region.reshape(n_sx * own_samples, n_sy, depth, height, width, per_dev)
    grad_back = lax.all_to_all(grad_region, "af", 0, 0, tiled=True)
    grad_back = grad_back.transpose(2, 3, 4, 1, 0, 5)
    grad_space = grad_back.reshape(samples, depth, height, width, filters)
    grad_flat = grad_space.reshape(rows, filters)
    kernel_terms = lax.dot_general(
        cols, grad_flat, (((0,), (0,)), ((), ())), preferred_element_type=jnp.float32
    )
    channels = kernel_full.shape[3]
    taps = kernel_terms.reshape(27, channels, n_sy * n_af, per_dev).transpose(2, 0, 1, 3)
    by_filter = lax.all_to_all(taps, ("sy", "af"), 0, 0, tiled=True).sum(axis=0)
    own_ch = channels // n_sx
    by_filter = by_filter.reshape(27, n_sx, own_ch, per_dev).transpose(1, 0, 2, 3)
    kernel_grad = lax.all_to_all(by_filter, "sx", 0, 0, tiled=True).sum(axis=0)
    kernel_grad = kernel_grad.reshape(3, 3, 3, own_ch, per_dev)
    partial_grad = spread_back(grad_space, kernel_full)
    from_above = from_behind(partial_grad[:, 0:1], "sx", -1)
    own_depth = partial_grad[:, 1:]
    own_depth = jnp.concatenate([own_depth[:, :-1], own_depth[:, -1:] + from_above], axis=1)
    from_right = from_behind(own_depth[:, :, 0:1].astype(jnp.bfloat16), "sy", -1).astype(
        jnp.float32
    )
    own_height = own_depth[:, :, 1:]
    own_height = jnp.concatenate(
        [own_height[:, :, :-1], own_height[:, :, -1:] + from_right], axis=2
    )
    volume_grad = own_height[:, :, :, 1:]
    return (features, volume_grad.astype(jnp.bfloat16), kernel_grad)


def solution(mesh):
    return jax.shard_map(
        on_device,
        mesh=mesh,
        in_specs=(
            P("af", "sx", "sy", None, None),
            P(None, None, None, "sx", ("sy", "af")),
            P("sx", ("sy", "af"), None, None),
        ),
        out_specs=(
            P("sx", ("sy", "af"), None, None),
            P("af", "sx", "sy", None, None),
            P(None, None, None, "sx", ("sy", "af")),
        ),
        check_vma=False,
    )
```

```python
import functools

import jax
import jax.numpy as jnp
from jax import lax
from jax.experimental import pallas as pl
from jax.experimental.pallas import tpu as pltpu
from jax.sharding import PartitionSpec as P


def _gather_body(n_sy, n_af, block_ref, out_ref, send_sem, recv_sem):
    group = n_sy * n_af
    sx = lax.axis_index("sx")
    me = lax.axis_index("sy") * n_af + lax.axis_index("af")
    barrier = pltpu.get_barrier_semaphore()
    for step in range(1, group):
        peer = lax.rem(me + step, group)
        pl.semaphore_signal(
            barrier,
            inc=1,
            device_id=(sx, peer // n_af, lax.rem(peer, n_af)),
            device_id_type=pl.DeviceIdType.MESH,
        )
    pl.semaphore_wait(barrier, group - 1)
    copies = []
    for step in range(1, group):
        peer = lax.rem(me + step, group)
        copy = pltpu.make_async_remote_copy(
            src_ref=block_ref,
            dst_ref=out_ref.at[me],
            send_sem=send_sem.at[step - 1],
            recv_sem=recv_sem.at[step - 1],
            device_id=(sx, peer // n_af, lax.rem(peer, n_af)),
            device_id_type=pl.DeviceIdType.MESH,
        )
        copy.start()
        copies.append(copy)
    out_ref[me] = block_ref[...]
    for copy in copies:
        copy.wait_send()
    for step in range(1, group):
        source = lax.rem(me + group - step, group)
        incoming = pltpu.make_async_remote_copy(
            src_ref=block_ref,
            dst_ref=out_ref.at[source],
            send_sem=send_sem.at[step - 1],
            recv_sem=recv_sem.at[step - 1],
            device_id=(sx, source // n_af, lax.rem(source, n_af)),
            device_id_type=pl.DeviceIdType.MESH,
        )
        incoming.wait_recv()


def _reduce_body(n_sy, n_af, terms_ref, out_ref, held, send_sem, recv_sem):
    group = n_sy * n_af
    rows = out_ref.shape[0]
    sx = lax.axis_index("sx")
    me = lax.axis_index("sy") * n_af + lax.axis_index("af")
    barrier = pltpu.get_barrier_semaphore()
    for step in range(1, group):
        peer = lax.rem(me + step, group)
        pl.semaphore_signal(
            barrier,
            inc=1,
            device_id=(sx, peer // n_af, lax.rem(peer, n_af)),
            device_id_type=pl.DeviceIdType.MESH,
        )
    pl.semaphore_wait(barrier, group - 1)
    copies = []
    for step in range(1, group):
        peer = lax.rem(me + step, group)
        copy = pltpu.make_async_remote_copy(
            src_ref=terms_ref.at[pl.ds(pl.multiple_of(peer * rows, rows), rows)],
            dst_ref=held.at[me],
            send_sem=send_sem.at[step - 1],
            recv_sem=recv_sem.at[step - 1],
            device_id=(sx, peer // n_af, lax.rem(peer, n_af)),
            device_id_type=pl.DeviceIdType.MESH,
        )
        copy.start()
        copies.append(copy)
    total = terms_ref[pl.ds(pl.multiple_of(me * rows, rows), rows), :]
    for copy in copies:
        copy.wait_send()
    for step in range(1, group):
        source = lax.rem(me + group - step, group)
        incoming = pltpu.make_async_remote_copy(
            src_ref=terms_ref.at[pl.ds(0, rows)],
            dst_ref=held.at[source],
            send_sem=send_sem.at[step - 1],
            recv_sem=recv_sem.at[step - 1],
            device_id=(sx, source // n_af, lax.rem(source, n_af)),
            device_id_type=pl.DeviceIdType.MESH,
        )
        incoming.wait_recv()
        total = total + held[source]
    out_ref[...] = total


def reduce_filters(terms):
    n_sy = lax.axis_size("sy")
    n_af = lax.axis_size("af")
    group = n_sy * n_af
    rows = terms.shape[0] // group
    return pl.pallas_call(
        functools.partial(_reduce_body, n_sy, n_af),
        out_shape=jax.ShapeDtypeStruct((rows, terms.shape[1]), terms.dtype),
        in_specs=[pl.BlockSpec(memory_space=pltpu.VMEM)],
        out_specs=pl.BlockSpec(memory_space=pltpu.VMEM),
        scratch_shapes=[
            pltpu.VMEM((group, rows, terms.shape[1]), terms.dtype),
            pltpu.SemaphoreType.DMA((group - 1,)),
            pltpu.SemaphoreType.DMA((group - 1,)),
        ],
        compiler_params=pltpu.CompilerParams(collective_id=1, has_side_effects=True),
    )(terms)


def gather_filters(kernel):
    n_sy = lax.axis_size("sy")
    n_af = lax.axis_size("af")
    group = n_sy * n_af
    taps, channels, per_dev = kernel.shape[0] * kernel.shape[1] * kernel.shape[2], kernel.shape[3], kernel.shape[4]
    block = kernel.reshape(-1, 128)
    gathered = pl.pallas_call(
        functools.partial(_gather_body, n_sy, n_af),
        out_shape=jax.ShapeDtypeStruct((group,) + block.shape, block.dtype),
        in_specs=[pl.BlockSpec(memory_space=pltpu.VMEM)],
        out_specs=pl.BlockSpec(memory_space=pltpu.VMEM),
        scratch_shapes=[
            pltpu.SemaphoreType.DMA((group - 1,)),
            pltpu.SemaphoreType.DMA((group - 1,)),
        ],
        compiler_params=pltpu.CompilerParams(collective_id=0, has_side_effects=True),
    )(block)
    gathered = gathered.reshape(group, taps, channels, per_dev).transpose(1, 2, 0, 3)
    return gathered.reshape(kernel.shape[:4] + (group * per_dev,))


def from_behind(value, axis, steps):
    count = lax.axis_size(axis)
    leading, last = (max(0, -steps), min(count, count - steps))
    return lax.ppermute(value, axis, [(source, source + steps) for source in range(leading, last)])


def strided_patch(extended, tap_d, tap_h, tap_w, depth, height, width):
    return extended[
        :,
        tap_d : tap_d + 2 * depth : 2,
        tap_h : tap_h + 2 * height : 2,
        tap_w : tap_w + 2 * width : 2,
        :,
    ]


def parity_view(extended):
    samples, d_ext, h_ext, w_ext, channels = extended.shape
    pads = [(0, 0)] + [(0, n % 2) for n in (d_ext, h_ext, w_ext)] + [(0, 0)]
    even = jnp.pad(extended, pads)
    _, d2, h2, w2, _ = even.shape
    split = even.reshape(samples, d2 // 2, 2, h2 // 2, 2, w2 // 2, 2, channels)
    return split.transpose(2, 4, 6, 0, 1, 3, 5, 7)


def im2col(classes, depth, height, width):
    patches = []
    for tap_d in range(3):
        for tap_h in range(3):
            for tap_w in range(3):
                cls = classes[tap_d % 2, tap_h % 2, tap_w % 2]
                od, oh, ow = tap_d // 2, tap_h // 2, tap_w // 2
                patches.append(cls[:, od : od + depth, oh : oh + height, ow : ow + width, :])
    return jnp.concatenate(patches, axis=-1)


def weave(even_part, odd_part, axis):
    stacked = jnp.stack([even_part, odd_part], axis=axis + 1)
    shape = list(even_part.shape)
    shape[axis] = shape[axis] * 2
    return stacked.reshape(shape)


def spread_back(grad_space, kernel_full):
    samples, depth, height, width, filters = grad_space.shape
    channels = kernel_full.shape[3]
    grad_flat = grad_space.reshape(-1, filters)
    classes = {}
    for tap_d in range(3):
        for tap_h in range(3):
            for tap_w in range(3):
                term = lax.dot_general(
                    grad_flat,
                    kernel_full[tap_d, tap_h, tap_w],
                    (((1,), (1,)), ((), ())),
                    preferred_element_type=jnp.float32,
                )
                term = term.reshape(samples, depth, height, width, channels)
                pads = [(0, 0)]
                for tap in (tap_d, tap_h, tap_w):
                    pads.append((1, 0) if tap == 2 else (0, 1))
                pads.append((0, 0))
                term = jnp.pad(term, pads)
                key_name = (tap_d % 2, tap_h % 2, tap_w % 2)
                classes[key_name] = classes[key_name] + term if key_name in classes else term
    planes = []
    for parity_d in range(2):
        rows_h = []
        for parity_h in range(2):
            rows_h.append(weave(classes[parity_d, parity_h, 0], classes[parity_d, parity_h, 1], 3))
        planes.append(weave(rows_h[0], rows_h[1], 2))
    whole = weave(planes[0], planes[1], 1)
    return whole[:, : 2 * depth + 1, : 2 * height + 1, : 2 * width + 1, :]


def on_device(volume, kernel, cotangent):
    samples = volume.shape[0]
    depth = volume.shape[1] // 2
    height = volume.shape[2] // 2
    width = volume.shape[3] // 2
    n_sy = lax.axis_size("sy")
    n_af = lax.axis_size("af")
    kernel_part = gather_filters(kernel)
    kernel_full = lax.all_gather(kernel_part, "sx", axis=3, tiled=True)
    filters = kernel_full.shape[4]
    per_dev = filters // (n_sy * n_af)
    below = from_behind(volume[:, -1:], "sx", 1)
    extended = jnp.concatenate([below, volume], axis=1)
    beside = from_behind(extended[:, :, -1:], "sy", 1)
    extended = jnp.concatenate([beside, extended], axis=2)
    extended = jnp.pad(extended, ((0, 0), (0, 0), (0, 0), (1, 0), (0, 0)))
    rows = samples * depth * height * width
    classes = parity_view(extended)
    cols = im2col(classes, depth, height, width).reshape(rows, -1)
    kernel_mat = kernel_full.reshape(-1, filters)
    total = jnp.dot(cols, kernel_mat, preferred_element_type=jnp.float32)
    n_sx = lax.axis_size("sx")
    conv_space = total.astype(jnp.bfloat16).reshape(depth, height, width, n_sy, n_af, per_dev)
    by_af = lax.all_to_all(conv_space.transpose(4, 3, 0, 1, 2, 5), "af", 0, 0, tiled=True)
    by_region = by_af.reshape(n_sx * n_sy, depth, height, width, per_dev)
    gathered = lax.all_to_all(by_region, ("sx", "sy"), 0, 0, tiled=True)
    own_samples = cotangent.shape[0]
    features = (
        gathered.reshape(n_sx, n_sy, depth, height, width, per_dev)
        .transpose(5, 0, 2, 1, 3, 4)
        .reshape(cotangent.shape)
    )
    grad_blocks = (
        cotangent.reshape(per_dev, n_sx, depth, n_sy, height, width)
        .transpose(1, 3, 2, 4, 5, 0)
        .reshape(n_sx * n_sy, depth, height, width, per_dev)
    )
    grad_region = lax.all_to_all(grad_blocks, ("sx", "sy"), 0, 0, tiled=True)
    grad_region = grad_region.reshape(n_sx * own_samples, n_sy, depth, height, width, per_dev)
    grad_back = lax.all_to_all(grad_region, "af", 0, 0, tiled=True)
    grad_back = grad_back.transpose(2, 3, 4, 1, 0, 5)
    grad_space = grad_back.reshape(samples, depth, height, width, filters)
    grad_flat = grad_space.reshape(rows, filters)
    kernel_terms = lax.dot_general(
        grad_flat, cols, (((0,), (0,)), ((), ())), preferred_element_type=jnp.float32
    )
    channels = kernel_full.shape[3]
    own_ch = channels // n_sx
    by_filter = reduce_filters(kernel_terms)
    by_filter = by_filter.reshape(per_dev, 27, n_sx, own_ch).transpose(2, 1, 3, 0)
    kernel_grad = lax.all_to_all(by_filter, "sx", 0, 0, tiled=True).sum(axis=0)
    kernel_grad = kernel_grad.reshape(3, 3, 3, own_ch, per_dev)
    partial_grad = spread_back(grad_space, kernel_full)
    from_above = from_behind(partial_grad[:, 0:1], "sx", -1)
    own_depth = partial_grad[:, 1:]
    own_depth = jnp.concatenate([own_depth[:, :-1], own_depth[:, -1:] + from_above], axis=1)
    from_right = from_behind(own_depth[:, :, 0:1].astype(jnp.bfloat16), "sy", -1).astype(
        jnp.float32
    )
    own_height = own_depth[:, :, 1:]
    own_height = jnp.concatenate(
        [own_height[:, :, :-1], own_height[:, :, -1:] + from_right], axis=2
    )
    volume_grad = own_height[:, :, :, 1:]
    return (features, volume_grad.astype(jnp.bfloat16), kernel_grad)


def solution(mesh):
    return jax.shard_map(
        on_device,
        mesh=mesh,
        in_specs=(
            P("af", "sx", "sy", None, None),
            P(None, None, None, "sx", ("sy", "af")),
            P("sx", ("sy", "af"), None, None),
        ),
        out_specs=(
            P("sx", ("sy", "af"), None, None),
            P("af", "sx", "sy", None, None),
            P(None, None, None, "sx", ("sy", "af")),
        ),
        check_vma=False,
    )
```

```python
import functools

import jax
import jax.numpy as jnp
from jax import lax
from jax.experimental import pallas as pl
from jax.experimental.pallas import tpu as pltpu
from jax.sharding import PartitionSpec as P


def _gather_body(n_sy, n_af, block_ref, out_ref, send_sem, recv_sem):
    group = n_sy * n_af
    sx = lax.axis_index("sx")
    me = lax.axis_index("sy") * n_af + lax.axis_index("af")
    barrier = pltpu.get_barrier_semaphore()
    for step in range(1, group):
        peer = lax.rem(me + step, group)
        pl.semaphore_signal(
            barrier,
            inc=1,
            device_id=(sx, peer // n_af, lax.rem(peer, n_af)),
            device_id_type=pl.DeviceIdType.MESH,
        )
    pl.semaphore_wait(barrier, group - 1)
    copies = []
    for step in range(1, group):
        peer = lax.rem(me + step, group)
        copy = pltpu.make_async_remote_copy(
            src_ref=block_ref,
            dst_ref=out_ref.at[me],
            send_sem=send_sem.at[step - 1],
            recv_sem=recv_sem.at[step - 1],
            device_id=(sx, peer // n_af, lax.rem(peer, n_af)),
            device_id_type=pl.DeviceIdType.MESH,
        )
        copy.start()
        copies.append(copy)
    out_ref[me] = block_ref[...]
    for copy in copies:
        copy.wait_send()
    for step in range(1, group):
        source = lax.rem(me + group - step, group)
        incoming = pltpu.make_async_remote_copy(
            src_ref=block_ref,
            dst_ref=out_ref.at[source],
            send_sem=send_sem.at[step - 1],
            recv_sem=recv_sem.at[step - 1],
            device_id=(sx, source // n_af, lax.rem(source, n_af)),
            device_id_type=pl.DeviceIdType.MESH,
        )
        incoming.wait_recv()


def _reduce_body(n_sy, n_af, terms_ref, out_ref, from_sib, mine, held, sib_send, sib_recv, send_sem, recv_sem):
    half = n_sy * n_af // 2
    rows = out_ref.shape[0]
    span = half * rows
    sx = lax.axis_index("sx")
    sy = lax.axis_index("sy")
    af = lax.axis_index("af")
    parity = lax.rem(af, 2)
    sib_af = af + 1 - 2 * parity
    me = sy * (n_af // 2) + af // 2

    def peer_of(index):
        block = 2 * index + parity
        return (sx, block // n_af, lax.rem(block, n_af))

    barrier = pltpu.get_barrier_semaphore()
    pl.semaphore_signal(barrier, inc=1, device_id=(sx, sy, sib_af), device_id_type=pl.DeviceIdType.MESH)
    for step in range(1, half):
        pl.semaphore_signal(
            barrier,
            inc=1,
            device_id=peer_of(lax.rem(me + step, half)),
            device_id_type=pl.DeviceIdType.MESH,
        )
    pl.semaphore_wait(barrier, half)
    to_sib = pltpu.make_async_remote_copy(
        src_ref=terms_ref.at[pl.ds(pl.multiple_of((1 - parity) * span, span), span)],
        dst_ref=from_sib,
        send_sem=sib_send,
        recv_sem=sib_recv,
        device_id=(sx, sy, sib_af),
        device_id_type=pl.DeviceIdType.MESH,
    )
    to_sib.start()
    to_sib.wait_send()
    to_sib.wait_recv()
    mine[...] = terms_ref[pl.ds(pl.multiple_of(parity * span, span), span), :] + from_sib[...]
    copies = []
    for step in range(1, half):
        peer = lax.rem(me + step, half)
        copy = pltpu.make_async_remote_copy(
            src_ref=mine.at[pl.ds(pl.multiple_of(peer * rows, rows), rows)],
            dst_ref=held.at[me],
            send_sem=send_sem.at[step - 1],
            recv_sem=recv_sem.at[step - 1],
            device_id=peer_of(peer),
            device_id_type=pl.DeviceIdType.MESH,
        )
        copy.start()
        copies.append(copy)
    total = mine[pl.ds(pl.multiple_of(me * rows, rows), rows), :]
    for copy in copies:
        copy.wait_send()
    for step in range(1, half):
        source = lax.rem(me + half - step, half)
        incoming = pltpu.make_async_remote_copy(
            src_ref=mine.at[pl.ds(0, rows)],
            dst_ref=held.at[source],
            send_sem=send_sem.at[step - 1],
            recv_sem=recv_sem.at[step - 1],
            device_id=peer_of(source),
            device_id_type=pl.DeviceIdType.MESH,
        )
        incoming.wait_recv()
        total = total + held[source]
    out_ref[...] = total


def reduce_filters(terms):
    n_sy = lax.axis_size("sy")
    n_af = lax.axis_size("af")
    group = n_sy * n_af
    rows = terms.shape[0] // group
    return pl.pallas_call(
        functools.partial(_reduce_body, n_sy, n_af),
        out_shape=jax.ShapeDtypeStruct((rows, terms.shape[1]), terms.dtype),
        in_specs=[pl.BlockSpec(memory_space=pltpu.VMEM)],
        out_specs=pl.BlockSpec(memory_space=pltpu.VMEM),
        scratch_shapes=[
            pltpu.VMEM((group // 2 * rows, terms.shape[1]), terms.dtype),
            pltpu.VMEM((group // 2 * rows, terms.shape[1]), terms.dtype),
            pltpu.VMEM((group // 2, rows, terms.shape[1]), terms.dtype),
            pltpu.SemaphoreType.DMA(()),
            pltpu.SemaphoreType.DMA(()),
            pltpu.SemaphoreType.DMA((group // 2 - 1,)),
            pltpu.SemaphoreType.DMA((group // 2 - 1,)),
        ],
        compiler_params=pltpu.CompilerParams(collective_id=1, has_side_effects=True),
        cost_estimate=pl.CostEstimate(
            flops=terms.size, bytes_accessed=2 * terms.size * 4, transcendentals=0
        ),
    )(terms)


def gather_filters(kernel):
    n_sy = lax.axis_size("sy")
    n_af = lax.axis_size("af")
    group = n_sy * n_af
    taps, channels, per_dev = kernel.shape[0] * kernel.shape[1] * kernel.shape[2], kernel.shape[3], kernel.shape[4]
    block = kernel.reshape(-1, 128)
    gathered = pl.pallas_call(
        functools.partial(_gather_body, n_sy, n_af),
        out_shape=jax.ShapeDtypeStruct((group,) + block.shape, block.dtype),
        in_specs=[pl.BlockSpec(memory_space=pltpu.VMEM)],
        out_specs=pl.BlockSpec(memory_space=pltpu.VMEM),
        scratch_shapes=[
            pltpu.SemaphoreType.DMA((group - 1,)),
            pltpu.SemaphoreType.DMA((group - 1,)),
        ],
        compiler_params=pltpu.CompilerParams(collective_id=0, has_side_effects=True),
    )(block)
    gathered = gathered.reshape(group, taps, channels, per_dev).transpose(1, 2, 0, 3)
    return gathered.reshape(kernel.shape[:4] + (group * per_dev,))


def from_behind(value, axis, steps):
    count = lax.axis_size(axis)
    leading, last = (max(0, -steps), min(count, count - steps))
    return lax.ppermute(value, axis, [(source, source + steps) for source in range(leading, last)])


def strided_patch(extended, tap_d, tap_h, tap_w, depth, height, width):
    return extended[
        :,
        tap_d : tap_d + 2 * depth : 2,
        tap_h : tap_h + 2 * height : 2,
        tap_w : tap_w + 2 * width : 2,
        :,
    ]


def parity_view(extended):
    samples, d_ext, h_ext, w_ext, channels = extended.shape
    pads = [(0, 0)] + [(0, n % 2) for n in (d_ext, h_ext, w_ext)] + [(0, 0)]
    even = jnp.pad(extended, pads)
    _, d2, h2, w2, _ = even.shape
    split = even.reshape(samples, d2 // 2, 2, h2 // 2, 2, w2 // 2, 2, channels)
    return split.transpose(2, 4, 6, 0, 1, 3, 5, 7)


def im2col(classes, depth, height, width):
    patches = []
    for tap_d in range(3):
        for tap_h in range(3):
            for tap_w in range(3):
                cls = classes[tap_d % 2, tap_h % 2, tap_w % 2]
                od, oh, ow = tap_d // 2, tap_h // 2, tap_w // 2
                patches.append(cls[:, od : od + depth, oh : oh + height, ow : ow + width, :])
    return jnp.concatenate(patches, axis=-1)


def weave(even_part, odd_part, axis):
    stacked = jnp.stack([even_part, odd_part], axis=axis + 1)
    shape = list(even_part.shape)
    shape[axis] = shape[axis] * 2
    return stacked.reshape(shape)


def spread_back(grad_space, kernel_full):
    samples, depth, height, width, filters = grad_space.shape
    channels = kernel_full.shape[3]
    grad_flat = grad_space.reshape(-1, filters)
    classes = {}
    for tap_d in range(3):
        for tap_h in range(3):
            for tap_w in range(3):
                term = lax.dot_general(
                    grad_flat,
                    kernel_full[tap_d, tap_h, tap_w],
                    (((1,), (1,)), ((), ())),
                    preferred_element_type=jnp.float32,
                )
                term = term.reshape(samples, depth, height, width, channels)
                pads = [(0, 0)]
                for tap in (tap_d, tap_h, tap_w):
                    pads.append((1, 0) if tap == 2 else (0, 1))
                pads.append((0, 0))
                term = jnp.pad(term, pads)
                key_name = (tap_d % 2, tap_h % 2, tap_w % 2)
                classes[key_name] = classes[key_name] + term if key_name in classes else term
    planes = []
    for parity_d in range(2):
        rows_h = []
        for parity_h in range(2):
            rows_h.append(weave(classes[parity_d, parity_h, 0], classes[parity_d, parity_h, 1], 3))
        planes.append(weave(rows_h[0], rows_h[1], 2))
    whole = weave(planes[0], planes[1], 1)
    return whole[:, : 2 * depth + 1, : 2 * height + 1, : 2 * width + 1, :]


def on_device(volume, kernel, cotangent):
    samples = volume.shape[0]
    depth = volume.shape[1] // 2
    height = volume.shape[2] // 2
    width = volume.shape[3] // 2
    n_sy = lax.axis_size("sy")
    n_af = lax.axis_size("af")
    kernel_part = gather_filters(kernel)
    kernel_full = lax.all_gather(kernel_part, "sx", axis=3, tiled=True)
    filters = kernel_full.shape[4]
    per_dev = filters // (n_sy * n_af)
    below = from_behind(volume[:, -1:], "sx", 1)
    extended = jnp.concatenate([below, volume], axis=1)
    beside = from_behind(extended[:, :, -1:], "sy", 1)
    extended = jnp.concatenate([beside, extended], axis=2)
    extended = jnp.pad(extended, ((0, 0), (0, 0), (0, 0), (1, 0), (0, 0)))
    rows = samples * depth * height * width
    classes = parity_view(extended)
    cols = im2col(classes, depth, height, width).reshape(rows, -1)
    kernel_mat = kernel_full.reshape(-1, filters)
    total = jnp.dot(cols, kernel_mat, preferred_element_type=jnp.float32)
    n_sx = lax.axis_size("sx")
    conv_space = total.astype(jnp.bfloat16).reshape(depth, height, width, n_sy, n_af, per_dev)
    by_af = lax.all_to_all(conv_space.transpose(4, 3, 0, 1, 2, 5), "af", 0, 0, tiled=True)
    by_region = by_af.reshape(n_sx * n_sy, depth, height, width, per_dev)
    gathered = lax.all_to_all(by_region, ("sx", "sy"), 0, 0, tiled=True)
    own_samples = cotangent.shape[0]
    features = (
        gathered.reshape(n_sx, n_sy, depth, height, width, per_dev)
        .transpose(5, 0, 2, 1, 3, 4)
        .reshape(cotangent.shape)
    )
    grad_blocks = (
        cotangent.reshape(per_dev, n_sx, depth, n_sy, height, width)
        .transpose(1, 3, 2, 4, 5, 0)
        .reshape(n_sx * n_sy, depth, height, width, per_dev)
    )
    grad_region = lax.all_to_all(grad_blocks, ("sx", "sy"), 0, 0, tiled=True)
    grad_region = grad_region.reshape(n_sx * own_samples, n_sy, depth, height, width, per_dev)
    grad_back = lax.all_to_all(grad_region, "af", 0, 0, tiled=True)
    grad_back = grad_back.transpose(2, 3, 4, 1, 0, 5)
    grad_space = grad_back.reshape(samples, depth, height, width, filters)
    grad_flat = grad_space.reshape(rows, filters)
    by_parity = grad_flat.reshape(rows, n_sy * n_af // 2, 2, per_dev).transpose(0, 2, 1, 3)
    kernel_terms = lax.dot_general(
        by_parity.reshape(rows, filters), cols, (((0,), (0,)), ((), ())), preferred_element_type=jnp.float32
    )
    channels = kernel_full.shape[3]
    own_ch = channels // n_sx
    by_filter = reduce_filters(kernel_terms)
    by_filter = by_filter.reshape(per_dev, 27, n_sx, own_ch).transpose(2, 1, 3, 0)
    kernel_grad = lax.all_to_all(by_filter, "sx", 0, 0, tiled=True).sum(axis=0)
    kernel_grad = kernel_grad.reshape(3, 3, 3, own_ch, per_dev)
    partial_grad = spread_back(grad_space, kernel_full)
    from_above = from_behind(partial_grad[:, 0:1], "sx", -1)
    own_depth = partial_grad[:, 1:]
    own_depth = jnp.concatenate([own_depth[:, :-1], own_depth[:, -1:] + from_above], axis=1)
    from_right = from_behind(own_depth[:, :, 0:1].astype(jnp.bfloat16), "sy", -1).astype(
        jnp.float32
    )
    own_height = own_depth[:, :, 1:]
    own_height = jnp.concatenate(
        [own_height[:, :, :-1], own_height[:, :, -1:] + from_right], axis=2
    )
    volume_grad = own_height[:, :, :, 1:]
    return (features, volume_grad.astype(jnp.bfloat16), kernel_grad)


def solution(mesh):
    return jax.shard_map(
        on_device,
        mesh=mesh,
        in_specs=(
            P("af", "sx", "sy", None, None),
            P(None, None, None, "sx", ("sy", "af")),
            P("sx", ("sy", "af"), None, None),
        ),
        out_specs=(
            P("sx", ("sy", "af"), None, None),
            P("af", "sx", "sy", None, None),
            P(None, None, None, "sx", ("sy", "af")),
        ),
        check_vma=False,
    )
```

```python
import functools

import jax
import jax.numpy as jnp
from jax import lax
from jax.experimental import pallas as pl
from jax.experimental.pallas import tpu as pltpu
from jax.sharding import PartitionSpec as P


def _gather_body(n_sy, n_af, block_ref, out_ref, send_sem, recv_sem):
    group = n_sy * n_af
    sx = lax.axis_index("sx")
    me = lax.axis_index("sy") * n_af + lax.axis_index("af")
    barrier = pltpu.get_barrier_semaphore()
    for step in range(1, group):
        peer = lax.rem(me + step, group)
        pl.semaphore_signal(
            barrier,
            inc=1,
            device_id=(sx, peer // n_af, lax.rem(peer, n_af)),
            device_id_type=pl.DeviceIdType.MESH,
        )
    pl.semaphore_wait(barrier, group - 1)
    copies = []
    for step in range(1, group):
        peer = lax.rem(me + step, group)
        copy = pltpu.make_async_remote_copy(
            src_ref=block_ref,
            dst_ref=out_ref.at[me],
            send_sem=send_sem.at[step - 1],
            recv_sem=recv_sem.at[step - 1],
            device_id=(sx, peer // n_af, lax.rem(peer, n_af)),
            device_id_type=pl.DeviceIdType.MESH,
        )
        copy.start()
        copies.append(copy)
    out_ref[me] = block_ref[...]
    for copy in copies:
        copy.wait_send()
    for step in range(1, group):
        source = lax.rem(me + group - step, group)
        incoming = pltpu.make_async_remote_copy(
            src_ref=block_ref,
            dst_ref=out_ref.at[source],
            send_sem=send_sem.at[step - 1],
            recv_sem=recv_sem.at[step - 1],
            device_id=(sx, source // n_af, lax.rem(source, n_af)),
            device_id_type=pl.DeviceIdType.MESH,
        )
        incoming.wait_recv()


def _reduce_body(n_sy, n_af, terms_ref, out_ref, from_sib, mine, held, sib_send, sib_recv, send_sem, recv_sem):
    half = n_sy * n_af // 2
    rows = out_ref.shape[0]
    span = half * rows
    sx = lax.axis_index("sx")
    sy = lax.axis_index("sy")
    af = lax.axis_index("af")
    parity = lax.rem(af, 2)
    sib_af = af + 1 - 2 * parity
    me = sy * (n_af // 2) + af // 2

    def peer_of(index):
        block = 2 * index + parity
        return (sx, block // n_af, lax.rem(block, n_af))

    barrier = pltpu.get_barrier_semaphore()
    pl.semaphore_signal(barrier, inc=1, device_id=(sx, sy, sib_af), device_id_type=pl.DeviceIdType.MESH)
    for step in range(1, half):
        pl.semaphore_signal(
            barrier,
            inc=1,
            device_id=peer_of(lax.rem(me + step, half)),
            device_id_type=pl.DeviceIdType.MESH,
        )
    pl.semaphore_wait(barrier, half)
    to_sib = pltpu.make_async_remote_copy(
        src_ref=terms_ref.at[pl.ds(pl.multiple_of((1 - parity) * span, span), span)],
        dst_ref=from_sib,
        send_sem=sib_send,
        recv_sem=sib_recv,
        device_id=(sx, sy, sib_af),
        device_id_type=pl.DeviceIdType.MESH,
    )
    to_sib.start()
    to_sib.wait_send()
    to_sib.wait_recv()
    mine[...] = terms_ref[pl.ds(pl.multiple_of(parity * span, span), span), :] + from_sib[...]
    copies = []
    for step in range(1, half):
        peer = lax.rem(me + step, half)
        copy = pltpu.make_async_remote_copy(
            src_ref=mine.at[pl.ds(pl.multiple_of(peer * rows, rows), rows)],
            dst_ref=held.at[me],
            send_sem=send_sem.at[step - 1],
            recv_sem=recv_sem.at[step - 1],
            device_id=peer_of(peer),
            device_id_type=pl.DeviceIdType.MESH,
        )
        copy.start()
        copies.append(copy)
    total = mine[pl.ds(pl.multiple_of(me * rows, rows), rows), :]
    for copy in copies:
        copy.wait_send()
    for step in range(1, half):
        source = lax.rem(me + half - step, half)
        incoming = pltpu.make_async_remote_copy(
            src_ref=mine.at[pl.ds(0, rows)],
            dst_ref=held.at[source],
            send_sem=send_sem.at[step - 1],
            recv_sem=recv_sem.at[step - 1],
            device_id=peer_of(source),
            device_id_type=pl.DeviceIdType.MESH,
        )
        incoming.wait_recv()
        total = total + held[source]
    out_ref[...] = total


def reduce_filters(terms):
    n_sy = lax.axis_size("sy")
    n_af = lax.axis_size("af")
    group = n_sy * n_af
    rows = terms.shape[0] // group
    return pl.pallas_call(
        functools.partial(_reduce_body, n_sy, n_af),
        out_shape=jax.ShapeDtypeStruct((rows, terms.shape[1]), terms.dtype),
        in_specs=[pl.BlockSpec(memory_space=pltpu.VMEM)],
        out_specs=pl.BlockSpec(memory_space=pltpu.VMEM),
        scratch_shapes=[
            pltpu.VMEM((group // 2 * rows, terms.shape[1]), terms.dtype),
            pltpu.VMEM((group // 2 * rows, terms.shape[1]), terms.dtype),
            pltpu.VMEM((group // 2, rows, terms.shape[1]), terms.dtype),
            pltpu.SemaphoreType.DMA(()),
            pltpu.SemaphoreType.DMA(()),
            pltpu.SemaphoreType.DMA((group // 2 - 1,)),
            pltpu.SemaphoreType.DMA((group // 2 - 1,)),
        ],
        compiler_params=pltpu.CompilerParams(collective_id=1, has_side_effects=True),
        cost_estimate=pl.CostEstimate(
            flops=terms.size, bytes_accessed=2 * terms.size * 4, transcendentals=0
        ),
    )(terms)


def gather_filters(kernel):
    n_sy = lax.axis_size("sy")
    n_af = lax.axis_size("af")
    group = n_sy * n_af
    taps, channels, per_dev = kernel.shape[0] * kernel.shape[1] * kernel.shape[2], kernel.shape[3], kernel.shape[4]
    block = kernel.reshape(-1, 128)
    gathered = pl.pallas_call(
        functools.partial(_gather_body, n_sy, n_af),
        out_shape=jax.ShapeDtypeStruct((group,) + block.shape, block.dtype),
        in_specs=[pl.BlockSpec(memory_space=pltpu.VMEM)],
        out_specs=pl.BlockSpec(memory_space=pltpu.VMEM),
        scratch_shapes=[
            pltpu.SemaphoreType.DMA((group - 1,)),
            pltpu.SemaphoreType.DMA((group - 1,)),
        ],
        compiler_params=pltpu.CompilerParams(collective_id=0, has_side_effects=True),
    )(block)
    gathered = gathered.reshape(group, taps, channels, per_dev).transpose(1, 2, 0, 3)
    return gathered.reshape(kernel.shape[:4] + (group * per_dev,))


MESH_AXES = ("sx", "sy", "af")


def _exchange_body(axes, x_ref, out_ref, send_sem, recv_sem):
    sizes = [lax.axis_size(name) for name in axes]
    group = x_ref.shape[0]
    me = 0
    for name, size in zip(axes, sizes):
        me = me * size + lax.axis_index(name)

    def device(index):
        digits = {}
        for name, size in reversed(list(zip(axes, sizes))):
            digits[name] = lax.rem(index, size)
            index = index // size
        return tuple(digits[name] if name in digits else lax.axis_index(name) for name in MESH_AXES)

    barrier = pltpu.get_barrier_semaphore()
    for step in range(1, group):
        pl.semaphore_signal(
            barrier,
            inc=1,
            device_id=device(lax.rem(me + step, group)),
            device_id_type=pl.DeviceIdType.MESH,
        )
    pl.semaphore_wait(barrier, group - 1)
    copies = []
    for step in range(1, group):
        peer = lax.rem(me + step, group)
        copy = pltpu.make_async_remote_copy(
            src_ref=x_ref.at[peer],
            dst_ref=out_ref.at[me],
            send_sem=send_sem.at[step - 1],
            recv_sem=recv_sem.at[step - 1],
            device_id=device(peer),
            device_id_type=pl.DeviceIdType.MESH,
        )
        copy.start()
        copies.append(copy)
    out_ref[me] = x_ref[me]
    for copy in copies:
        copy.wait_send()
    for step in range(1, group):
        source = lax.rem(me + group - step, group)
        incoming = pltpu.make_async_remote_copy(
            src_ref=x_ref.at[source],
            dst_ref=out_ref.at[source],
            send_sem=send_sem.at[step - 1],
            recv_sem=recv_sem.at[step - 1],
            device_id=device(source),
            device_id_type=pl.DeviceIdType.MESH,
        )
        incoming.wait_recv()


def exchange(x, axes, collective_id):
    group = x.shape[0]
    flat = x.reshape(group, -1, 128)
    out = pl.pallas_call(
        functools.partial(_exchange_body, axes),
        out_shape=jax.ShapeDtypeStruct(flat.shape, flat.dtype),
        in_specs=[pl.BlockSpec(memory_space=pltpu.VMEM)],
        out_specs=pl.BlockSpec(memory_space=pltpu.VMEM),
        scratch_shapes=[
            pltpu.SemaphoreType.DMA((group - 1,)),
            pltpu.SemaphoreType.DMA((group - 1,)),
        ],
        compiler_params=pltpu.CompilerParams(collective_id=collective_id, has_side_effects=True),
    )(flat)
    return out.reshape(x.shape)


def from_behind(value, axis, steps):
    count = lax.axis_size(axis)
    leading, last = (max(0, -steps), min(count, count - steps))
    return lax.ppermute(value, axis, [(source, source + steps) for source in range(leading, last)])


def strided_patch(extended, tap_d, tap_h, tap_w, depth, height, width):
    return extended[
        :,
        tap_d : tap_d + 2 * depth : 2,
        tap_h : tap_h + 2 * height : 2,
        tap_w : tap_w + 2 * width : 2,
        :,
    ]


def parity_view(extended):
    samples, d_ext, h_ext, w_ext, channels = extended.shape
    pads = [(0, 0)] + [(0, n % 2) for n in (d_ext, h_ext, w_ext)] + [(0, 0)]
    even = jnp.pad(extended, pads)
    _, d2, h2, w2, _ = even.shape
    split = even.reshape(samples, d2 // 2, 2, h2 // 2, 2, w2 // 2, 2, channels)
    return split.transpose(2, 4, 6, 0, 1, 3, 5, 7)


def im2col(classes, depth, height, width):
    patches = []
    for tap_d in range(3):
        for tap_h in range(3):
            for tap_w in range(3):
                cls = classes[tap_d % 2, tap_h % 2, tap_w % 2]
                od, oh, ow = tap_d // 2, tap_h // 2, tap_w // 2
                patches.append(cls[:, od : od + depth, oh : oh + height, ow : ow + width, :])
    return jnp.concatenate(patches, axis=-1)


def weave(even_part, odd_part, axis):
    stacked = jnp.stack([even_part, odd_part], axis=axis + 1)
    shape = list(even_part.shape)
    shape[axis] = shape[axis] * 2
    return stacked.reshape(shape)


def spread_back(grad_space, kernel_full):
    samples, depth, height, width, filters = grad_space.shape
    channels = kernel_full.shape[3]
    grad_flat = grad_space.reshape(-1, filters)
    classes = {}
    for tap_d in range(3):
        for tap_h in range(3):
            for tap_w in range(3):
                term = lax.dot_general(
                    grad_flat,
                    kernel_full[tap_d, tap_h, tap_w],
                    (((1,), (1,)), ((), ())),
                    preferred_element_type=jnp.float32,
                )
                term = term.reshape(samples, depth, height, width, channels)
                pads = [(0, 0)]
                for tap in (tap_d, tap_h, tap_w):
                    pads.append((1, 0) if tap == 2 else (0, 1))
                pads.append((0, 0))
                term = jnp.pad(term, pads)
                key_name = (tap_d % 2, tap_h % 2, tap_w % 2)
                classes[key_name] = classes[key_name] + term if key_name in classes else term
    planes = []
    for parity_d in range(2):
        rows_h = []
        for parity_h in range(2):
            rows_h.append(weave(classes[parity_d, parity_h, 0], classes[parity_d, parity_h, 1], 3))
        planes.append(weave(rows_h[0], rows_h[1], 2))
    whole = weave(planes[0], planes[1], 1)
    return whole[:, : 2 * depth + 1, : 2 * height + 1, : 2 * width + 1, :]


def on_device(volume, kernel, cotangent):
    samples = volume.shape[0]
    depth = volume.shape[1] // 2
    height = volume.shape[2] // 2
    width = volume.shape[3] // 2
    n_sy = lax.axis_size("sy")
    n_af = lax.axis_size("af")
    kernel_part = gather_filters(kernel)
    kernel_full = lax.all_gather(kernel_part, "sx", axis=3, tiled=True)
    filters = kernel_full.shape[4]
    per_dev = filters // (n_sy * n_af)
    below = from_behind(volume[:, -1:], "sx", 1)
    extended = jnp.concatenate([below, volume], axis=1)
    beside = from_behind(extended[:, :, -1:], "sy", 1)
    extended = jnp.concatenate([beside, extended], axis=2)
    extended = jnp.pad(extended, ((0, 0), (0, 0), (0, 0), (1, 0), (0, 0)))
    rows = samples * depth * height * width
    classes = parity_view(extended)
    cols = im2col(classes, depth, height, width).reshape(rows, -1)
    kernel_mat = kernel_full.reshape(-1, filters)
    total = jnp.dot(cols, kernel_mat, preferred_element_type=jnp.float32)
    n_sx = lax.axis_size("sx")
    conv_space = total.astype(jnp.bfloat16).reshape(depth, height, width, n_sy, n_af, per_dev)
    by_af = exchange(conv_space.transpose(4, 3, 0, 1, 2, 5), ("af",), 2)
    by_region = by_af.reshape(n_sx * n_sy, depth, height, width, per_dev)
    gathered = exchange(by_region, ("sx", "sy"), 3)
    own_samples = cotangent.shape[0]
    features = (
        gathered.reshape(n_sx, n_sy, depth, height, width, per_dev)
        .transpose(5, 0, 2, 1, 3, 4)
        .reshape(cotangent.shape)
    )
    grad_blocks = (
        cotangent.reshape(per_dev, n_sx, depth, n_sy, height, width)
        .transpose(1, 3, 2, 4, 5, 0)
        .reshape(n_sx * n_sy, depth, height, width, per_dev)
    )
    grad_region = exchange(grad_blocks, ("sx", "sy"), 4)
    grad_region = grad_region.reshape(n_sx * own_samples, n_sy, depth, height, width, per_dev)
    grad_back = exchange(grad_region, ("af",), 5)
    grad_back = grad_back.transpose(2, 3, 4, 1, 0, 5)
    grad_space = grad_back.reshape(samples, depth, height, width, filters)
    grad_flat = grad_space.reshape(rows, filters)
    by_parity = grad_flat.reshape(rows, n_sy * n_af // 2, 2, per_dev).transpose(0, 2, 1, 3)
    kernel_terms = lax.dot_general(
        by_parity.reshape(rows, filters), cols, (((0,), (0,)), ((), ())), preferred_element_type=jnp.float32
    )
    channels = kernel_full.shape[3]
    own_ch = channels // n_sx
    by_filter = reduce_filters(kernel_terms)
    by_filter = by_filter.reshape(per_dev, 27, n_sx, own_ch).transpose(2, 1, 3, 0)
    kernel_grad = lax.all_to_all(by_filter, "sx", 0, 0, tiled=True).sum(axis=0)
    kernel_grad = kernel_grad.reshape(3, 3, 3, own_ch, per_dev)
    partial_grad = spread_back(grad_space, kernel_full)
    from_above = from_behind(partial_grad[:, 0:1], "sx", -1)
    own_depth = partial_grad[:, 1:]
    own_depth = jnp.concatenate([own_depth[:, :-1], own_depth[:, -1:] + from_above], axis=1)
    from_right = from_behind(own_depth[:, :, 0:1].astype(jnp.bfloat16), "sy", -1).astype(
        jnp.float32
    )
    own_height = own_depth[:, :, 1:]
    own_height = jnp.concatenate(
        [own_height[:, :, :-1], own_height[:, :, -1:] + from_right], axis=2
    )
    volume_grad = own_height[:, :, :, 1:]
    return (features, volume_grad.astype(jnp.bfloat16), kernel_grad)


def solution(mesh):
    return jax.shard_map(
        on_device,
        mesh=mesh,
        in_specs=(
            P("af", "sx", "sy", None, None),
            P(None, None, None, "sx", ("sy", "af")),
            P("sx", ("sy", "af"), None, None),
        ),
        out_specs=(
            P("sx", ("sy", "af"), None, None),
            P("af", "sx", "sy", None, None),
            P(None, None, None, "sx", ("sy", "af")),
        ),
        check_vma=False,
    )
```

```python
import functools

import jax
import jax.numpy as jnp
from jax import lax
from jax.experimental import pallas as pl
from jax.experimental.pallas import tpu as pltpu
from jax.sharding import PartitionSpec as P


def _gather_body(n_sy, n_af, block_ref, out_ref, send_sem, recv_sem):
    group = n_sy * n_af
    sx = lax.axis_index("sx")
    me = lax.axis_index("sy") * n_af + lax.axis_index("af")
    barrier = pltpu.get_barrier_semaphore()
    for step in range(1, group):
        peer = lax.rem(me + step, group)
        pl.semaphore_signal(
            barrier,
            inc=1,
            device_id=(sx, peer // n_af, lax.rem(peer, n_af)),
            device_id_type=pl.DeviceIdType.MESH,
        )
    pl.semaphore_wait(barrier, group - 1)
    copies = []
    for step in range(1, group):
        peer = lax.rem(me + step, group)
        copy = pltpu.make_async_remote_copy(
            src_ref=block_ref,
            dst_ref=out_ref.at[me],
            send_sem=send_sem.at[step - 1],
            recv_sem=recv_sem.at[step - 1],
            device_id=(sx, peer // n_af, lax.rem(peer, n_af)),
            device_id_type=pl.DeviceIdType.MESH,
        )
        copy.start()
        copies.append(copy)
    out_ref[me] = block_ref[...]
    for copy in copies:
        copy.wait_send()
    for step in range(1, group):
        source = lax.rem(me + group - step, group)
        incoming = pltpu.make_async_remote_copy(
            src_ref=block_ref,
            dst_ref=out_ref.at[source],
            send_sem=send_sem.at[step - 1],
            recv_sem=recv_sem.at[step - 1],
            device_id=(sx, source // n_af, lax.rem(source, n_af)),
            device_id_type=pl.DeviceIdType.MESH,
        )
        incoming.wait_recv()


def _reduce_body(n_sy, n_af, terms_ref, out_ref, from_sib, mine, held, sib_send, sib_recv, send_sem, recv_sem):
    half = n_sy * n_af // 2
    rows = out_ref.shape[0]
    span = half * rows
    sx = lax.axis_index("sx")
    sy = lax.axis_index("sy")
    af = lax.axis_index("af")
    parity = lax.rem(af, 2)
    sib_af = af + 1 - 2 * parity
    me = sy * (n_af // 2) + af // 2

    def peer_of(index):
        block = 2 * index + parity
        return (sx, block // n_af, lax.rem(block, n_af))

    barrier = pltpu.get_barrier_semaphore()
    pl.semaphore_signal(barrier, inc=1, device_id=(sx, sy, sib_af), device_id_type=pl.DeviceIdType.MESH)
    for step in range(1, half):
        pl.semaphore_signal(
            barrier,
            inc=1,
            device_id=peer_of(lax.rem(me + step, half)),
            device_id_type=pl.DeviceIdType.MESH,
        )
    pl.semaphore_wait(barrier, half)
    to_sib = pltpu.make_async_remote_copy(
        src_ref=terms_ref.at[pl.ds(pl.multiple_of((1 - parity) * span, span), span)],
        dst_ref=from_sib,
        send_sem=sib_send,
        recv_sem=sib_recv,
        device_id=(sx, sy, sib_af),
        device_id_type=pl.DeviceIdType.MESH,
    )
    to_sib.start()
    to_sib.wait_send()
    to_sib.wait_recv()
    mine[...] = terms_ref[pl.ds(pl.multiple_of(parity * span, span), span), :] + from_sib[...]
    copies = []
    for step in range(1, half):
        peer = lax.rem(me + step, half)
        copy = pltpu.make_async_remote_copy(
            src_ref=mine.at[pl.ds(pl.multiple_of(peer * rows, rows), rows)],
            dst_ref=held.at[me],
            send_sem=send_sem.at[step - 1],
            recv_sem=recv_sem.at[step - 1],
            device_id=peer_of(peer),
            device_id_type=pl.DeviceIdType.MESH,
        )
        copy.start()
        copies.append(copy)
    total = mine[pl.ds(pl.multiple_of(me * rows, rows), rows), :]
    for copy in copies:
        copy.wait_send()
    for step in range(1, half):
        source = lax.rem(me + half - step, half)
        incoming = pltpu.make_async_remote_copy(
            src_ref=mine.at[pl.ds(0, rows)],
            dst_ref=held.at[source],
            send_sem=send_sem.at[step - 1],
            recv_sem=recv_sem.at[step - 1],
            device_id=peer_of(source),
            device_id_type=pl.DeviceIdType.MESH,
        )
        incoming.wait_recv()
        total = total + held[source]
    out_ref[...] = total


def reduce_filters(terms):
    n_sy = lax.axis_size("sy")
    n_af = lax.axis_size("af")
    group = n_sy * n_af
    rows = terms.shape[0] // group
    return pl.pallas_call(
        functools.partial(_reduce_body, n_sy, n_af),
        out_shape=jax.ShapeDtypeStruct((rows, terms.shape[1]), terms.dtype),
        in_specs=[pl.BlockSpec(memory_space=pltpu.VMEM)],
        out_specs=pl.BlockSpec(memory_space=pltpu.VMEM),
        scratch_shapes=[
            pltpu.VMEM((group // 2 * rows, terms.shape[1]), terms.dtype),
            pltpu.VMEM((group // 2 * rows, terms.shape[1]), terms.dtype),
            pltpu.VMEM((group // 2, rows, terms.shape[1]), terms.dtype),
            pltpu.SemaphoreType.DMA(()),
            pltpu.SemaphoreType.DMA(()),
            pltpu.SemaphoreType.DMA((group // 2 - 1,)),
            pltpu.SemaphoreType.DMA((group // 2 - 1,)),
        ],
        compiler_params=pltpu.CompilerParams(collective_id=1, has_side_effects=True),
        cost_estimate=pl.CostEstimate(
            flops=terms.size, bytes_accessed=2 * terms.size * 4, transcendentals=0
        ),
    )(terms)


def gather_filters(kernel):
    n_sy = lax.axis_size("sy")
    n_af = lax.axis_size("af")
    group = n_sy * n_af
    taps, channels, per_dev = kernel.shape[0] * kernel.shape[1] * kernel.shape[2], kernel.shape[3], kernel.shape[4]
    block = kernel.reshape(-1, 128)
    gathered = pl.pallas_call(
        functools.partial(_gather_body, n_sy, n_af),
        out_shape=jax.ShapeDtypeStruct((group,) + block.shape, block.dtype),
        in_specs=[pl.BlockSpec(memory_space=pltpu.VMEM)],
        out_specs=pl.BlockSpec(memory_space=pltpu.VMEM),
        scratch_shapes=[
            pltpu.SemaphoreType.DMA((group - 1,)),
            pltpu.SemaphoreType.DMA((group - 1,)),
        ],
        compiler_params=pltpu.CompilerParams(collective_id=0, has_side_effects=True),
    )(block)
    gathered = gathered.reshape(group, taps, channels, per_dev).transpose(1, 2, 0, 3)
    return gathered.reshape(kernel.shape[:4] + (group * per_dev,))


def from_behind(value, axis, steps):
    count = lax.axis_size(axis)
    leading, last = (max(0, -steps), min(count, count - steps))
    return lax.ppermute(value, axis, [(source, source + steps) for source in range(leading, last)])


def strided_patch(extended, tap_d, tap_h, tap_w, depth, height, width):
    return extended[
        :,
        tap_d : tap_d + 2 * depth : 2,
        tap_h : tap_h + 2 * height : 2,
        tap_w : tap_w + 2 * width : 2,
        :,
    ]


def parity_view(extended):
    samples, d_ext, h_ext, w_ext, channels = extended.shape
    pads = [(0, 0)] + [(0, n % 2) for n in (d_ext, h_ext, w_ext)] + [(0, 0)]
    even = jnp.pad(extended, pads)
    _, d2, h2, w2, _ = even.shape
    split = even.reshape(samples, d2 // 2, 2, h2 // 2, 2, w2 // 2, 2, channels)
    return split.transpose(2, 4, 6, 0, 1, 3, 5, 7)


def im2col(classes, depth, height, width):
    patches = []
    for tap_d in range(3):
        for tap_h in range(3):
            for tap_w in range(3):
                cls = classes[tap_d % 2, tap_h % 2, tap_w % 2]
                od, oh, ow = tap_d // 2, tap_h // 2, tap_w // 2
                patches.append(cls[:, od : od + depth, oh : oh + height, ow : ow + width, :])
    return jnp.concatenate(patches, axis=-1)


def weave(even_part, odd_part, axis):
    stacked = jnp.stack([even_part, odd_part], axis=axis + 1)
    shape = list(even_part.shape)
    shape[axis] = shape[axis] * 2
    return stacked.reshape(shape)


def spread_back(grad_space, kernel_full):
    samples, depth, height, width, filters = grad_space.shape
    channels = kernel_full.shape[3]
    grad_flat = grad_space.reshape(-1, filters)
    spread = lax.dot_general(
        grad_flat,
        kernel_full.reshape(-1, channels, filters),
        (((1,), (2,)), ((), ())),
        preferred_element_type=jnp.float32,
    ).reshape(samples, depth, height, width, 27, channels)
    classes = {}
    for tap_d in range(3):
        for tap_h in range(3):
            for tap_w in range(3):
                term = spread[:, :, :, :, tap_d * 9 + tap_h * 3 + tap_w]
                pads = [(0, 0)]
                for tap in (tap_d, tap_h, tap_w):
                    pads.append((1, 0) if tap == 2 else (0, 1))
                pads.append((0, 0))
                term = jnp.pad(term, pads)
                key_name = (tap_d % 2, tap_h % 2, tap_w % 2)
                classes[key_name] = classes[key_name] + term if key_name in classes else term
    planes = []
    for parity_d in range(2):
        rows_h = []
        for parity_h in range(2):
            rows_h.append(weave(classes[parity_d, parity_h, 0], classes[parity_d, parity_h, 1], 3))
        planes.append(weave(rows_h[0], rows_h[1], 2))
    whole = weave(planes[0], planes[1], 1)
    return whole[:, : 2 * depth + 1, : 2 * height + 1, : 2 * width + 1, :]


def on_device(volume, kernel, cotangent):
    samples = volume.shape[0]
    depth = volume.shape[1] // 2
    height = volume.shape[2] // 2
    width = volume.shape[3] // 2
    n_sy = lax.axis_size("sy")
    n_af = lax.axis_size("af")
    kernel_part = gather_filters(kernel)
    kernel_full = lax.all_gather(kernel_part, "sx", axis=3, tiled=True)
    filters = kernel_full.shape[4]
    per_dev = filters // (n_sy * n_af)
    below = from_behind(volume[:, -1:], "sx", 1)
    extended = jnp.concatenate([below, volume], axis=1)
    beside = from_behind(extended[:, :, -1:], "sy", 1)
    extended = jnp.concatenate([beside, extended], axis=2)
    extended = jnp.pad(extended, ((0, 0), (0, 0), (0, 0), (1, 0), (0, 0)))
    rows = samples * depth * height * width
    classes = parity_view(extended)
    cols = im2col(classes, depth, height, width).reshape(rows, -1)
    kernel_mat = kernel_full.reshape(-1, filters)
    total = jnp.dot(cols, kernel_mat, preferred_element_type=jnp.float32)
    n_sx = lax.axis_size("sx")
    conv_space = total.astype(jnp.bfloat16).reshape(depth, height, width, n_sy, n_af, per_dev)
    by_af = lax.all_to_all(conv_space.transpose(4, 3, 0, 1, 2, 5), "af", 0, 0, tiled=True)
    by_region = by_af.reshape(n_sx * n_sy, depth, height, width, per_dev)
    gathered = lax.all_to_all(by_region, ("sx", "sy"), 0, 0, tiled=True)
    own_samples = cotangent.shape[0]
    features = (
        gathered.reshape(n_sx, n_sy, depth, height, width, per_dev)
        .transpose(5, 0, 2, 1, 3, 4)
        .reshape(cotangent.shape)
    )
    grad_blocks = (
        cotangent.reshape(per_dev, n_sx, depth, n_sy, height, width)
        .transpose(1, 3, 2, 4, 5, 0)
        .reshape(n_sx * n_sy, depth, height, width, per_dev)
    )
    grad_region = lax.all_to_all(grad_blocks, ("sx", "sy"), 0, 0, tiled=True)
    grad_region = grad_region.reshape(n_sx * own_samples, n_sy, depth, height, width, per_dev)
    grad_back = lax.all_to_all(grad_region, "af", 0, 0, tiled=True)
    grad_back = grad_back.transpose(2, 3, 4, 1, 0, 5)
    grad_space = grad_back.reshape(samples, depth, height, width, filters)
    grad_flat = grad_space.reshape(rows, filters)
    by_parity = grad_flat.reshape(rows, n_sy * n_af // 2, 2, per_dev).transpose(0, 2, 1, 3)
    kernel_terms = lax.dot_general(
        by_parity.reshape(rows, filters), cols, (((0,), (0,)), ((), ())), preferred_element_type=jnp.float32
    )
    channels = kernel_full.shape[3]
    own_ch = channels // n_sx
    by_filter = reduce_filters(kernel_terms)
    by_filter = by_filter.reshape(per_dev, 27, n_sx, own_ch).transpose(2, 1, 3, 0)
    kernel_grad = lax.all_to_all(by_filter, "sx", 0, 0, tiled=True).sum(axis=0)
    kernel_grad = kernel_grad.reshape(3, 3, 3, own_ch, per_dev)
    partial_grad = spread_back(grad_space, kernel_full)
    from_above = from_behind(partial_grad[:, 0:1], "sx", -1)
    own_depth = partial_grad[:, 1:]
    own_depth = jnp.concatenate([own_depth[:, :-1], own_depth[:, -1:] + from_above], axis=1)
    from_right = from_behind(own_depth[:, :, 0:1].astype(jnp.bfloat16), "sy", -1).astype(
        jnp.float32
    )
    own_height = own_depth[:, :, 1:]
    own_height = jnp.concatenate(
        [own_height[:, :, :-1], own_height[:, :, -1:] + from_right], axis=2
    )
    volume_grad = own_height[:, :, :, 1:]
    return (features, volume_grad.astype(jnp.bfloat16), kernel_grad)


def solution(mesh):
    return jax.shard_map(
        on_device,
        mesh=mesh,
        in_specs=(
            P("af", "sx", "sy", None, None),
            P(None, None, None, "sx", ("sy", "af")),
            P("sx", ("sy", "af"), None, None),
        ),
        out_specs=(
            P("sx", ("sy", "af"), None, None),
            P("af", "sx", "sy", None, None),
            P(None, None, None, "sx", ("sy", "af")),
        ),
        check_vma=False,
    )
```

```python
import functools

import jax
import jax.numpy as jnp
from jax import lax
from jax.experimental import pallas as pl
from jax.experimental.pallas import tpu as pltpu
from jax.sharding import PartitionSpec as P


def _gather_body(n_sy, n_af, block_ref, out_ref, send_sem, recv_sem):
    group = n_sy * n_af
    sx = lax.axis_index("sx")
    me = lax.axis_index("sy") * n_af + lax.axis_index("af")
    barrier = pltpu.get_barrier_semaphore()
    for step in range(1, group):
        peer = lax.rem(me + step, group)
        pl.semaphore_signal(
            barrier,
            inc=1,
            device_id=(sx, peer // n_af, lax.rem(peer, n_af)),
            device_id_type=pl.DeviceIdType.MESH,
        )
    pl.semaphore_wait(barrier, group - 1)
    copies = []
    for step in range(1, group):
        peer = lax.rem(me + step, group)
        copy = pltpu.make_async_remote_copy(
            src_ref=block_ref,
            dst_ref=out_ref.at[me],
            send_sem=send_sem.at[step - 1],
            recv_sem=recv_sem.at[step - 1],
            device_id=(sx, peer // n_af, lax.rem(peer, n_af)),
            device_id_type=pl.DeviceIdType.MESH,
        )
        copy.start()
        copies.append(copy)
    out_ref[me] = block_ref[...]
    for copy in copies:
        copy.wait_send()
    for step in range(1, group):
        source = lax.rem(me + group - step, group)
        incoming = pltpu.make_async_remote_copy(
            src_ref=block_ref,
            dst_ref=out_ref.at[source],
            send_sem=send_sem.at[step - 1],
            recv_sem=recv_sem.at[step - 1],
            device_id=(sx, source // n_af, lax.rem(source, n_af)),
            device_id_type=pl.DeviceIdType.MESH,
        )
        incoming.wait_recv()


def _reduce_body(n_sy, n_af, terms_ref, out_ref, from_sib, mine, held, sib_send, sib_recv, send_sem, recv_sem):
    half = n_sy * n_af // 2
    rows = out_ref.shape[0]
    span = half * rows
    sx = lax.axis_index("sx")
    sy = lax.axis_index("sy")
    af = lax.axis_index("af")
    parity = lax.rem(af, 2)
    sib_af = af + 1 - 2 * parity
    me = sy * (n_af // 2) + af // 2

    def peer_of(index):
        block = 2 * index + parity
        return (sx, block // n_af, lax.rem(block, n_af))

    barrier = pltpu.get_barrier_semaphore()
    pl.semaphore_signal(barrier, inc=1, device_id=(sx, sy, sib_af), device_id_type=pl.DeviceIdType.MESH)
    for step in range(1, half):
        pl.semaphore_signal(
            barrier,
            inc=1,
            device_id=peer_of(lax.rem(me + step, half)),
            device_id_type=pl.DeviceIdType.MESH,
        )
    pl.semaphore_wait(barrier, half)
    to_sib = pltpu.make_async_remote_copy(
        src_ref=terms_ref.at[pl.ds(pl.multiple_of((1 - parity) * span, span), span)],
        dst_ref=from_sib,
        send_sem=sib_send,
        recv_sem=sib_recv,
        device_id=(sx, sy, sib_af),
        device_id_type=pl.DeviceIdType.MESH,
    )
    to_sib.start()
    to_sib.wait_send()
    to_sib.wait_recv()
    mine[...] = terms_ref[pl.ds(pl.multiple_of(parity * span, span), span), :] + from_sib[...]
    copies = []
    for step in range(1, half):
        peer = lax.rem(me + step, half)
        copy = pltpu.make_async_remote_copy(
            src_ref=mine.at[pl.ds(pl.multiple_of(peer * rows, rows), rows)],
            dst_ref=held.at[me],
            send_sem=send_sem.at[step - 1],
            recv_sem=recv_sem.at[step - 1],
            device_id=peer_of(peer),
            device_id_type=pl.DeviceIdType.MESH,
        )
        copy.start()
        copies.append(copy)
    total = mine[pl.ds(pl.multiple_of(me * rows, rows), rows), :]
    for copy in copies:
        copy.wait_send()
    for step in range(1, half):
        source = lax.rem(me + half - step, half)
        incoming = pltpu.make_async_remote_copy(
            src_ref=mine.at[pl.ds(0, rows)],
            dst_ref=held.at[source],
            send_sem=send_sem.at[step - 1],
            recv_sem=recv_sem.at[step - 1],
            device_id=peer_of(source),
            device_id_type=pl.DeviceIdType.MESH,
        )
        incoming.wait_recv()
        total = total + held[source]
    out_ref[...] = total


def reduce_filters(terms):
    n_sy = lax.axis_size("sy")
    n_af = lax.axis_size("af")
    group = n_sy * n_af
    rows = terms.shape[0] // group
    return pl.pallas_call(
        functools.partial(_reduce_body, n_sy, n_af),
        out_shape=jax.ShapeDtypeStruct((rows, terms.shape[1]), terms.dtype),
        in_specs=[pl.BlockSpec(memory_space=pltpu.VMEM)],
        out_specs=pl.BlockSpec(memory_space=pltpu.VMEM),
        scratch_shapes=[
            pltpu.VMEM((group // 2 * rows, terms.shape[1]), terms.dtype),
            pltpu.VMEM((group // 2 * rows, terms.shape[1]), terms.dtype),
            pltpu.VMEM((group // 2, rows, terms.shape[1]), terms.dtype),
            pltpu.SemaphoreType.DMA(()),
            pltpu.SemaphoreType.DMA(()),
            pltpu.SemaphoreType.DMA((group // 2 - 1,)),
            pltpu.SemaphoreType.DMA((group // 2 - 1,)),
        ],
        compiler_params=pltpu.CompilerParams(collective_id=1, has_side_effects=True),
        cost_estimate=pl.CostEstimate(
            flops=terms.size, bytes_accessed=2 * terms.size * 4, transcendentals=0
        ),
    )(terms)


def gather_filters(kernel):
    n_sy = lax.axis_size("sy")
    n_af = lax.axis_size("af")
    group = n_sy * n_af
    taps, channels, per_dev = kernel.shape[0] * kernel.shape[1] * kernel.shape[2], kernel.shape[3], kernel.shape[4]
    block = kernel.reshape(-1, 128)
    gathered = pl.pallas_call(
        functools.partial(_gather_body, n_sy, n_af),
        out_shape=jax.ShapeDtypeStruct((group,) + block.shape, block.dtype),
        in_specs=[pl.BlockSpec(memory_space=pltpu.VMEM)],
        out_specs=pl.BlockSpec(memory_space=pltpu.VMEM),
        scratch_shapes=[
            pltpu.SemaphoreType.DMA((group - 1,)),
            pltpu.SemaphoreType.DMA((group - 1,)),
        ],
        compiler_params=pltpu.CompilerParams(collective_id=0, has_side_effects=True),
    )(block)
    gathered = gathered.reshape(group, taps, channels, per_dev).transpose(1, 2, 0, 3)
    return gathered.reshape(kernel.shape[:4] + (group * per_dev,))


def from_behind(value, axis, steps):
    count = lax.axis_size(axis)
    leading, last = (max(0, -steps), min(count, count - steps))
    return lax.ppermute(value, axis, [(source, source + steps) for source in range(leading, last)])


def strided_patch(extended, tap_d, tap_h, tap_w, depth, height, width):
    return extended[
        :,
        tap_d : tap_d + 2 * depth : 2,
        tap_h : tap_h + 2 * height : 2,
        tap_w : tap_w + 2 * width : 2,
        :,
    ]


def parity_view(extended):
    samples, d_ext, h_ext, w_ext, channels = extended.shape
    pads = [(0, 0)] + [(0, n % 2) for n in (d_ext, h_ext, w_ext)] + [(0, 0)]
    even = jnp.pad(extended, pads)
    _, d2, h2, w2, _ = even.shape
    split = even.reshape(samples, d2 // 2, 2, h2 // 2, 2, w2 // 2, 2, channels)
    return split.transpose(2, 4, 6, 0, 1, 3, 5, 7)


def im2col(classes, depth, height, width):
    patches = []
    for tap_d in range(3):
        for tap_h in range(3):
            for tap_w in range(3):
                cls = classes[tap_d % 2, tap_h % 2, tap_w % 2]
                od, oh, ow = tap_d // 2, tap_h // 2, tap_w // 2
                patches.append(cls[:, od : od + depth, oh : oh + height, ow : ow + width, :])
    return jnp.concatenate(patches, axis=-1)


def weave(even_part, odd_part, axis):
    stacked = jnp.stack([even_part, odd_part], axis=axis + 1)
    shape = list(even_part.shape)
    shape[axis] = shape[axis] * 2
    return stacked.reshape(shape)


def spread_back(grad_t, kernel_full, samples, depth, height, width):
    filters = grad_t.shape[0]
    channels = kernel_full.shape[3]
    spread = lax.dot_general(
        grad_t,
        kernel_full.reshape(-1, channels, filters),
        (((0,), (2,)), ((), ())),
        preferred_element_type=jnp.float32,
    ).reshape(samples, depth, height, width, 27, channels)
    classes = {}
    for tap_d in range(3):
        for tap_h in range(3):
            for tap_w in range(3):
                term = spread[:, :, :, :, tap_d * 9 + tap_h * 3 + tap_w]
                pads = [(0, 0)]
                for tap in (tap_d, tap_h, tap_w):
                    pads.append((1, 0) if tap == 2 else (0, 1))
                pads.append((0, 0))
                term = jnp.pad(term, pads)
                key_name = (tap_d % 2, tap_h % 2, tap_w % 2)
                classes[key_name] = classes[key_name] + term if key_name in classes else term
    planes = []
    for parity_d in range(2):
        rows_h = []
        for parity_h in range(2):
            rows_h.append(weave(classes[parity_d, parity_h, 0], classes[parity_d, parity_h, 1], 3))
        planes.append(weave(rows_h[0], rows_h[1], 2))
    whole = weave(planes[0], planes[1], 1)
    return whole[:, : 2 * depth + 1, : 2 * height + 1, : 2 * width + 1, :]


def on_device(volume, kernel, cotangent):
    samples = volume.shape[0]
    depth = volume.shape[1] // 2
    height = volume.shape[2] // 2
    width = volume.shape[3] // 2
    n_sy = lax.axis_size("sy")
    n_af = lax.axis_size("af")
    kernel_part = gather_filters(kernel)
    kernel_full = lax.all_gather(kernel_part, "sx", axis=3, tiled=True)
    filters = kernel_full.shape[4]
    per_dev = filters // (n_sy * n_af)
    below = from_behind(volume[:, -1:], "sx", 1)
    extended = jnp.concatenate([below, volume], axis=1)
    beside = from_behind(extended[:, :, -1:], "sy", 1)
    extended = jnp.concatenate([beside, extended], axis=2)
    extended = jnp.pad(extended, ((0, 0), (0, 0), (0, 0), (1, 0), (0, 0)))
    rows = samples * depth * height * width
    classes = parity_view(extended)
    cols = im2col(classes, depth, height, width).reshape(rows, -1)
    kernel_mat = kernel_full.reshape(-1, filters)
    total = lax.dot_general(
        kernel_mat, cols, (((0,), (1,)), ((), ())), preferred_element_type=jnp.float32
    )
    n_sx = lax.axis_size("sx")
    conv_t = total.astype(jnp.bfloat16).reshape(n_sy, n_af, per_dev, depth, height, width)
    by_af = lax.all_to_all(conv_t.transpose(1, 0, 2, 3, 4, 5), "af", 0, 0, tiled=True)
    by_region = by_af.reshape(n_sx * n_sy, per_dev, depth, height, width)
    gathered = lax.all_to_all(by_region, ("sx", "sy"), 0, 0, tiled=True)
    own_samples = cotangent.shape[0]
    features = (
        gathered.reshape(n_sx, n_sy, per_dev, depth, height, width)
        .transpose(2, 0, 3, 1, 4, 5)
        .reshape(cotangent.shape)
    )
    grad_blocks = (
        cotangent.reshape(per_dev, n_sx, depth, n_sy, height, width)
        .transpose(1, 3, 0, 2, 4, 5)
        .reshape(n_sx * n_sy, per_dev, depth, height, width)
    )
    grad_region = lax.all_to_all(grad_blocks, ("sx", "sy"), 0, 0, tiled=True)
    grad_region = grad_region.reshape(n_sx * own_samples, n_sy, per_dev, depth, height, width)
    grad_back = lax.all_to_all(grad_region, "af", 0, 0, tiled=True)
    grad_t = grad_back.transpose(1, 0, 2, 3, 4, 5).reshape(filters, rows)
    by_parity = grad_t.reshape(n_sy * n_af // 2, 2, per_dev, rows).transpose(1, 0, 2, 3)
    kernel_terms = lax.dot_general(
        by_parity.reshape(filters, rows), cols, (((1,), (0,)), ((), ())),
        preferred_element_type=jnp.float32,
    )
    channels = kernel_full.shape[3]
    own_ch = channels // n_sx
    by_filter = reduce_filters(kernel_terms)
    by_filter = by_filter.reshape(per_dev, 27, n_sx, own_ch).transpose(2, 1, 3, 0)
    kernel_grad = lax.all_to_all(by_filter, "sx", 0, 0, tiled=True).sum(axis=0)
    kernel_grad = kernel_grad.reshape(3, 3, 3, own_ch, per_dev)
    partial_grad = spread_back(grad_t, kernel_full, samples, depth, height, width)
    from_above = from_behind(partial_grad[:, 0:1], "sx", -1)
    own_depth = partial_grad[:, 1:]
    own_depth = jnp.concatenate([own_depth[:, :-1], own_depth[:, -1:] + from_above], axis=1)
    from_right = from_behind(own_depth[:, :, 0:1].astype(jnp.bfloat16), "sy", -1).astype(
        jnp.float32
    )
    own_height = own_depth[:, :, 1:]
    own_height = jnp.concatenate(
        [own_height[:, :, :-1], own_height[:, :, -1:] + from_right], axis=2
    )
    volume_grad = own_height[:, :, :, 1:]
    return (features, volume_grad.astype(jnp.bfloat16), kernel_grad)


def solution(mesh):
    return jax.shard_map(
        on_device,
        mesh=mesh,
        in_specs=(
            P("af", "sx", "sy", None, None),
            P(None, None, None, "sx", ("sy", "af")),
            P("sx", ("sy", "af"), None, None),
        ),
        out_specs=(
            P("sx", ("sy", "af"), None, None),
            P("af", "sx", "sy", None, None),
            P(None, None, None, "sx", ("sy", "af")),
        ),
        check_vma=False,
    )
```

```python
import functools

import jax
import jax.numpy as jnp
from jax import lax
from jax.experimental import pallas as pl
from jax.experimental.pallas import tpu as pltpu
from jax.sharding import PartitionSpec as P


def _gather_body(n_sy, n_af, block_ref, out_ref, send_sem, recv_sem):
    group = n_sy * n_af
    sx = lax.axis_index("sx")
    me = lax.axis_index("sy") * n_af + lax.axis_index("af")
    barrier = pltpu.get_barrier_semaphore()
    for step in range(1, group):
        peer = lax.rem(me + step, group)
        pl.semaphore_signal(
            barrier,
            inc=1,
            device_id=(sx, peer // n_af, lax.rem(peer, n_af)),
            device_id_type=pl.DeviceIdType.MESH,
        )
    pl.semaphore_wait(barrier, group - 1)
    copies = []
    for step in range(1, group):
        peer = lax.rem(me + step, group)
        copy = pltpu.make_async_remote_copy(
            src_ref=block_ref,
            dst_ref=out_ref.at[me],
            send_sem=send_sem.at[step - 1],
            recv_sem=recv_sem.at[step - 1],
            device_id=(sx, peer // n_af, lax.rem(peer, n_af)),
            device_id_type=pl.DeviceIdType.MESH,
        )
        copy.start()
        copies.append(copy)
    out_ref[me] = block_ref[...]
    for copy in copies:
        copy.wait_send()
    for step in range(1, group):
        source = lax.rem(me + group - step, group)
        incoming = pltpu.make_async_remote_copy(
            src_ref=block_ref,
            dst_ref=out_ref.at[source],
            send_sem=send_sem.at[step - 1],
            recv_sem=recv_sem.at[step - 1],
            device_id=(sx, source // n_af, lax.rem(source, n_af)),
            device_id_type=pl.DeviceIdType.MESH,
        )
        incoming.wait_recv()


def _reduce_body(n_sy, n_af, terms_ref, out_ref, from_sib, mine, held, sib_send, sib_recv, send_sem, recv_sem):
    half = n_sy * n_af // 2
    rows = out_ref.shape[0]
    span = half * rows
    sx = lax.axis_index("sx")
    sy = lax.axis_index("sy")
    af = lax.axis_index("af")
    parity = lax.rem(af, 2)
    sib_af = af + 1 - 2 * parity
    me = sy * (n_af // 2) + af // 2

    def peer_of(index):
        block = 2 * index + parity
        return (sx, block // n_af, lax.rem(block, n_af))

    barrier = pltpu.get_barrier_semaphore()
    pl.semaphore_signal(barrier, inc=1, device_id=(sx, sy, sib_af), device_id_type=pl.DeviceIdType.MESH)
    for step in range(1, half):
        pl.semaphore_signal(
            barrier,
            inc=1,
            device_id=peer_of(lax.rem(me + step, half)),
            device_id_type=pl.DeviceIdType.MESH,
        )
    pl.semaphore_wait(barrier, half)
    to_sib = pltpu.make_async_remote_copy(
        src_ref=terms_ref.at[pl.ds(pl.multiple_of((1 - parity) * span, span), span)],
        dst_ref=from_sib,
        send_sem=sib_send,
        recv_sem=sib_recv,
        device_id=(sx, sy, sib_af),
        device_id_type=pl.DeviceIdType.MESH,
    )
    to_sib.start()
    to_sib.wait_send()
    to_sib.wait_recv()
    mine[...] = terms_ref[pl.ds(pl.multiple_of(parity * span, span), span), :] + from_sib[...]
    copies = []
    for step in range(1, half):
        peer = lax.rem(me + step, half)
        copy = pltpu.make_async_remote_copy(
            src_ref=mine.at[pl.ds(pl.multiple_of(peer * rows, rows), rows)],
            dst_ref=held.at[me],
            send_sem=send_sem.at[step - 1],
            recv_sem=recv_sem.at[step - 1],
            device_id=peer_of(peer),
            device_id_type=pl.DeviceIdType.MESH,
        )
        copy.start()
        copies.append(copy)
    total = mine[pl.ds(pl.multiple_of(me * rows, rows), rows), :]
    for copy in copies:
        copy.wait_send()
    for step in range(1, half):
        source = lax.rem(me + half - step, half)
        incoming = pltpu.make_async_remote_copy(
            src_ref=mine.at[pl.ds(0, rows)],
            dst_ref=held.at[source],
            send_sem=send_sem.at[step - 1],
            recv_sem=recv_sem.at[step - 1],
            device_id=peer_of(source),
            device_id_type=pl.DeviceIdType.MESH,
        )
        incoming.wait_recv()
        total = total + held[source]
    out_ref[...] = total


def reduce_filters(terms):
    n_sy = lax.axis_size("sy")
    n_af = lax.axis_size("af")
    group = n_sy * n_af
    rows = terms.shape[0] // group
    return pl.pallas_call(
        functools.partial(_reduce_body, n_sy, n_af),
        out_shape=jax.ShapeDtypeStruct((rows, terms.shape[1]), terms.dtype),
        in_specs=[pl.BlockSpec(memory_space=pltpu.VMEM)],
        out_specs=pl.BlockSpec(memory_space=pltpu.VMEM),
        scratch_shapes=[
            pltpu.VMEM((group // 2 * rows, terms.shape[1]), terms.dtype),
            pltpu.VMEM((group // 2 * rows, terms.shape[1]), terms.dtype),
            pltpu.VMEM((group // 2, rows, terms.shape[1]), terms.dtype),
            pltpu.SemaphoreType.DMA(()),
            pltpu.SemaphoreType.DMA(()),
            pltpu.SemaphoreType.DMA((group // 2 - 1,)),
            pltpu.SemaphoreType.DMA((group // 2 - 1,)),
        ],
        compiler_params=pltpu.CompilerParams(collective_id=1, has_side_effects=True),
        cost_estimate=pl.CostEstimate(
            flops=terms.size, bytes_accessed=2 * terms.size * 4, transcendentals=0
        ),
    )(terms)


def gather_filters(kernel):
    n_sy = lax.axis_size("sy")
    n_af = lax.axis_size("af")
    group = n_sy * n_af
    taps, channels, per_dev = kernel.shape[0] * kernel.shape[1] * kernel.shape[2], kernel.shape[3], kernel.shape[4]
    block = kernel.reshape(-1, 128)
    gathered = pl.pallas_call(
        functools.partial(_gather_body, n_sy, n_af),
        out_shape=jax.ShapeDtypeStruct((group,) + block.shape, block.dtype),
        in_specs=[pl.BlockSpec(memory_space=pltpu.VMEM)],
        out_specs=pl.BlockSpec(memory_space=pltpu.VMEM),
        scratch_shapes=[
            pltpu.SemaphoreType.DMA((group - 1,)),
            pltpu.SemaphoreType.DMA((group - 1,)),
        ],
        compiler_params=pltpu.CompilerParams(collective_id=0, has_side_effects=True),
    )(block)
    gathered = gathered.reshape(group, taps, channels, per_dev).transpose(1, 2, 0, 3)
    return gathered.reshape(kernel.shape[:4] + (group * per_dev,))


def flat_all_to_all(x, axes):
    moved = lax.all_to_all(x.reshape(x.shape[0], 2, -1), axes, 0, 0, tiled=True)
    return moved.reshape(x.shape)


def from_behind(value, axis, steps):
    count = lax.axis_size(axis)
    leading, last = (max(0, -steps), min(count, count - steps))
    return lax.ppermute(value, axis, [(source, source + steps) for source in range(leading, last)])


def strided_patch(extended, tap_d, tap_h, tap_w, depth, height, width):
    return extended[
        :,
        tap_d : tap_d + 2 * depth : 2,
        tap_h : tap_h + 2 * height : 2,
        tap_w : tap_w + 2 * width : 2,
        :,
    ]


def parity_view(extended):
    samples, d_ext, h_ext, w_ext, channels = extended.shape
    pads = [(0, 0)] + [(0, n % 2) for n in (d_ext, h_ext, w_ext)] + [(0, 0)]
    even = jnp.pad(extended, pads)
    _, d2, h2, w2, _ = even.shape
    split = even.reshape(samples, d2 // 2, 2, h2 // 2, 2, w2 // 2, 2, channels)
    return split.transpose(2, 4, 6, 0, 1, 3, 5, 7)


def im2col(classes, depth, height, width):
    patches = []
    for tap_d in range(3):
        for tap_h in range(3):
            for tap_w in range(3):
                cls = classes[tap_d % 2, tap_h % 2, tap_w % 2]
                od, oh, ow = tap_d // 2, tap_h // 2, tap_w // 2
                patches.append(cls[:, od : od + depth, oh : oh + height, ow : ow + width, :])
    return jnp.concatenate(patches, axis=-1)


def weave(even_part, odd_part, axis):
    stacked = jnp.stack([even_part, odd_part], axis=axis + 1)
    shape = list(even_part.shape)
    shape[axis] = shape[axis] * 2
    return stacked.reshape(shape)


def spread_back(grad_t, kernel_full, samples, depth, height, width):
    filters = grad_t.shape[0]
    channels = kernel_full.shape[3]
    spread = lax.dot_general(
        grad_t,
        kernel_full.reshape(-1, channels, filters),
        (((0,), (2,)), ((), ())),
        preferred_element_type=jnp.float32,
    ).reshape(samples, depth, height, width, 27, channels)
    classes = {}
    for tap_d in range(3):
        for tap_h in range(3):
            for tap_w in range(3):
                term = spread[:, :, :, :, tap_d * 9 + tap_h * 3 + tap_w]
                pads = [(0, 0)]
                for tap in (tap_d, tap_h, tap_w):
                    pads.append((1, 0) if tap == 2 else (0, 1))
                pads.append((0, 0))
                term = jnp.pad(term, pads)
                key_name = (tap_d % 2, tap_h % 2, tap_w % 2)
                classes[key_name] = classes[key_name] + term if key_name in classes else term
    planes = []
    for parity_d in range(2):
        rows_h = []
        for parity_h in range(2):
            rows_h.append(weave(classes[parity_d, parity_h, 0], classes[parity_d, parity_h, 1], 3))
        planes.append(weave(rows_h[0], rows_h[1], 2))
    whole = weave(planes[0], planes[1], 1)
    return whole[:, : 2 * depth + 1, : 2 * height + 1, : 2 * width + 1, :]


def on_device(volume, kernel, cotangent):
    samples = volume.shape[0]
    depth = volume.shape[1] // 2
    height = volume.shape[2] // 2
    width = volume.shape[3] // 2
    n_sy = lax.axis_size("sy")
    n_af = lax.axis_size("af")
    kernel_part = gather_filters(kernel)
    kernel_full = lax.all_gather(kernel_part, "sx", axis=3, tiled=True)
    filters = kernel_full.shape[4]
    per_dev = filters // (n_sy * n_af)
    below = from_behind(volume[:, -1:], "sx", 1)
    extended = jnp.concatenate([below, volume], axis=1)
    beside = from_behind(extended[:, :, -1:], "sy", 1)
    extended = jnp.concatenate([beside, extended], axis=2)
    extended = jnp.pad(extended, ((0, 0), (0, 0), (0, 0), (1, 0), (0, 0)))
    rows = samples * depth * height * width
    classes = parity_view(extended)
    cols = im2col(classes, depth, height, width).reshape(rows, -1)
    kernel_mat = kernel_full.reshape(-1, filters)
    total = lax.dot_general(
        kernel_mat, cols, (((0,), (1,)), ((), ())), preferred_element_type=jnp.float32
    )
    n_sx = lax.axis_size("sx")
    conv_t = total.astype(jnp.bfloat16).reshape(n_sy, n_af, per_dev, depth, height, width)
    by_af = flat_all_to_all(conv_t.transpose(1, 0, 2, 3, 4, 5), "af")
    by_region = by_af.reshape(n_sx * n_sy, per_dev, depth, height, width)
    gathered = flat_all_to_all(by_region, ("sx", "sy"))
    own_samples = cotangent.shape[0]
    features = (
        gathered.reshape(n_sx, n_sy, per_dev, depth, height, width)
        .transpose(2, 0, 3, 1, 4, 5)
        .reshape(cotangent.shape)
    )
    grad_blocks = (
        cotangent.reshape(per_dev, n_sx, depth, n_sy, height, width)
        .transpose(1, 3, 0, 2, 4, 5)
        .reshape(n_sx * n_sy, per_dev, depth, height, width)
    )
    grad_region = flat_all_to_all(grad_blocks, ("sx", "sy"))
    grad_region = grad_region.reshape(n_sx * own_samples, n_sy, per_dev, depth, height, width)
    grad_back = flat_all_to_all(grad_region, "af")
    grad_t = grad_back.transpose(1, 0, 2, 3, 4, 5).reshape(filters, rows)
    by_parity = grad_t.reshape(n_sy * n_af // 2, 2, per_dev, rows).transpose(1, 0, 2, 3)
    kernel_terms = lax.dot_general(
        by_parity.reshape(filters, rows), cols, (((1,), (0,)), ((), ())),
        preferred_element_type=jnp.float32,
    )
    channels = kernel_full.shape[3]
    own_ch = channels // n_sx
    by_filter = reduce_filters(kernel_terms)
    by_filter = by_filter.reshape(per_dev, 27, n_sx, own_ch).transpose(2, 1, 3, 0)
    kernel_grad = lax.all_to_all(by_filter, "sx", 0, 0, tiled=True).sum(axis=0)
    kernel_grad = kernel_grad.reshape(3, 3, 3, own_ch, per_dev)
    partial_grad = spread_back(grad_t, kernel_full, samples, depth, height, width)
    from_above = from_behind(partial_grad[:, 0:1], "sx", -1)
    own_depth = partial_grad[:, 1:]
    own_depth = jnp.concatenate([own_depth[:, :-1], own_depth[:, -1:] + from_above], axis=1)
    from_right = from_behind(own_depth[:, :, 0:1].astype(jnp.bfloat16), "sy", -1).astype(
        jnp.float32
    )
    own_height = own_depth[:, :, 1:]
    own_height = jnp.concatenate(
        [own_height[:, :, :-1], own_height[:, :, -1:] + from_right], axis=2
    )
    volume_grad = own_height[:, :, :, 1:]
    return (features, volume_grad.astype(jnp.bfloat16), kernel_grad)


def solution(mesh):
    return jax.shard_map(
        on_device,
        mesh=mesh,
        in_specs=(
            P("af", "sx", "sy", None, None),
            P(None, None, None, "sx", ("sy", "af")),
            P("sx", ("sy", "af"), None, None),
        ),
        out_specs=(
            P("sx", ("sy", "af"), None, None),
            P("af", "sx", "sy", None, None),
            P(None, None, None, "sx", ("sy", "af")),
        ),
        check_vma=False,
    )
```

```python
import functools

import jax
import jax.numpy as jnp
from jax import lax
from jax.experimental import pallas as pl
from jax.experimental.pallas import tpu as pltpu
from jax.sharding import PartitionSpec as P


def _gather_body(n_sy, n_af, block_ref, out_ref, send_sem, recv_sem):
    group = n_sy * n_af
    sx = lax.axis_index("sx")
    me = lax.axis_index("sy") * n_af + lax.axis_index("af")
    barrier = pltpu.get_barrier_semaphore()
    for step in range(1, group):
        peer = lax.rem(me + step, group)
        pl.semaphore_signal(
            barrier,
            inc=1,
            device_id=(sx, peer // n_af, lax.rem(peer, n_af)),
            device_id_type=pl.DeviceIdType.MESH,
        )
    pl.semaphore_wait(barrier, group - 1)
    copies = []
    for step in range(1, group):
        peer = lax.rem(me + step, group)
        copy = pltpu.make_async_remote_copy(
            src_ref=block_ref,
            dst_ref=out_ref.at[me],
            send_sem=send_sem.at[step - 1],
            recv_sem=recv_sem.at[step - 1],
            device_id=(sx, peer // n_af, lax.rem(peer, n_af)),
            device_id_type=pl.DeviceIdType.MESH,
        )
        copy.start()
        copies.append(copy)
    out_ref[me] = block_ref[...]
    for copy in copies:
        copy.wait_send()
    for step in range(1, group):
        source = lax.rem(me + group - step, group)
        incoming = pltpu.make_async_remote_copy(
            src_ref=block_ref,
            dst_ref=out_ref.at[source],
            send_sem=send_sem.at[step - 1],
            recv_sem=recv_sem.at[step - 1],
            device_id=(sx, source // n_af, lax.rem(source, n_af)),
            device_id_type=pl.DeviceIdType.MESH,
        )
        incoming.wait_recv()


def _reduce_body(n_sy, n_af, terms_ref, out_ref, from_sib, mine, held, sib_send, sib_recv, send_sem, recv_sem):
    half = n_sy * n_af // 2
    rows = out_ref.shape[0]
    span = half * rows
    sx = lax.axis_index("sx")
    sy = lax.axis_index("sy")
    af = lax.axis_index("af")
    parity = lax.rem(af, 2)
    sib_af = af + 1 - 2 * parity
    me = sy * (n_af // 2) + af // 2

    def peer_of(index):
        block = 2 * index + parity
        return (sx, block // n_af, lax.rem(block, n_af))

    barrier = pltpu.get_barrier_semaphore()
    pl.semaphore_signal(barrier, inc=1, device_id=(sx, sy, sib_af), device_id_type=pl.DeviceIdType.MESH)
    for step in range(1, half):
        pl.semaphore_signal(
            barrier,
            inc=1,
            device_id=peer_of(lax.rem(me + step, half)),
            device_id_type=pl.DeviceIdType.MESH,
        )
    pl.semaphore_wait(barrier, half)
    to_sib = pltpu.make_async_remote_copy(
        src_ref=terms_ref.at[pl.ds(pl.multiple_of((1 - parity) * span, span), span)],
        dst_ref=from_sib,
        send_sem=sib_send,
        recv_sem=sib_recv,
        device_id=(sx, sy, sib_af),
        device_id_type=pl.DeviceIdType.MESH,
    )
    to_sib.start()
    to_sib.wait_send()
    to_sib.wait_recv()
    mine[...] = terms_ref[pl.ds(pl.multiple_of(parity * span, span), span), :] + from_sib[...]
    copies = []
    for step in range(1, half):
        peer = lax.rem(me + step, half)
        copy = pltpu.make_async_remote_copy(
            src_ref=mine.at[pl.ds(pl.multiple_of(peer * rows, rows), rows)],
            dst_ref=held.at[me],
            send_sem=send_sem.at[step - 1],
            recv_sem=recv_sem.at[step - 1],
            device_id=peer_of(peer),
            device_id_type=pl.DeviceIdType.MESH,
        )
        copy.start()
        copies.append(copy)
    total = mine[pl.ds(pl.multiple_of(me * rows, rows), rows), :]
    for copy in copies:
        copy.wait_send()
    for step in range(1, half):
        source = lax.rem(me + half - step, half)
        incoming = pltpu.make_async_remote_copy(
            src_ref=mine.at[pl.ds(0, rows)],
            dst_ref=held.at[source],
            send_sem=send_sem.at[step - 1],
            recv_sem=recv_sem.at[step - 1],
            device_id=peer_of(source),
            device_id_type=pl.DeviceIdType.MESH,
        )
        incoming.wait_recv()
        total = total + held[source]
    out_ref[...] = total


def reduce_filters(terms):
    n_sy = lax.axis_size("sy")
    n_af = lax.axis_size("af")
    group = n_sy * n_af
    rows = terms.shape[0] // group
    return pl.pallas_call(
        functools.partial(_reduce_body, n_sy, n_af),
        out_shape=jax.ShapeDtypeStruct((rows, terms.shape[1]), terms.dtype),
        in_specs=[pl.BlockSpec(memory_space=pltpu.VMEM)],
        out_specs=pl.BlockSpec(memory_space=pltpu.VMEM),
        scratch_shapes=[
            pltpu.VMEM((group // 2 * rows, terms.shape[1]), terms.dtype),
            pltpu.VMEM((group // 2 * rows, terms.shape[1]), terms.dtype),
            pltpu.VMEM((group // 2, rows, terms.shape[1]), terms.dtype),
            pltpu.SemaphoreType.DMA(()),
            pltpu.SemaphoreType.DMA(()),
            pltpu.SemaphoreType.DMA((group // 2 - 1,)),
            pltpu.SemaphoreType.DMA((group // 2 - 1,)),
        ],
        compiler_params=pltpu.CompilerParams(collective_id=1, has_side_effects=True),
        cost_estimate=pl.CostEstimate(
            flops=terms.size, bytes_accessed=2 * terms.size * 4, transcendentals=0
        ),
    )(terms)


def gather_filters(kernel):
    n_sy = lax.axis_size("sy")
    n_af = lax.axis_size("af")
    group = n_sy * n_af
    taps, channels, per_dev = kernel.shape[0] * kernel.shape[1] * kernel.shape[2], kernel.shape[3], kernel.shape[4]
    block = kernel.reshape(-1, 128)
    gathered = pl.pallas_call(
        functools.partial(_gather_body, n_sy, n_af),
        out_shape=jax.ShapeDtypeStruct((group,) + block.shape, block.dtype),
        in_specs=[pl.BlockSpec(memory_space=pltpu.VMEM)],
        out_specs=pl.BlockSpec(memory_space=pltpu.VMEM),
        scratch_shapes=[
            pltpu.SemaphoreType.DMA((group - 1,)),
            pltpu.SemaphoreType.DMA((group - 1,)),
        ],
        compiler_params=pltpu.CompilerParams(collective_id=0, has_side_effects=True),
    )(block)
    gathered = gathered.reshape(group, taps, channels, per_dev).transpose(1, 2, 0, 3)
    return gathered.reshape(kernel.shape[:4] + (group * per_dev,))


def flat_all_to_all(x, axes):
    moved = lax.all_to_all(x.reshape(x.shape[0], 2, -1), axes, 0, 0, tiled=True)
    return moved.reshape(x.shape)


def from_behind(value, axis, steps):
    count = lax.axis_size(axis)
    leading, last = (max(0, -steps), min(count, count - steps))
    return lax.ppermute(value, axis, [(source, source + steps) for source in range(leading, last)])


def strided_patch(extended, tap_d, tap_h, tap_w, depth, height, width):
    return extended[
        :,
        tap_d : tap_d + 2 * depth : 2,
        tap_h : tap_h + 2 * height : 2,
        tap_w : tap_w + 2 * width : 2,
        :,
    ]


def parity_view(extended):
    samples, d_ext, h_ext, w_ext, channels = extended.shape
    pads = [(0, 0)] + [(0, n % 2) for n in (d_ext, h_ext, w_ext)] + [(0, 0)]
    even = jnp.pad(extended, pads)
    _, d2, h2, w2, _ = even.shape
    split = even.reshape(samples, d2 // 2, 2, h2 // 2, 2, w2 // 2, 2, channels)
    return split.transpose(2, 4, 6, 0, 1, 3, 5, 7)


def im2col(classes, depth, height, width):
    patches = []
    for tap_d in range(3):
        for tap_h in range(3):
            for tap_w in range(3):
                cls = classes[tap_d % 2, tap_h % 2, tap_w % 2]
                od, oh, ow = tap_d // 2, tap_h // 2, tap_w // 2
                patches.append(cls[:, od : od + depth, oh : oh + height, ow : ow + width, :])
    return jnp.concatenate(patches, axis=-1)


def weave(even_part, odd_part, axis):
    stacked = jnp.stack([even_part, odd_part], axis=axis + 1)
    shape = list(even_part.shape)
    shape[axis] = shape[axis] * 2
    return stacked.reshape(shape)


def spread_back(grad_t, kernel_full, samples, depth, height, width):
    filters = grad_t.shape[0]
    channels = kernel_full.shape[3]
    spread = lax.dot_general(
        grad_t,
        kernel_full.reshape(-1, channels, filters),
        (((0,), (2,)), ((), ())),
        preferred_element_type=jnp.float32,
    ).reshape(samples, depth, height, width, 27, channels)
    classes = {}
    for tap_d in range(3):
        for tap_h in range(3):
            for tap_w in range(3):
                term = spread[:, :, :, :, tap_d * 9 + tap_h * 3 + tap_w]
                pads = [(0, 0)]
                for tap in (tap_d, tap_h, tap_w):
                    pads.append((1, 0) if tap == 2 else (0, 1))
                pads.append((0, 0))
                term = jnp.pad(term, pads)
                key_name = (tap_d % 2, tap_h % 2, tap_w % 2)
                classes[key_name] = classes[key_name] + term if key_name in classes else term
    planes = []
    for parity_d in range(2):
        rows_h = []
        for parity_h in range(2):
            rows_h.append(weave(classes[parity_d, parity_h, 0], classes[parity_d, parity_h, 1], 3))
        planes.append(weave(rows_h[0], rows_h[1], 2))
    whole = weave(planes[0], planes[1], 1)
    return whole[:, : 2 * depth + 1, : 2 * height + 1, : 2 * width + 1, :]


def on_device(volume, kernel, cotangent):
    samples = volume.shape[0]
    depth = volume.shape[1] // 2
    height = volume.shape[2] // 2
    width = volume.shape[3] // 2
    n_sy = lax.axis_size("sy")
    n_af = lax.axis_size("af")
    kernel_part = gather_filters(kernel)
    kernel_full = lax.all_gather(kernel_part, "sx", axis=3, tiled=True)
    filters = kernel_full.shape[4]
    per_dev = filters // (n_sy * n_af)
    below = from_behind(volume[:, -1:], "sx", 1)
    extended = jnp.concatenate([below, volume], axis=1)
    beside = from_behind(extended[:, :, -1:], "sy", 1)
    extended = jnp.concatenate([beside, extended], axis=2)
    extended = jnp.pad(extended, ((0, 0), (0, 0), (0, 0), (1, 0), (0, 0)))
    rows = samples * depth * height * width
    classes = parity_view(extended)
    cols = im2col(classes, depth, height, width).reshape(rows, -1)
    kernel_mat = kernel_full.reshape(-1, filters)
    total = lax.dot_general(
        kernel_mat, cols, (((0,), (1,)), ((), ())), preferred_element_type=jnp.float32
    )
    n_sx = lax.axis_size("sx")
    conv_t = total.astype(jnp.bfloat16).reshape(n_sy, n_af, per_dev, depth, height, width)
    by_af = flat_all_to_all(conv_t.transpose(1, 0, 2, 3, 4, 5), "af")
    by_region = by_af.reshape(n_sx * n_sy, per_dev, depth, height, width)
    gathered = flat_all_to_all(by_region, ("sx", "sy"))
    own_samples = cotangent.shape[0]
    features = (
        gathered.reshape(n_sx, n_sy, per_dev, depth, height, width)
        .transpose(2, 0, 3, 1, 4, 5)
        .reshape(cotangent.shape)
    )
    grad_blocks = (
        cotangent.reshape(per_dev, n_sx, depth, n_sy, height, width)
        .transpose(1, 3, 0, 2, 4, 5)
        .reshape(n_sx * n_sy, per_dev, depth, height, width)
    )
    grad_region = flat_all_to_all(grad_blocks, ("sx", "sy"))
    grad_region = grad_region.reshape(n_sx * own_samples, n_sy, per_dev, depth, height, width)
    grad_back = flat_all_to_all(grad_region, "af")
    grad_t = grad_back.transpose(1, 0, 2, 3, 4, 5).reshape(filters, rows)
    by_parity = grad_t.reshape(n_sy * n_af // 2, 2, per_dev, rows).transpose(1, 0, 2, 3)
    kernel_terms = lax.dot_general(
        by_parity.reshape(filters, rows), cols, (((1,), (0,)), ((), ())),
        preferred_element_type=jnp.float32,
    )
    channels = kernel_full.shape[3]
    own_ch = channels // n_sx
    by_filter = reduce_filters(kernel_terms)
    by_filter = by_filter.reshape(per_dev, 27, n_sx, own_ch).transpose(2, 1, 3, 0)
    moved = lax.all_to_all(by_filter.reshape(n_sx, 1, -1), "sx", 0, 0, tiled=True)
    kernel_grad = moved.reshape(by_filter.shape).sum(axis=0)
    kernel_grad = kernel_grad.reshape(3, 3, 3, own_ch, per_dev)
    partial_grad = spread_back(grad_t, kernel_full, samples, depth, height, width)
    from_above = from_behind(partial_grad[:, 0:1], "sx", -1)
    own_depth = partial_grad[:, 1:]
    own_depth = jnp.concatenate([own_depth[:, :-1], own_depth[:, -1:] + from_above], axis=1)
    from_right = from_behind(own_depth[:, :, 0:1].astype(jnp.bfloat16), "sy", -1).astype(
        jnp.float32
    )
    own_height = own_depth[:, :, 1:]
    own_height = jnp.concatenate(
        [own_height[:, :, :-1], own_height[:, :, -1:] + from_right], axis=2
    )
    volume_grad = own_height[:, :, :, 1:]
    return (features, volume_grad.astype(jnp.bfloat16), kernel_grad)


def solution(mesh):
    return jax.shard_map(
        on_device,
        mesh=mesh,
        in_specs=(
            P("af", "sx", "sy", None, None),
            P(None, None, None, "sx", ("sy", "af")),
            P("sx", ("sy", "af"), None, None),
        ),
        out_specs=(
            P("sx", ("sy", "af"), None, None),
            P("af", "sx", "sy", None, None),
            P(None, None, None, "sx", ("sy", "af")),
        ),
        check_vma=False,
    )
```

```python
import functools

import jax
import jax.numpy as jnp
from jax import lax
from jax.experimental import pallas as pl
from jax.experimental.pallas import tpu as pltpu
from jax.sharding import PartitionSpec as P


def _gather_body(n_sy, n_af, block_ref, out_ref, send_sem, recv_sem):
    group = n_sy * n_af
    sx = lax.axis_index("sx")
    me = lax.axis_index("sy") * n_af + lax.axis_index("af")
    barrier = pltpu.get_barrier_semaphore()
    for step in range(1, group):
        peer = lax.rem(me + step, group)
        pl.semaphore_signal(
            barrier,
            inc=1,
            device_id=(sx, peer // n_af, lax.rem(peer, n_af)),
            device_id_type=pl.DeviceIdType.MESH,
        )
    pl.semaphore_wait(barrier, group - 1)
    copies = []
    for step in range(1, group):
        peer = lax.rem(me + step, group)
        copy = pltpu.make_async_remote_copy(
            src_ref=block_ref,
            dst_ref=out_ref.at[me],
            send_sem=send_sem.at[step - 1],
            recv_sem=recv_sem.at[step - 1],
            device_id=(sx, peer // n_af, lax.rem(peer, n_af)),
            device_id_type=pl.DeviceIdType.MESH,
        )
        copy.start()
        copies.append(copy)
    out_ref[me] = block_ref[...]
    for copy in copies:
        copy.wait_send()
    for step in range(1, group):
        source = lax.rem(me + group - step, group)
        incoming = pltpu.make_async_remote_copy(
            src_ref=block_ref,
            dst_ref=out_ref.at[source],
            send_sem=send_sem.at[step - 1],
            recv_sem=recv_sem.at[step - 1],
            device_id=(sx, source // n_af, lax.rem(source, n_af)),
            device_id_type=pl.DeviceIdType.MESH,
        )
        incoming.wait_recv()


def _reduce_body(n_sy, n_af, terms_ref, out_ref, from_sib, mine, held, sib_send, sib_recv, send_sem, recv_sem):
    half = n_sy * n_af // 2
    rows = out_ref.shape[0]
    span = half * rows
    sx = lax.axis_index("sx")
    sy = lax.axis_index("sy")
    af = lax.axis_index("af")
    parity = lax.rem(af, 2)
    sib_af = af + 1 - 2 * parity
    me = sy * (n_af // 2) + af // 2

    def peer_of(index):
        block = 2 * index + parity
        return (sx, block // n_af, lax.rem(block, n_af))

    barrier = pltpu.get_barrier_semaphore()
    pl.semaphore_signal(barrier, inc=1, device_id=(sx, sy, sib_af), device_id_type=pl.DeviceIdType.MESH)
    for step in range(1, half):
        pl.semaphore_signal(
            barrier,
            inc=1,
            device_id=peer_of(lax.rem(me + step, half)),
            device_id_type=pl.DeviceIdType.MESH,
        )
    pl.semaphore_wait(barrier, half)
    to_sib = pltpu.make_async_remote_copy(
        src_ref=terms_ref.at[pl.ds(pl.multiple_of((1 - parity) * span, span), span)],
        dst_ref=from_sib,
        send_sem=sib_send,
        recv_sem=sib_recv,
        device_id=(sx, sy, sib_af),
        device_id_type=pl.DeviceIdType.MESH,
    )
    to_sib.start()
    to_sib.wait_send()
    to_sib.wait_recv()
    mine[...] = terms_ref[pl.ds(pl.multiple_of(parity * span, span), span), :] + from_sib[...]
    copies = []
    for step in range(1, half):
        peer = lax.rem(me + step, half)
        copy = pltpu.make_async_remote_copy(
            src_ref=mine.at[pl.ds(pl.multiple_of(peer * rows, rows), rows)],
            dst_ref=held.at[me],
            send_sem=send_sem.at[step - 1],
            recv_sem=recv_sem.at[step - 1],
            device_id=peer_of(peer),
            device_id_type=pl.DeviceIdType.MESH,
        )
        copy.start()
        copies.append(copy)
    total = mine[pl.ds(pl.multiple_of(me * rows, rows), rows), :]
    for copy in copies:
        copy.wait_send()
    for step in range(1, half):
        source = lax.rem(me + half - step, half)
        incoming = pltpu.make_async_remote_copy(
            src_ref=mine.at[pl.ds(0, rows)],
            dst_ref=held.at[source],
            send_sem=send_sem.at[step - 1],
            recv_sem=recv_sem.at[step - 1],
            device_id=peer_of(source),
            device_id_type=pl.DeviceIdType.MESH,
        )
        incoming.wait_recv()
        total = total + held[source]
    out_ref[...] = total


def reduce_filters(terms):
    n_sy = lax.axis_size("sy")
    n_af = lax.axis_size("af")
    group = n_sy * n_af
    rows = terms.shape[0] // group
    return pl.pallas_call(
        functools.partial(_reduce_body, n_sy, n_af),
        out_shape=jax.ShapeDtypeStruct((rows, terms.shape[1]), terms.dtype),
        in_specs=[pl.BlockSpec(memory_space=pltpu.VMEM)],
        out_specs=pl.BlockSpec(memory_space=pltpu.VMEM),
        scratch_shapes=[
            pltpu.VMEM((group // 2 * rows, terms.shape[1]), terms.dtype),
            pltpu.VMEM((group // 2 * rows, terms.shape[1]), terms.dtype),
            pltpu.VMEM((group // 2, rows, terms.shape[1]), terms.dtype),
            pltpu.SemaphoreType.DMA(()),
            pltpu.SemaphoreType.DMA(()),
            pltpu.SemaphoreType.DMA((group // 2 - 1,)),
            pltpu.SemaphoreType.DMA((group // 2 - 1,)),
        ],
        compiler_params=pltpu.CompilerParams(collective_id=1, has_side_effects=True),
        cost_estimate=pl.CostEstimate(
            flops=terms.size, bytes_accessed=2 * terms.size * 4, transcendentals=0
        ),
    )(terms)


def gather_filters(kernel):
    n_sy = lax.axis_size("sy")
    n_af = lax.axis_size("af")
    group = n_sy * n_af
    taps, channels, per_dev = kernel.shape[0] * kernel.shape[1] * kernel.shape[2], kernel.shape[3], kernel.shape[4]
    block = kernel.reshape(-1, 128)
    gathered = pl.pallas_call(
        functools.partial(_gather_body, n_sy, n_af),
        out_shape=jax.ShapeDtypeStruct((group,) + block.shape, block.dtype),
        in_specs=[pl.BlockSpec(memory_space=pltpu.VMEM)],
        out_specs=pl.BlockSpec(memory_space=pltpu.VMEM),
        scratch_shapes=[
            pltpu.SemaphoreType.DMA((group - 1,)),
            pltpu.SemaphoreType.DMA((group - 1,)),
        ],
        compiler_params=pltpu.CompilerParams(collective_id=0, has_side_effects=True),
    )(block)
    gathered = gathered.reshape(group, taps, channels, per_dev).transpose(1, 2, 0, 3)
    return gathered.reshape(kernel.shape[:4] + (group * per_dev,))


def flat_all_to_all(x, axes):
    moved = lax.all_to_all(x.reshape(x.shape[0], 2, -1), axes, 0, 0, tiled=True)
    return moved.reshape(x.shape)


def from_behind(value, axis, steps):
    count = lax.axis_size(axis)
    leading, last = (max(0, -steps), min(count, count - steps))
    return lax.ppermute(value, axis, [(source, source + steps) for source in range(leading, last)])


def strided_patch(extended, tap_d, tap_h, tap_w, depth, height, width):
    return extended[
        :,
        tap_d : tap_d + 2 * depth : 2,
        tap_h : tap_h + 2 * height : 2,
        tap_w : tap_w + 2 * width : 2,
        :,
    ]


def parity_view(extended):
    samples, d_ext, h_ext, w_ext, channels = extended.shape
    pads = [(0, 0)] + [(0, n % 2) for n in (d_ext, h_ext, w_ext)] + [(0, 0)]
    even = jnp.pad(extended, pads)
    _, d2, h2, w2, _ = even.shape
    split = even.reshape(samples, d2 // 2, 2, h2 // 2, 2, w2 // 2, 2, channels)
    return split.transpose(2, 4, 6, 0, 1, 3, 5, 7)


def im2col(classes, depth, height, width):
    patches = []
    for tap_d in range(3):
        for tap_h in range(3):
            for tap_w in range(3):
                cls = classes[tap_d % 2, tap_h % 2, tap_w % 2]
                od, oh, ow = tap_d // 2, tap_h // 2, tap_w // 2
                patches.append(cls[:, od : od + depth, oh : oh + height, ow : ow + width, :])
    return jnp.concatenate(patches, axis=-1)


def weave(even_part, odd_part, axis):
    stacked = jnp.stack([even_part, odd_part], axis=axis + 1)
    shape = list(even_part.shape)
    shape[axis] = shape[axis] * 2
    return stacked.reshape(shape)


def spread_back(grad_t, kernel_full, samples, depth, height, width):
    filters = grad_t.shape[0]
    channels = kernel_full.shape[3]
    spread = lax.dot_general(
        grad_t,
        kernel_full.reshape(-1, channels, filters),
        (((0,), (2,)), ((), ())),
        preferred_element_type=jnp.float32,
    ).reshape(samples, depth, height, width, 27, channels)
    classes = {}
    for tap_d in range(3):
        for tap_h in range(3):
            for tap_w in range(3):
                term = spread[:, :, :, :, tap_d * 9 + tap_h * 3 + tap_w]
                pads = [(0, 0)]
                for tap in (tap_d, tap_h, tap_w):
                    pads.append((1, 0) if tap == 2 else (0, 1))
                pads.append((0, 0))
                term = jnp.pad(term, pads)
                key_name = (tap_d % 2, tap_h % 2, tap_w % 2)
                classes[key_name] = classes[key_name] + term if key_name in classes else term
    planes = []
    for parity_d in range(2):
        rows_h = []
        for parity_h in range(2):
            rows_h.append(weave(classes[parity_d, parity_h, 0], classes[parity_d, parity_h, 1], 3))
        planes.append(weave(rows_h[0], rows_h[1], 2))
    whole = weave(planes[0], planes[1], 1)
    return whole[:, : 2 * depth + 1, : 2 * height + 1, : 2 * width + 1, :]


def on_device(volume, kernel, cotangent):
    samples = volume.shape[0]
    depth = volume.shape[1] // 2
    height = volume.shape[2] // 2
    width = volume.shape[3] // 2
    n_sy = lax.axis_size("sy")
    n_af = lax.axis_size("af")
    kernel_part = gather_filters(kernel)
    kernel_full = lax.all_gather(kernel_part, "sx", axis=3, tiled=True)
    filters = kernel_full.shape[4]
    per_dev = filters // (n_sy * n_af)
    below = from_behind(volume[:, -1:], "sx", 1)
    n_sx_axis = lax.axis_size("sx")
    corner = lax.ppermute(
        volume[:, -1:, -1:],
        ("sx", "sy"),
        [
            (i * n_sy + j, (i + 1) * n_sy + j + 1)
            for i in range(n_sx_axis - 1)
            for j in range(n_sy - 1)
        ],
    )
    beside = jnp.concatenate([corner, from_behind(volume[:, :, -1:], "sy", 1)], axis=1)
    extended = jnp.concatenate([below, volume], axis=1)
    extended = jnp.concatenate([beside, extended], axis=2)
    extended = jnp.pad(extended, ((0, 0), (0, 0), (0, 0), (1, 0), (0, 0)))
    rows = samples * depth * height * width
    classes = parity_view(extended)
    cols = im2col(classes, depth, height, width).reshape(rows, -1)
    kernel_mat = kernel_full.reshape(-1, filters)
    total = lax.dot_general(
        kernel_mat, cols, (((0,), (1,)), ((), ())), preferred_element_type=jnp.float32
    )
    n_sx = lax.axis_size("sx")
    conv_t = total.astype(jnp.bfloat16).reshape(n_sy, n_af, per_dev, depth, height, width)
    by_af = flat_all_to_all(conv_t.transpose(1, 0, 2, 3, 4, 5), "af")
    by_region = by_af.reshape(n_sx * n_sy, per_dev, depth, height, width)
    gathered = flat_all_to_all(by_region, ("sx", "sy"))
    own_samples = cotangent.shape[0]
    features = (
        gathered.reshape(n_sx, n_sy, per_dev, depth, height, width)
        .transpose(2, 0, 3, 1, 4, 5)
        .reshape(cotangent.shape)
    )
    grad_blocks = (
        cotangent.reshape(per_dev, n_sx, depth, n_sy, height, width)
        .transpose(1, 3, 0, 2, 4, 5)
        .reshape(n_sx * n_sy, per_dev, depth, height, width)
    )
    grad_region = flat_all_to_all(grad_blocks, ("sx", "sy"))
    grad_region = grad_region.reshape(n_sx * own_samples, n_sy, per_dev, depth, height, width)
    grad_back = flat_all_to_all(grad_region, "af")
    grad_t = grad_back.transpose(1, 0, 2, 3, 4, 5).reshape(filters, rows)
    by_parity = grad_t.reshape(n_sy * n_af // 2, 2, per_dev, rows).transpose(1, 0, 2, 3)
    kernel_terms = lax.dot_general(
        by_parity.reshape(filters, rows), cols, (((1,), (0,)), ((), ())),
        preferred_element_type=jnp.float32,
    )
    channels = kernel_full.shape[3]
    own_ch = channels // n_sx
    by_filter = reduce_filters(kernel_terms)
    by_filter = by_filter.reshape(per_dev, 27, n_sx, own_ch).transpose(2, 1, 3, 0)
    kernel_grad = lax.all_to_all(by_filter, "sx", 0, 0, tiled=True).sum(axis=0)
    kernel_grad = kernel_grad.reshape(3, 3, 3, own_ch, per_dev)
    partial_grad = spread_back(grad_t, kernel_full, samples, depth, height, width)
    from_above = from_behind(partial_grad[:, 0:1], "sx", -1)
    own_depth = partial_grad[:, 1:]
    own_depth = jnp.concatenate([own_depth[:, :-1], own_depth[:, -1:] + from_above], axis=1)
    from_right = from_behind(own_depth[:, :, 0:1].astype(jnp.bfloat16), "sy", -1).astype(
        jnp.float32
    )
    own_height = own_depth[:, :, 1:]
    own_height = jnp.concatenate(
        [own_height[:, :, :-1], own_height[:, :, -1:] + from_right], axis=2
    )
    volume_grad = own_height[:, :, :, 1:]
    return (features, volume_grad.astype(jnp.bfloat16), kernel_grad)


def solution(mesh):
    return jax.shard_map(
        on_device,
        mesh=mesh,
        in_specs=(
            P("af", "sx", "sy", None, None),
            P(None, None, None, "sx", ("sy", "af")),
            P("sx", ("sy", "af"), None, None),
        ),
        out_specs=(
            P("sx", ("sy", "af"), None, None),
            P("af", "sx", "sy", None, None),
            P(None, None, None, "sx", ("sy", "af")),
        ),
        check_vma=False,
    )
```

```python
import functools

import jax
import jax.numpy as jnp
from jax import lax
from jax.experimental import pallas as pl
from jax.experimental.pallas import tpu as pltpu
from jax.sharding import PartitionSpec as P


def _gather_body(n_sy, n_af, block_ref, out_ref, send_sem, recv_sem):
    group = n_sy * n_af
    sx = lax.axis_index("sx")
    me = lax.axis_index("sy") * n_af + lax.axis_index("af")
    barrier = pltpu.get_barrier_semaphore()
    for step in range(1, group):
        peer = lax.rem(me + step, group)
        pl.semaphore_signal(
            barrier,
            inc=1,
            device_id=(sx, peer // n_af, lax.rem(peer, n_af)),
            device_id_type=pl.DeviceIdType.MESH,
        )
    pl.semaphore_wait(barrier, group - 1)
    copies = []
    for step in range(1, group):
        peer = lax.rem(me + step, group)
        copy = pltpu.make_async_remote_copy(
            src_ref=block_ref,
            dst_ref=out_ref.at[me],
            send_sem=send_sem.at[step - 1],
            recv_sem=recv_sem.at[step - 1],
            device_id=(sx, peer // n_af, lax.rem(peer, n_af)),
            device_id_type=pl.DeviceIdType.MESH,
        )
        copy.start()
        copies.append(copy)
    out_ref[me] = block_ref[...]
    for copy in copies:
        copy.wait_send()
    for step in range(1, group):
        source = lax.rem(me + group - step, group)
        incoming = pltpu.make_async_remote_copy(
            src_ref=block_ref,
            dst_ref=out_ref.at[source],
            send_sem=send_sem.at[step - 1],
            recv_sem=recv_sem.at[step - 1],
            device_id=(sx, source // n_af, lax.rem(source, n_af)),
            device_id_type=pl.DeviceIdType.MESH,
        )
        incoming.wait_recv()


def _reduce_body(n_sy, n_af, terms_ref, out_ref, from_sib, mine, held, sib_send, sib_recv, send_sem, recv_sem):
    half = n_sy * n_af // 2
    rows = out_ref.shape[0]
    span = half * rows
    sx = lax.axis_index("sx")
    sy = lax.axis_index("sy")
    af = lax.axis_index("af")
    parity = lax.rem(af, 2)
    sib_af = af + 1 - 2 * parity
    me = sy * (n_af // 2) + af // 2

    def peer_of(index):
        block = 2 * index + parity
        return (sx, block // n_af, lax.rem(block, n_af))

    barrier = pltpu.get_barrier_semaphore()
    pl.semaphore_signal(barrier, inc=1, device_id=(sx, sy, sib_af), device_id_type=pl.DeviceIdType.MESH)
    for step in range(1, half):
        pl.semaphore_signal(
            barrier,
            inc=1,
            device_id=peer_of(lax.rem(me + step, half)),
            device_id_type=pl.DeviceIdType.MESH,
        )
    pl.semaphore_wait(barrier, half)
    to_sib = pltpu.make_async_remote_copy(
        src_ref=terms_ref.at[pl.ds(pl.multiple_of((1 - parity) * span, span), span)],
        dst_ref=from_sib,
        send_sem=sib_send,
        recv_sem=sib_recv,
        device_id=(sx, sy, sib_af),
        device_id_type=pl.DeviceIdType.MESH,
    )
    to_sib.start()
    to_sib.wait_send()
    to_sib.wait_recv()
    mine[...] = terms_ref[pl.ds(pl.multiple_of(parity * span, span), span), :] + from_sib[...]
    copies = []
    for step in range(1, half):
        peer = lax.rem(me + step, half)
        copy = pltpu.make_async_remote_copy(
            src_ref=mine.at[pl.ds(pl.multiple_of(peer * rows, rows), rows)],
            dst_ref=held.at[me],
            send_sem=send_sem.at[step - 1],
            recv_sem=recv_sem.at[step - 1],
            device_id=peer_of(peer),
            device_id_type=pl.DeviceIdType.MESH,
        )
        copy.start()
        copies.append(copy)
    total = mine[pl.ds(pl.multiple_of(me * rows, rows), rows), :]
    for copy in copies:
        copy.wait_send()
    for step in range(1, half):
        source = lax.rem(me + half - step, half)
        incoming = pltpu.make_async_remote_copy(
            src_ref=mine.at[pl.ds(0, rows)],
            dst_ref=held.at[source],
            send_sem=send_sem.at[step - 1],
            recv_sem=recv_sem.at[step - 1],
            device_id=peer_of(source),
            device_id_type=pl.DeviceIdType.MESH,
        )
        incoming.wait_recv()
        total = total + held[source]
    out_ref[...] = total


def reduce_filters(terms):
    n_sy = lax.axis_size("sy")
    n_af = lax.axis_size("af")
    group = n_sy * n_af
    rows = terms.shape[0] // group
    return pl.pallas_call(
        functools.partial(_reduce_body, n_sy, n_af),
        out_shape=jax.ShapeDtypeStruct((rows, terms.shape[1]), terms.dtype),
        in_specs=[pl.BlockSpec(memory_space=pltpu.VMEM)],
        out_specs=pl.BlockSpec(memory_space=pltpu.VMEM),
        scratch_shapes=[
            pltpu.VMEM((group // 2 * rows, terms.shape[1]), terms.dtype),
            pltpu.VMEM((group // 2 * rows, terms.shape[1]), terms.dtype),
            pltpu.VMEM((group // 2, rows, terms.shape[1]), terms.dtype),
            pltpu.SemaphoreType.DMA(()),
            pltpu.SemaphoreType.DMA(()),
            pltpu.SemaphoreType.DMA((group // 2 - 1,)),
            pltpu.SemaphoreType.DMA((group // 2 - 1,)),
        ],
        compiler_params=pltpu.CompilerParams(collective_id=1, has_side_effects=True),
        cost_estimate=pl.CostEstimate(
            flops=terms.size, bytes_accessed=2 * terms.size * 4, transcendentals=0
        ),
    )(terms)


def gather_filters(kernel):
    n_sy = lax.axis_size("sy")
    n_af = lax.axis_size("af")
    group = n_sy * n_af
    taps, channels, per_dev = kernel.shape[0] * kernel.shape[1] * kernel.shape[2], kernel.shape[3], kernel.shape[4]
    block = kernel.reshape(-1, 128)
    gathered = pl.pallas_call(
        functools.partial(_gather_body, n_sy, n_af),
        out_shape=jax.ShapeDtypeStruct((group,) + block.shape, block.dtype),
        in_specs=[pl.BlockSpec(memory_space=pltpu.VMEM)],
        out_specs=pl.BlockSpec(memory_space=pltpu.VMEM),
        scratch_shapes=[
            pltpu.SemaphoreType.DMA((group - 1,)),
            pltpu.SemaphoreType.DMA((group - 1,)),
        ],
        compiler_params=pltpu.CompilerParams(collective_id=0, has_side_effects=True),
    )(block)
    gathered = gathered.reshape(group, taps, channels, per_dev).transpose(1, 2, 0, 3)
    return gathered.reshape(kernel.shape[:4] + (group * per_dev,))


def flat_all_to_all(x, axes):
    moved = lax.all_to_all(x.reshape(x.shape[0], 2, -1), axes, 0, 0, tiled=True)
    return moved.reshape(x.shape)


def from_behind(value, axis, steps):
    count = lax.axis_size(axis)
    leading, last = (max(0, -steps), min(count, count - steps))
    return lax.ppermute(value, axis, [(source, source + steps) for source in range(leading, last)])


def strided_patch(extended, tap_d, tap_h, tap_w, depth, height, width):
    return extended[
        :,
        tap_d : tap_d + 2 * depth : 2,
        tap_h : tap_h + 2 * height : 2,
        tap_w : tap_w + 2 * width : 2,
        :,
    ]


def parity_view(extended):
    samples, d_ext, h_ext, w_ext, channels = extended.shape
    pads = [(0, 0)] + [(0, n % 2) for n in (d_ext, h_ext, w_ext)] + [(0, 0)]
    even = jnp.pad(extended, pads)
    _, d2, h2, w2, _ = even.shape
    split = even.reshape(samples, d2 // 2, 2, h2 // 2, 2, w2 // 2, 2, channels)
    return split.transpose(2, 4, 6, 0, 1, 3, 5, 7)


def im2col(classes, depth, height, width):
    patches = []
    for tap_d in range(3):
        for tap_h in range(3):
            for tap_w in range(3):
                cls = classes[tap_d % 2, tap_h % 2, tap_w % 2]
                od, oh, ow = tap_d // 2, tap_h // 2, tap_w // 2
                patches.append(cls[:, od : od + depth, oh : oh + height, ow : ow + width, :])
    return jnp.concatenate(patches, axis=-1)


def weave(even_part, odd_part, axis):
    stacked = jnp.stack([even_part, odd_part], axis=axis + 1)
    shape = list(even_part.shape)
    shape[axis] = shape[axis] * 2
    return stacked.reshape(shape)


def spread_back(grad_t, kernel_full, samples, depth, height, width):
    filters = grad_t.shape[0]
    channels = kernel_full.shape[3]
    spread = lax.dot_general(
        grad_t,
        kernel_full.reshape(-1, channels, filters),
        (((0,), (2,)), ((), ())),
        preferred_element_type=jnp.float32,
    ).reshape(samples, depth, height, width, 27, channels)
    classes = {}
    for tap_d in range(3):
        for tap_h in range(3):
            for tap_w in range(3):
                term = spread[:, :, :, :, tap_d * 9 + tap_h * 3 + tap_w]
                pads = [(0, 0)]
                for tap in (tap_d, tap_h, tap_w):
                    pads.append((1, 0) if tap == 2 else (0, 1))
                pads.append((0, 0))
                term = jnp.pad(term, pads)
                key_name = (tap_d % 2, tap_h % 2, tap_w % 2)
                classes[key_name] = classes[key_name] + term if key_name in classes else term
    planes = []
    for parity_d in range(2):
        rows_h = []
        for parity_h in range(2):
            rows_h.append(weave(classes[parity_d, parity_h, 0], classes[parity_d, parity_h, 1], 3))
        planes.append(weave(rows_h[0], rows_h[1], 2))
    whole = weave(planes[0], planes[1], 1)
    return whole[:, : 2 * depth + 1, : 2 * height + 1, : 2 * width + 1, :]


def on_device(volume, kernel, cotangent):
    samples = volume.shape[0]
    depth = volume.shape[1] // 2
    height = volume.shape[2] // 2
    width = volume.shape[3] // 2
    n_sy = lax.axis_size("sy")
    n_af = lax.axis_size("af")
    kernel_part = gather_filters(kernel)
    kernel_full = lax.all_gather(kernel_part, "sx", axis=3, tiled=True)
    filters = kernel_full.shape[4]
    per_dev = filters // (n_sy * n_af)
    below = from_behind(volume[:, -1:], "sx", 1)
    n_sx_axis = lax.axis_size("sx")
    corner = lax.ppermute(
        volume[:, -1:, -1:],
        ("sx", "sy"),
        [
            (i * n_sy + j, (i + 1) * n_sy + j + 1)
            for i in range(n_sx_axis - 1)
            for j in range(n_sy - 1)
        ],
    )
    beside = jnp.concatenate([corner, from_behind(volume[:, :, -1:], "sy", 1)], axis=1)
    extended = jnp.concatenate([below, volume], axis=1)
    extended = jnp.concatenate([beside, extended], axis=2)
    extended = jnp.pad(extended, ((0, 0), (0, 0), (0, 0), (1, 0), (0, 0)))
    rows = samples * depth * height * width
    classes = parity_view(extended)
    cols = im2col(classes, depth, height, width).reshape(rows, -1)
    kernel_mat = kernel_full.reshape(-1, filters)
    total = lax.dot_general(
        kernel_mat, cols, (((0,), (1,)), ((), ())), preferred_element_type=jnp.float32
    )
    n_sx = lax.axis_size("sx")
    conv_t = total.astype(jnp.bfloat16).reshape(n_sy, n_af, per_dev, depth, height, width)
    by_af = flat_all_to_all(conv_t.transpose(1, 0, 2, 3, 4, 5), "af")
    by_region = by_af.reshape(n_sx * n_sy, per_dev, depth, height, width)
    gathered = flat_all_to_all(by_region, ("sx", "sy"))
    own_samples = cotangent.shape[0]
    features = (
        gathered.reshape(n_sx, n_sy, per_dev, depth, height, width)
        .transpose(2, 0, 3, 1, 4, 5)
        .reshape(cotangent.shape)
    )
    grad_blocks = (
        cotangent.reshape(per_dev, n_sx, depth, n_sy, height, width)
        .transpose(1, 3, 0, 2, 4, 5)
        .reshape(n_sx * n_sy, per_dev, depth, height, width)
    )
    grad_region = flat_all_to_all(grad_blocks, ("sx", "sy"))
    grad_region = grad_region.reshape(n_sx * own_samples, n_sy, per_dev, depth, height, width)
    grad_back = flat_all_to_all(grad_region, "af")
    grad_t = grad_back.transpose(1, 0, 2, 3, 4, 5).reshape(filters, rows)
    by_parity = grad_t.reshape(n_sy * n_af // 2, 2, per_dev, rows).transpose(1, 0, 2, 3)
    kernel_terms = lax.dot_general(
        by_parity.reshape(filters, rows), cols, (((1,), (0,)), ((), ())),
        preferred_element_type=jnp.float32,
    )
    channels = kernel_full.shape[3]
    own_ch = channels // n_sx
    by_filter = reduce_filters(kernel_terms)
    by_filter = by_filter.reshape(per_dev, 27, n_sx, own_ch).transpose(2, 1, 3, 0)
    kernel_grad = lax.all_to_all(by_filter, "sx", 0, 0, tiled=True).sum(axis=0)
    kernel_grad = kernel_grad.reshape(3, 3, 3, own_ch, per_dev)
    partial_grad = spread_back(grad_t, kernel_full, samples, depth, height, width)
    from_above = from_behind(partial_grad[:, 0:1, 1:], "sx", -1)
    corner = lax.ppermute(
        partial_grad[:, 0:1, 0:1],
        ("sx", "sy"),
        [
            ((i + 1) * n_sy + j + 1, i * n_sy + j)
            for i in range(n_sx_axis - 1)
            for j in range(n_sy - 1)
        ],
    )
    from_right = from_behind(partial_grad[:, 1:, 0:1].astype(jnp.bfloat16), "sy", -1).astype(
        jnp.float32
    )
    from_right = jnp.concatenate([from_right[:, :-1], from_right[:, -1:] + corner], axis=1)
    own_height = partial_grad[:, 1:, 1:]
    own_height = jnp.concatenate([own_height[:, :-1], own_height[:, -1:] + from_above], axis=1)
    own_height = jnp.concatenate(
        [own_height[:, :, :-1], own_height[:, :, -1:] + from_right], axis=2
    )
    volume_grad = own_height[:, :, :, 1:]
    return (features, volume_grad.astype(jnp.bfloat16), kernel_grad)


def solution(mesh):
    return jax.shard_map(
        on_device,
        mesh=mesh,
        in_specs=(
            P("af", "sx", "sy", None, None),
            P(None, None, None, "sx", ("sy", "af")),
            P("sx", ("sy", "af"), None, None),
        ),
        out_specs=(
            P("sx", ("sy", "af"), None, None),
            P("af", "sx", "sy", None, None),
            P(None, None, None, "sx", ("sy", "af")),
        ),
        check_vma=False,
    )
```

```python
import functools

import jax
import jax.numpy as jnp
from jax import lax
from jax.experimental import pallas as pl
from jax.experimental.pallas import tpu as pltpu
from jax.sharding import PartitionSpec as P


def _gather_body(n_sy, n_af, block_ref, out_ref, send_sem, recv_sem):
    group = n_sy * n_af
    sx = lax.axis_index("sx")
    me = lax.axis_index("sy") * n_af + lax.axis_index("af")
    barrier = pltpu.get_barrier_semaphore()
    for step in range(1, group):
        peer = lax.rem(me + step, group)
        pl.semaphore_signal(
            barrier,
            inc=1,
            device_id=(sx, peer // n_af, lax.rem(peer, n_af)),
            device_id_type=pl.DeviceIdType.MESH,
        )
    pl.semaphore_wait(barrier, group - 1)
    copies = []
    for step in range(1, group):
        peer = lax.rem(me + step, group)
        copy = pltpu.make_async_remote_copy(
            src_ref=block_ref,
            dst_ref=out_ref.at[me],
            send_sem=send_sem.at[step - 1],
            recv_sem=recv_sem.at[step - 1],
            device_id=(sx, peer // n_af, lax.rem(peer, n_af)),
            device_id_type=pl.DeviceIdType.MESH,
        )
        copy.start()
        copies.append(copy)
    out_ref[me] = block_ref[...]
    for copy in copies:
        copy.wait_send()
    for step in range(1, group):
        source = lax.rem(me + group - step, group)
        incoming = pltpu.make_async_remote_copy(
            src_ref=block_ref,
            dst_ref=out_ref.at[source],
            send_sem=send_sem.at[step - 1],
            recv_sem=recv_sem.at[step - 1],
            device_id=(sx, source // n_af, lax.rem(source, n_af)),
            device_id_type=pl.DeviceIdType.MESH,
        )
        incoming.wait_recv()


def _reduce_body(n_sy, n_af, terms_ref, out_ref, from_sib, mine, held, sib_send, sib_recv, send_sem, recv_sem):
    half = n_sy * n_af // 2
    rows = out_ref.shape[0]
    span = half * rows
    sx = lax.axis_index("sx")
    sy = lax.axis_index("sy")
    af = lax.axis_index("af")
    parity = lax.rem(af, 2)
    sib_af = af + 1 - 2 * parity
    me = sy * (n_af // 2) + af // 2

    def peer_of(index):
        block = 2 * index + parity
        return (sx, block // n_af, lax.rem(block, n_af))

    barrier = pltpu.get_barrier_semaphore()
    pl.semaphore_signal(barrier, inc=1, device_id=(sx, sy, sib_af), device_id_type=pl.DeviceIdType.MESH)
    for step in range(1, half):
        pl.semaphore_signal(
            barrier,
            inc=1,
            device_id=peer_of(lax.rem(me + step, half)),
            device_id_type=pl.DeviceIdType.MESH,
        )
    pl.semaphore_wait(barrier, half)
    to_sib = pltpu.make_async_remote_copy(
        src_ref=terms_ref.at[pl.ds(pl.multiple_of((1 - parity) * span, span), span)],
        dst_ref=from_sib,
        send_sem=sib_send,
        recv_sem=sib_recv,
        device_id=(sx, sy, sib_af),
        device_id_type=pl.DeviceIdType.MESH,
    )
    to_sib.start()
    to_sib.wait_send()
    to_sib.wait_recv()
    mine[...] = terms_ref[pl.ds(pl.multiple_of(parity * span, span), span), :] + from_sib[...]
    copies = []
    for step in range(1, half):
        peer = lax.rem(me + step, half)
        copy = pltpu.make_async_remote_copy(
            src_ref=mine.at[pl.ds(pl.multiple_of(peer * rows, rows), rows)],
            dst_ref=held.at[me],
            send_sem=send_sem.at[step - 1],
            recv_sem=recv_sem.at[step - 1],
            device_id=peer_of(peer),
            device_id_type=pl.DeviceIdType.MESH,
        )
        copy.start()
        copies.append(copy)
    total = mine[pl.ds(pl.multiple_of(me * rows, rows), rows), :]
    for copy in copies:
        copy.wait_send()
    for step in range(1, half):
        source = lax.rem(me + half - step, half)
        incoming = pltpu.make_async_remote_copy(
            src_ref=mine.at[pl.ds(0, rows)],
            dst_ref=held.at[source],
            send_sem=send_sem.at[step - 1],
            recv_sem=recv_sem.at[step - 1],
            device_id=peer_of(source),
            device_id_type=pl.DeviceIdType.MESH,
        )
        incoming.wait_recv()
        total = total + held[source]
    out_ref[...] = total


def reduce_filters(terms):
    n_sy = lax.axis_size("sy")
    n_af = lax.axis_size("af")
    group = n_sy * n_af
    rows = terms.shape[0] // group
    return pl.pallas_call(
        functools.partial(_reduce_body, n_sy, n_af),
        out_shape=jax.ShapeDtypeStruct((rows, terms.shape[1]), terms.dtype),
        in_specs=[pl.BlockSpec(memory_space=pltpu.VMEM)],
        out_specs=pl.BlockSpec(memory_space=pltpu.VMEM),
        scratch_shapes=[
            pltpu.VMEM((group // 2 * rows, terms.shape[1]), terms.dtype),
            pltpu.VMEM((group // 2 * rows, terms.shape[1]), terms.dtype),
            pltpu.VMEM((group // 2, rows, terms.shape[1]), terms.dtype),
            pltpu.SemaphoreType.DMA(()),
            pltpu.SemaphoreType.DMA(()),
            pltpu.SemaphoreType.DMA((group // 2 - 1,)),
            pltpu.SemaphoreType.DMA((group // 2 - 1,)),
        ],
        compiler_params=pltpu.CompilerParams(collective_id=1, has_side_effects=True),
        cost_estimate=pl.CostEstimate(
            flops=terms.size, bytes_accessed=2 * terms.size * 4, transcendentals=0
        ),
    )(terms)


def gather_filters(kernel):
    n_sy = lax.axis_size("sy")
    n_af = lax.axis_size("af")
    group = n_sy * n_af
    taps, channels, per_dev = kernel.shape[0] * kernel.shape[1] * kernel.shape[2], kernel.shape[3], kernel.shape[4]
    block = kernel.reshape(-1, 128)
    gathered = pl.pallas_call(
        functools.partial(_gather_body, n_sy, n_af),
        out_shape=jax.ShapeDtypeStruct((group,) + block.shape, block.dtype),
        in_specs=[pl.BlockSpec(memory_space=pltpu.VMEM)],
        out_specs=pl.BlockSpec(memory_space=pltpu.VMEM),
        scratch_shapes=[
            pltpu.SemaphoreType.DMA((group - 1,)),
            pltpu.SemaphoreType.DMA((group - 1,)),
        ],
        compiler_params=pltpu.CompilerParams(collective_id=0, has_side_effects=True),
    )(block)
    gathered = gathered.reshape(group, taps, channels, per_dev).transpose(1, 2, 0, 3)
    return gathered.reshape(kernel.shape[:4] + (group * per_dev,))


def flat_all_to_all(x, axes):
    moved = lax.all_to_all(x.reshape(x.shape[0], 2, -1), axes, 0, 0, tiled=True)
    return moved.reshape(x.shape)


def from_behind(value, axis, steps):
    count = lax.axis_size(axis)
    leading, last = (max(0, -steps), min(count, count - steps))
    return lax.ppermute(value, axis, [(source, source + steps) for source in range(leading, last)])


def strided_patch(extended, tap_d, tap_h, tap_w, depth, height, width):
    return extended[
        :,
        tap_d : tap_d + 2 * depth : 2,
        tap_h : tap_h + 2 * height : 2,
        tap_w : tap_w + 2 * width : 2,
        :,
    ]


def parity_view(extended):
    samples, d_ext, h_ext, w_ext, channels = extended.shape
    pads = [(0, 0)] + [(0, n % 2) for n in (d_ext, h_ext, w_ext)] + [(0, 0)]
    even = jnp.pad(extended, pads)
    _, d2, h2, w2, _ = even.shape
    split = even.reshape(samples, d2 // 2, 2, h2 // 2, 2, w2 // 2, 2, channels)
    return split.transpose(2, 4, 6, 0, 1, 3, 5, 7)


def im2col(classes, depth, height, width):
    patches = []
    for tap_d in range(3):
        for tap_h in range(3):
            for tap_w in range(3):
                cls = classes[tap_d % 2, tap_h % 2, tap_w % 2]
                od, oh, ow = tap_d // 2, tap_h // 2, tap_w // 2
                patch = cls[:, od : od + depth, oh : oh + height, ow : ow + width, :]
                patches.append(patch.reshape(-1, patch.shape[-1]))
    return jnp.concatenate(patches, axis=-1)


def weave(even_part, odd_part, axis):
    stacked = jnp.stack([even_part, odd_part], axis=axis + 1)
    shape = list(even_part.shape)
    shape[axis] = shape[axis] * 2
    return stacked.reshape(shape)


def spread_back(grad_t, kernel_full, samples, depth, height, width):
    filters = grad_t.shape[0]
    channels = kernel_full.shape[3]
    spread = lax.dot_general(
        grad_t,
        kernel_full.reshape(-1, channels, filters),
        (((0,), (2,)), ((), ())),
        preferred_element_type=jnp.float32,
    ).reshape(samples, depth, height, width, 27, channels)
    classes = {}
    for tap_d in range(3):
        for tap_h in range(3):
            for tap_w in range(3):
                term = spread[:, :, :, :, tap_d * 9 + tap_h * 3 + tap_w]
                pads = [(0, 0)]
                for tap in (tap_d, tap_h, tap_w):
                    pads.append((1, 0) if tap == 2 else (0, 1))
                pads.append((0, 0))
                term = jnp.pad(term, pads)
                key_name = (tap_d % 2, tap_h % 2, tap_w % 2)
                classes[key_name] = classes[key_name] + term if key_name in classes else term
    planes = []
    for parity_d in range(2):
        rows_h = []
        for parity_h in range(2):
            rows_h.append(weave(classes[parity_d, parity_h, 0], classes[parity_d, parity_h, 1], 3))
        planes.append(weave(rows_h[0], rows_h[1], 2))
    whole = weave(planes[0], planes[1], 1)
    return whole[:, : 2 * depth + 1, : 2 * height + 1, : 2 * width + 1, :]


def on_device(volume, kernel, cotangent):
    samples = volume.shape[0]
    depth = volume.shape[1] // 2
    height = volume.shape[2] // 2
    width = volume.shape[3] // 2
    n_sy = lax.axis_size("sy")
    n_af = lax.axis_size("af")
    kernel_part = gather_filters(kernel)
    kernel_full = lax.all_gather(kernel_part, "sx", axis=3, tiled=True)
    filters = kernel_full.shape[4]
    per_dev = filters // (n_sy * n_af)
    below = from_behind(volume[:, -1:], "sx", 1)
    n_sx_axis = lax.axis_size("sx")
    corner = lax.ppermute(
        volume[:, -1:, -1:],
        ("sx", "sy"),
        [
            (i * n_sy + j, (i + 1) * n_sy + j + 1)
            for i in range(n_sx_axis - 1)
            for j in range(n_sy - 1)
        ],
    )
    beside = jnp.concatenate([corner, from_behind(volume[:, :, -1:], "sy", 1)], axis=1)
    extended = jnp.concatenate([below, volume], axis=1)
    extended = jnp.concatenate([beside, extended], axis=2)
    extended = jnp.pad(extended, ((0, 0), (0, 0), (0, 0), (1, 0), (0, 0)))
    rows = samples * depth * height * width
    classes = parity_view(extended)
    cols = im2col(classes, depth, height, width).reshape(rows, -1)
    kernel_mat = kernel_full.reshape(-1, filters)
    total = lax.dot_general(
        kernel_mat, cols, (((0,), (1,)), ((), ())), preferred_element_type=jnp.float32
    )
    n_sx = lax.axis_size("sx")
    conv_t = total.astype(jnp.bfloat16).reshape(n_sy, n_af, per_dev, depth, height, width)
    by_af = flat_all_to_all(conv_t.transpose(1, 0, 2, 3, 4, 5), "af")
    by_region = by_af.reshape(n_sx * n_sy, per_dev, depth, height, width)
    gathered = flat_all_to_all(by_region, ("sx", "sy"))
    own_samples = cotangent.shape[0]
    features = (
        gathered.reshape(n_sx, n_sy, per_dev, depth, height, width)
        .transpose(2, 0, 3, 1, 4, 5)
        .reshape(cotangent.shape)
    )
    grad_blocks = (
        cotangent.reshape(per_dev, n_sx, depth, n_sy, height, width)
        .transpose(1, 3, 0, 2, 4, 5)
        .reshape(n_sx * n_sy, per_dev, depth, height, width)
    )
    grad_region = flat_all_to_all(grad_blocks, ("sx", "sy"))
    grad_region = grad_region.reshape(n_sx * own_samples, n_sy, per_dev, depth, height, width)
    grad_back = flat_all_to_all(grad_region, "af")
    grad_t = grad_back.transpose(1, 0, 2, 3, 4, 5).reshape(filters, rows)
    by_parity = grad_t.reshape(n_sy * n_af // 2, 2, per_dev, rows).transpose(1, 0, 2, 3)
    kernel_terms = lax.dot_general(
        by_parity.reshape(filters, rows), cols, (((1,), (0,)), ((), ())),
        preferred_element_type=jnp.float32,
    )
    channels = kernel_full.shape[3]
    own_ch = channels // n_sx
    by_filter = reduce_filters(kernel_terms)
    by_filter = by_filter.reshape(per_dev, 27, n_sx, own_ch).transpose(2, 1, 3, 0)
    kernel_grad = lax.all_to_all(by_filter, "sx", 0, 0, tiled=True).sum(axis=0)
    kernel_grad = kernel_grad.reshape(3, 3, 3, own_ch, per_dev)
    partial_grad = spread_back(grad_t, kernel_full, samples, depth, height, width)
    from_above = from_behind(partial_grad[:, 0:1], "sx", -1)
    own_depth = partial_grad[:, 1:]
    own_depth = jnp.concatenate([own_depth[:, :-1], own_depth[:, -1:] + from_above], axis=1)
    from_right = from_behind(own_depth[:, :, 0:1].astype(jnp.bfloat16), "sy", -1).astype(
        jnp.float32
    )
    own_height = own_depth[:, :, 1:]
    own_height = jnp.concatenate(
        [own_height[:, :, :-1], own_height[:, :, -1:] + from_right], axis=2
    )
    volume_grad = own_height[:, :, :, 1:]
    return (features, volume_grad.astype(jnp.bfloat16), kernel_grad)


def solution(mesh):
    return jax.shard_map(
        on_device,
        mesh=mesh,
        in_specs=(
            P("af", "sx", "sy", None, None),
            P(None, None, None, "sx", ("sy", "af")),
            P("sx", ("sy", "af"), None, None),
        ),
        out_specs=(
            P("sx", ("sy", "af"), None, None),
            P("af", "sx", "sy", None, None),
            P(None, None, None, "sx", ("sy", "af")),
        ),
        check_vma=False,
    )
```

```python
import functools

import jax
import jax.numpy as jnp
from jax import lax
from jax.experimental import pallas as pl
from jax.experimental.pallas import tpu as pltpu
from jax.sharding import PartitionSpec as P


def _gather_body(n_sy, n_af, block_ref, out_ref, send_sem, recv_sem):
    group = n_sy * n_af
    sx = lax.axis_index("sx")
    me = lax.axis_index("sy") * n_af + lax.axis_index("af")
    barrier = pltpu.get_barrier_semaphore()
    for step in range(1, group):
        peer = lax.rem(me + step, group)
        pl.semaphore_signal(
            barrier,
            inc=1,
            device_id=(sx, peer // n_af, lax.rem(peer, n_af)),
            device_id_type=pl.DeviceIdType.MESH,
        )
    pl.semaphore_wait(barrier, group - 1)
    copies = []
    for step in range(1, group):
        peer = lax.rem(me + step, group)
        copy = pltpu.make_async_remote_copy(
            src_ref=block_ref,
            dst_ref=out_ref.at[me],
            send_sem=send_sem.at[step - 1],
            recv_sem=recv_sem.at[step - 1],
            device_id=(sx, peer // n_af, lax.rem(peer, n_af)),
            device_id_type=pl.DeviceIdType.MESH,
        )
        copy.start()
        copies.append(copy)
    out_ref[me] = block_ref[...]
    for copy in copies:
        copy.wait_send()
    for step in range(1, group):
        source = lax.rem(me + group - step, group)
        incoming = pltpu.make_async_remote_copy(
            src_ref=block_ref,
            dst_ref=out_ref.at[source],
            send_sem=send_sem.at[step - 1],
            recv_sem=recv_sem.at[step - 1],
            device_id=(sx, source // n_af, lax.rem(source, n_af)),
            device_id_type=pl.DeviceIdType.MESH,
        )
        incoming.wait_recv()


def _reduce_body(n_sy, n_af, terms_ref, out_ref, from_sib, mine, held, sib_send, sib_recv, send_sem, recv_sem):
    half = n_sy * n_af // 2
    rows = out_ref.shape[0]
    span = half * rows
    sx = lax.axis_index("sx")
    sy = lax.axis_index("sy")
    af = lax.axis_index("af")
    parity = lax.rem(af, 2)
    sib_af = af + 1 - 2 * parity
    me = sy * (n_af // 2) + af // 2

    def peer_of(index):
        block = 2 * index + parity
        return (sx, block // n_af, lax.rem(block, n_af))

    barrier = pltpu.get_barrier_semaphore()
    pl.semaphore_signal(barrier, inc=1, device_id=(sx, sy, sib_af), device_id_type=pl.DeviceIdType.MESH)
    for step in range(1, half):
        pl.semaphore_signal(
            barrier,
            inc=1,
            device_id=peer_of(lax.rem(me + step, half)),
            device_id_type=pl.DeviceIdType.MESH,
        )
    pl.semaphore_wait(barrier, half)
    to_sib = pltpu.make_async_remote_copy(
        src_ref=terms_ref.at[pl.ds(pl.multiple_of((1 - parity) * span, span), span)],
        dst_ref=from_sib,
        send_sem=sib_send,
        recv_sem=sib_recv,
        device_id=(sx, sy, sib_af),
        device_id_type=pl.DeviceIdType.MESH,
    )
    to_sib.start()
    to_sib.wait_send()
    to_sib.wait_recv()
    mine[...] = terms_ref[pl.ds(pl.multiple_of(parity * span, span), span), :] + from_sib[...]
    copies = []
    for step in range(1, half):
        peer = lax.rem(me + step, half)
        copy = pltpu.make_async_remote_copy(
            src_ref=mine.at[pl.ds(pl.multiple_of(peer * rows, rows), rows)],
            dst_ref=held.at[me],
            send_sem=send_sem.at[step - 1],
            recv_sem=recv_sem.at[step - 1],
            device_id=peer_of(peer),
            device_id_type=pl.DeviceIdType.MESH,
        )
        copy.start()
        copies.append(copy)
    total = mine[pl.ds(pl.multiple_of(me * rows, rows), rows), :]
    for copy in copies:
        copy.wait_send()
    for step in range(1, half):
        source = lax.rem(me + half - step, half)
        incoming = pltpu.make_async_remote_copy(
            src_ref=mine.at[pl.ds(0, rows)],
            dst_ref=held.at[source],
            send_sem=send_sem.at[step - 1],
            recv_sem=recv_sem.at[step - 1],
            device_id=peer_of(source),
            device_id_type=pl.DeviceIdType.MESH,
        )
        incoming.wait_recv()
        total = total + held[source]
    out_ref[...] = total


def reduce_filters(terms):
    n_sy = lax.axis_size("sy")
    n_af = lax.axis_size("af")
    group = n_sy * n_af
    rows = terms.shape[0] // group
    return pl.pallas_call(
        functools.partial(_reduce_body, n_sy, n_af),
        out_shape=jax.ShapeDtypeStruct((rows, terms.shape[1]), terms.dtype),
        in_specs=[pl.BlockSpec(memory_space=pltpu.VMEM)],
        out_specs=pl.BlockSpec(memory_space=pltpu.VMEM),
        scratch_shapes=[
            pltpu.VMEM((group // 2 * rows, terms.shape[1]), terms.dtype),
            pltpu.VMEM((group // 2 * rows, terms.shape[1]), terms.dtype),
            pltpu.VMEM((group // 2, rows, terms.shape[1]), terms.dtype),
            pltpu.SemaphoreType.DMA(()),
            pltpu.SemaphoreType.DMA(()),
            pltpu.SemaphoreType.DMA((group // 2 - 1,)),
            pltpu.SemaphoreType.DMA((group // 2 - 1,)),
        ],
        compiler_params=pltpu.CompilerParams(collective_id=1, has_side_effects=True),
        cost_estimate=pl.CostEstimate(
            flops=terms.size, bytes_accessed=2 * terms.size * 4, transcendentals=0
        ),
    )(terms)


def gather_filters(kernel):
    n_sy = lax.axis_size("sy")
    n_af = lax.axis_size("af")
    group = n_sy * n_af
    taps, channels, per_dev = kernel.shape[0] * kernel.shape[1] * kernel.shape[2], kernel.shape[3], kernel.shape[4]
    block = kernel.reshape(-1, 128)
    gathered = pl.pallas_call(
        functools.partial(_gather_body, n_sy, n_af),
        out_shape=jax.ShapeDtypeStruct((group,) + block.shape, block.dtype),
        in_specs=[pl.BlockSpec(memory_space=pltpu.VMEM)],
        out_specs=pl.BlockSpec(memory_space=pltpu.VMEM),
        scratch_shapes=[
            pltpu.SemaphoreType.DMA((group - 1,)),
            pltpu.SemaphoreType.DMA((group - 1,)),
        ],
        compiler_params=pltpu.CompilerParams(collective_id=0, has_side_effects=True),
    )(block)
    gathered = gathered.reshape(group, taps, channels, per_dev).transpose(1, 2, 0, 3)
    return gathered.reshape(kernel.shape[:4] + (group * per_dev,))


def flat_all_to_all(x, axes):
    moved = lax.all_to_all(x.reshape(x.shape[0], 2, -1), axes, 0, 0, tiled=True)
    return moved.reshape(x.shape)


def from_behind(value, axis, steps):
    count = lax.axis_size(axis)
    leading, last = (max(0, -steps), min(count, count - steps))
    return lax.ppermute(value, axis, [(source, source + steps) for source in range(leading, last)])


def strided_patch(extended, tap_d, tap_h, tap_w, depth, height, width):
    return extended[
        :,
        tap_d : tap_d + 2 * depth : 2,
        tap_h : tap_h + 2 * height : 2,
        tap_w : tap_w + 2 * width : 2,
        :,
    ]


def parity_view(extended):
    samples, d_ext, h_ext, w_ext, channels = extended.shape
    pads = [(0, 0)] + [(0, n % 2) for n in (d_ext, h_ext, w_ext)] + [(0, 0)]
    even = jnp.pad(extended, pads)
    _, d2, h2, w2, _ = even.shape
    split = even.reshape(samples, d2 // 2, 2, h2 // 2, 2, w2 // 2, 2, channels)
    return split.transpose(0, 1, 2, 3, 4, 6, 5, 7)


def im2col(classes, depth, height, width):
    patches = []
    for tap_d in range(3):
        for tap_h in range(3):
            for tap_w in range(3):
                od, oh, ow = tap_d // 2, tap_h // 2, tap_w // 2
                patch = classes[
                    :, od : od + depth, tap_d % 2, oh : oh + height, tap_h % 2, tap_w % 2, ow : ow + width, :
                ]
                patches.append(patch.reshape(-1, patch.shape[-1]))
    return jnp.concatenate(patches, axis=-1)


def weave(even_part, odd_part, axis):
    stacked = jnp.stack([even_part, odd_part], axis=axis + 1)
    shape = list(even_part.shape)
    shape[axis] = shape[axis] * 2
    return stacked.reshape(shape)


def spread_back(grad_t, kernel_full, samples, depth, height, width):
    filters = grad_t.shape[0]
    channels = kernel_full.shape[3]
    spread = lax.dot_general(
        grad_t,
        kernel_full.reshape(-1, channels, filters),
        (((0,), (2,)), ((), ())),
        preferred_element_type=jnp.float32,
    ).reshape(samples, depth, height, width, 27, channels)
    classes = {}
    for tap_d in range(3):
        for tap_h in range(3):
            for tap_w in range(3):
                term = spread[:, :, :, :, tap_d * 9 + tap_h * 3 + tap_w]
                pads = [(0, 0)]
                for tap in (tap_d, tap_h, tap_w):
                    pads.append((1, 0) if tap == 2 else (0, 1))
                pads.append((0, 0))
                term = jnp.pad(term, pads)
                key_name = (tap_d % 2, tap_h % 2, tap_w % 2)
                classes[key_name] = classes[key_name] + term if key_name in classes else term
    planes = []
    for parity_d in range(2):
        rows_h = []
        for parity_h in range(2):
            rows_h.append(weave(classes[parity_d, parity_h, 0], classes[parity_d, parity_h, 1], 3))
        planes.append(weave(rows_h[0], rows_h[1], 2))
    whole = weave(planes[0], planes[1], 1)
    return whole[:, : 2 * depth + 1, : 2 * height + 1, : 2 * width + 1, :]


def on_device(volume, kernel, cotangent):
    samples = volume.shape[0]
    depth = volume.shape[1] // 2
    height = volume.shape[2] // 2
    width = volume.shape[3] // 2
    n_sy = lax.axis_size("sy")
    n_af = lax.axis_size("af")
    kernel_part = gather_filters(kernel)
    kernel_full = lax.all_gather(kernel_part, "sx", axis=3, tiled=True)
    filters = kernel_full.shape[4]
    per_dev = filters // (n_sy * n_af)
    below = from_behind(volume[:, -1:], "sx", 1)
    n_sx_axis = lax.axis_size("sx")
    corner = lax.ppermute(
        volume[:, -1:, -1:],
        ("sx", "sy"),
        [
            (i * n_sy + j, (i + 1) * n_sy + j + 1)
            for i in range(n_sx_axis - 1)
            for j in range(n_sy - 1)
        ],
    )
    beside = jnp.concatenate([corner, from_behind(volume[:, :, -1:], "sy", 1)], axis=1)
    extended = jnp.concatenate([below, volume], axis=1)
    extended = jnp.concatenate([beside, extended], axis=2)
    extended = jnp.pad(extended, ((0, 0), (0, 0), (0, 0), (1, 0), (0, 0)))
    rows = samples * depth * height * width
    classes = parity_view(extended)
    cols = im2col(classes, depth, height, width).reshape(rows, -1)
    kernel_mat = kernel_full.reshape(-1, filters)
    total = lax.dot_general(
        kernel_mat, cols, (((0,), (1,)), ((), ())), preferred_element_type=jnp.float32
    )
    n_sx = lax.axis_size("sx")
    conv_t = total.astype(jnp.bfloat16).reshape(n_sy, n_af, per_dev, depth, height, width)
    by_af = flat_all_to_all(conv_t.transpose(1, 0, 2, 3, 4, 5), "af")
    by_region = by_af.reshape(n_sx * n_sy, per_dev, depth, height, width)
    gathered = flat_all_to_all(by_region, ("sx", "sy"))
    own_samples = cotangent.shape[0]
    features = (
        gathered.reshape(n_sx, n_sy, per_dev, depth, height, width)
        .transpose(2, 0, 3, 1, 4, 5)
        .reshape(cotangent.shape)
    )
    grad_blocks = (
        cotangent.reshape(per_dev, n_sx, depth, n_sy, height, width)
        .transpose(1, 3, 0, 2, 4, 5)
        .reshape(n_sx * n_sy, per_dev, depth, height, width)
    )
    grad_region = flat_all_to_all(grad_blocks, ("sx", "sy"))
    grad_region = grad_region.reshape(n_sx * own_samples, n_sy, per_dev, depth, height, width)
    grad_back = flat_all_to_all(grad_region, "af")
    grad_t = grad_back.transpose(1, 0, 2, 3, 4, 5).reshape(filters, rows)
    by_parity = grad_t.reshape(n_sy * n_af // 2, 2, per_dev, rows).transpose(1, 0, 2, 3)
    kernel_terms = lax.dot_general(
        by_parity.reshape(filters, rows), cols, (((1,), (0,)), ((), ())),
        preferred_element_type=jnp.float32,
    )
    channels = kernel_full.shape[3]
    own_ch = channels // n_sx
    by_filter = reduce_filters(kernel_terms)
    by_filter = by_filter.reshape(per_dev, 27, n_sx, own_ch).transpose(2, 1, 3, 0)
    kernel_grad = lax.all_to_all(by_filter, "sx", 0, 0, tiled=True).sum(axis=0)
    kernel_grad = kernel_grad.reshape(3, 3, 3, own_ch, per_dev)
    partial_grad = spread_back(grad_t, kernel_full, samples, depth, height, width)
    from_above = from_behind(partial_grad[:, 0:1], "sx", -1)
    own_depth = partial_grad[:, 1:]
    own_depth = jnp.concatenate([own_depth[:, :-1], own_depth[:, -1:] + from_above], axis=1)
    from_right = from_behind(own_depth[:, :, 0:1].astype(jnp.bfloat16), "sy", -1).astype(
        jnp.float32
    )
    own_height = own_depth[:, :, 1:]
    own_height = jnp.concatenate(
        [own_height[:, :, :-1], own_height[:, :, -1:] + from_right], axis=2
    )
    volume_grad = own_height[:, :, :, 1:]
    return (features, volume_grad.astype(jnp.bfloat16), kernel_grad)


def solution(mesh):
    return jax.shard_map(
        on_device,
        mesh=mesh,
        in_specs=(
            P("af", "sx", "sy", None, None),
            P(None, None, None, "sx", ("sy", "af")),
            P("sx", ("sy", "af"), None, None),
        ),
        out_specs=(
            P("sx", ("sy", "af"), None, None),
            P("af", "sx", "sy", None, None),
            P(None, None, None, "sx", ("sy", "af")),
        ),
        check_vma=False,
    )
```

```python
import functools

import jax
import jax.numpy as jnp
from jax import lax
from jax.experimental import pallas as pl
from jax.experimental.pallas import tpu as pltpu
from jax.sharding import PartitionSpec as P


def _gather_body(n_sy, n_af, block_ref, out_ref, send_sem, recv_sem):
    group = n_sy * n_af
    sx = lax.axis_index("sx")
    me = lax.axis_index("sy") * n_af + lax.axis_index("af")
    barrier = pltpu.get_barrier_semaphore()
    for step in range(1, group):
        peer = lax.rem(me + step, group)
        pl.semaphore_signal(
            barrier,
            inc=1,
            device_id=(sx, peer // n_af, lax.rem(peer, n_af)),
            device_id_type=pl.DeviceIdType.MESH,
        )
    pl.semaphore_wait(barrier, group - 1)
    copies = []
    for step in range(1, group):
        peer = lax.rem(me + step, group)
        copy = pltpu.make_async_remote_copy(
            src_ref=block_ref,
            dst_ref=out_ref.at[me],
            send_sem=send_sem.at[step - 1],
            recv_sem=recv_sem.at[step - 1],
            device_id=(sx, peer // n_af, lax.rem(peer, n_af)),
            device_id_type=pl.DeviceIdType.MESH,
        )
        copy.start()
        copies.append(copy)
    out_ref[me] = block_ref[...]
    for copy in copies:
        copy.wait_send()
    for step in range(1, group):
        source = lax.rem(me + group - step, group)
        incoming = pltpu.make_async_remote_copy(
            src_ref=block_ref,
            dst_ref=out_ref.at[source],
            send_sem=send_sem.at[step - 1],
            recv_sem=recv_sem.at[step - 1],
            device_id=(sx, source // n_af, lax.rem(source, n_af)),
            device_id_type=pl.DeviceIdType.MESH,
        )
        incoming.wait_recv()


def _reduce_body(n_sy, n_af, terms_ref, out_ref, from_sib, mine, held, sib_send, sib_recv, send_sem, recv_sem):
    half = n_sy * n_af // 2
    rows = out_ref.shape[0]
    span = half * rows
    sx = lax.axis_index("sx")
    sy = lax.axis_index("sy")
    af = lax.axis_index("af")
    parity = lax.rem(af, 2)
    sib_af = af + 1 - 2 * parity
    me = sy * (n_af // 2) + af // 2

    def peer_of(index):
        block = 2 * index + parity
        return (sx, block // n_af, lax.rem(block, n_af))

    barrier = pltpu.get_barrier_semaphore()
    pl.semaphore_signal(barrier, inc=1, device_id=(sx, sy, sib_af), device_id_type=pl.DeviceIdType.MESH)
    for step in range(1, half):
        pl.semaphore_signal(
            barrier,
            inc=1,
            device_id=peer_of(lax.rem(me + step, half)),
            device_id_type=pl.DeviceIdType.MESH,
        )
    pl.semaphore_wait(barrier, half)
    to_sib = pltpu.make_async_remote_copy(
        src_ref=terms_ref.at[pl.ds(pl.multiple_of((1 - parity) * span, span), span)],
        dst_ref=from_sib,
        send_sem=sib_send,
        recv_sem=sib_recv,
        device_id=(sx, sy, sib_af),
        device_id_type=pl.DeviceIdType.MESH,
    )
    to_sib.start()
    to_sib.wait_send()
    to_sib.wait_recv()
    mine[...] = terms_ref[pl.ds(pl.multiple_of(parity * span, span), span), :] + from_sib[...]
    copies = []
    for step in range(1, half):
        peer = lax.rem(me + step, half)
        copy = pltpu.make_async_remote_copy(
            src_ref=mine.at[pl.ds(pl.multiple_of(peer * rows, rows), rows)],
            dst_ref=held.at[me],
            send_sem=send_sem.at[step - 1],
            recv_sem=recv_sem.at[step - 1],
            device_id=peer_of(peer),
            device_id_type=pl.DeviceIdType.MESH,
        )
        copy.start()
        copies.append(copy)
    total = mine[pl.ds(pl.multiple_of(me * rows, rows), rows), :]
    for copy in copies:
        copy.wait_send()
    for step in range(1, half):
        source = lax.rem(me + half - step, half)
        incoming = pltpu.make_async_remote_copy(
            src_ref=mine.at[pl.ds(0, rows)],
            dst_ref=held.at[source],
            send_sem=send_sem.at[step - 1],
            recv_sem=recv_sem.at[step - 1],
            device_id=peer_of(source),
            device_id_type=pl.DeviceIdType.MESH,
        )
        incoming.wait_recv()
        total = total + held[source]
    out_ref[...] = total


def reduce_filters(terms):
    n_sy = lax.axis_size("sy")
    n_af = lax.axis_size("af")
    group = n_sy * n_af
    rows = terms.shape[0] // group
    return pl.pallas_call(
        functools.partial(_reduce_body, n_sy, n_af),
        out_shape=jax.ShapeDtypeStruct((rows, terms.shape[1]), terms.dtype),
        in_specs=[pl.BlockSpec(memory_space=pltpu.VMEM)],
        out_specs=pl.BlockSpec(memory_space=pltpu.VMEM),
        scratch_shapes=[
            pltpu.VMEM((group // 2 * rows, terms.shape[1]), terms.dtype),
            pltpu.VMEM((group // 2 * rows, terms.shape[1]), terms.dtype),
            pltpu.VMEM((group // 2, rows, terms.shape[1]), terms.dtype),
            pltpu.SemaphoreType.DMA(()),
            pltpu.SemaphoreType.DMA(()),
            pltpu.SemaphoreType.DMA((group // 2 - 1,)),
            pltpu.SemaphoreType.DMA((group // 2 - 1,)),
        ],
        compiler_params=pltpu.CompilerParams(collective_id=1, has_side_effects=True),
        cost_estimate=pl.CostEstimate(
            flops=terms.size, bytes_accessed=2 * terms.size * 4, transcendentals=0
        ),
    )(terms)


def gather_filters(kernel):
    n_sy = lax.axis_size("sy")
    n_af = lax.axis_size("af")
    group = n_sy * n_af
    taps, channels, per_dev = kernel.shape[0] * kernel.shape[1] * kernel.shape[2], kernel.shape[3], kernel.shape[4]
    block = kernel.reshape(-1, 128)
    gathered = pl.pallas_call(
        functools.partial(_gather_body, n_sy, n_af),
        out_shape=jax.ShapeDtypeStruct((group,) + block.shape, block.dtype),
        in_specs=[pl.BlockSpec(memory_space=pltpu.VMEM)],
        out_specs=pl.BlockSpec(memory_space=pltpu.VMEM),
        scratch_shapes=[
            pltpu.SemaphoreType.DMA((group - 1,)),
            pltpu.SemaphoreType.DMA((group - 1,)),
        ],
        compiler_params=pltpu.CompilerParams(collective_id=0, has_side_effects=True),
    )(block)
    gathered = gathered.reshape(group, taps, channels, per_dev).transpose(1, 2, 0, 3)
    return gathered.reshape(kernel.shape[:4] + (group * per_dev,))


def flat_all_to_all(x, axes):
    moved = lax.all_to_all(x.reshape(x.shape[0], 2, -1), axes, 0, 0, tiled=True)
    return moved.reshape(x.shape)


def from_behind(value, axis, steps):
    count = lax.axis_size(axis)
    leading, last = (max(0, -steps), min(count, count - steps))
    return lax.ppermute(value, axis, [(source, source + steps) for source in range(leading, last)])


def strided_patch(extended, tap_d, tap_h, tap_w, depth, height, width):
    return extended[
        :,
        tap_d : tap_d + 2 * depth : 2,
        tap_h : tap_h + 2 * height : 2,
        tap_w : tap_w + 2 * width : 2,
        :,
    ]


def parity_view(extended):
    samples, d_ext, h_ext, w_ext, channels = extended.shape
    pads = [(0, 0)] + [(0, n % 2) for n in (d_ext, h_ext, w_ext)] + [(0, 0)]
    even = jnp.pad(extended, pads)
    _, d2, h2, w2, _ = even.shape
    split = even.reshape(samples, d2 // 2, 2, h2 // 2, 2, w2 // 2, 2, channels)
    return split.transpose(0, 1, 2, 3, 4, 6, 5, 7)


def _im2col_body(depth, height, width, x_ref, out_ref):
    channels = x_ref.shape[-1]
    tap = 0
    for tap_d in range(3):
        for tap_h in range(3):
            for tap_w in range(3):
                od, oh, ow = tap_d // 2, tap_h // 2, tap_w // 2
                for p in range(depth):
                    for q in range(height):
                        row = x_ref[0, od + p, tap_d % 2, oh + q, tap_h % 2, tap_w % 2, ow : ow + width, :]
                        out_ref[p, q, :, tap * channels : (tap + 1) * channels] = row.astype(out_ref.dtype)
                tap += 1


def im2col(classes, depth, height, width):
    channels = classes.shape[-1]
    return pl.pallas_call(
        functools.partial(_im2col_body, depth, height, width),
        out_shape=jax.ShapeDtypeStruct((depth, height, width, 27 * channels), classes.dtype),
        in_specs=[pl.BlockSpec(memory_space=pltpu.VMEM)],
        out_specs=pl.BlockSpec(memory_space=pltpu.VMEM),
    )(classes.astype(jnp.float32))


def weave(even_part, odd_part, axis):
    stacked = jnp.stack([even_part, odd_part], axis=axis + 1)
    shape = list(even_part.shape)
    shape[axis] = shape[axis] * 2
    return stacked.reshape(shape)


def spread_back(grad_t, kernel_full, samples, depth, height, width):
    filters = grad_t.shape[0]
    channels = kernel_full.shape[3]
    spread = lax.dot_general(
        grad_t,
        kernel_full.reshape(-1, channels, filters),
        (((0,), (2,)), ((), ())),
        preferred_element_type=jnp.float32,
    ).reshape(samples, depth, height, width, 27, channels)
    classes = {}
    for tap_d in range(3):
        for tap_h in range(3):
            for tap_w in range(3):
                term = spread[:, :, :, :, tap_d * 9 + tap_h * 3 + tap_w]
                pads = [(0, 0)]
                for tap in (tap_d, tap_h, tap_w):
                    pads.append((1, 0) if tap == 2 else (0, 1))
                pads.append((0, 0))
                term = jnp.pad(term, pads)
                key_name = (tap_d % 2, tap_h % 2, tap_w % 2)
                classes[key_name] = classes[key_name] + term if key_name in classes else term
    planes = []
    for parity_d in range(2):
        rows_h = []
        for parity_h in range(2):
            rows_h.append(weave(classes[parity_d, parity_h, 0], classes[parity_d, parity_h, 1], 3))
        planes.append(weave(rows_h[0], rows_h[1], 2))
    whole = weave(planes[0], planes[1], 1)
    return whole[:, : 2 * depth + 1, : 2 * height + 1, : 2 * width + 1, :]


def on_device(volume, kernel, cotangent):
    samples = volume.shape[0]
    depth = volume.shape[1] // 2
    height = volume.shape[2] // 2
    width = volume.shape[3] // 2
    n_sy = lax.axis_size("sy")
    n_af = lax.axis_size("af")
    kernel_part = gather_filters(kernel)
    kernel_full = lax.all_gather(kernel_part, "sx", axis=3, tiled=True)
    filters = kernel_full.shape[4]
    per_dev = filters // (n_sy * n_af)
    below = from_behind(volume[:, -1:], "sx", 1)
    n_sx_axis = lax.axis_size("sx")
    corner = lax.ppermute(
        volume[:, -1:, -1:],
        ("sx", "sy"),
        [
            (i * n_sy + j, (i + 1) * n_sy + j + 1)
            for i in range(n_sx_axis - 1)
            for j in range(n_sy - 1)
        ],
    )
    beside = jnp.concatenate([corner, from_behind(volume[:, :, -1:], "sy", 1)], axis=1)
    extended = jnp.concatenate([below, volume], axis=1)
    extended = jnp.concatenate([beside, extended], axis=2)
    extended = jnp.pad(extended, ((0, 0), (0, 0), (0, 0), (1, 0), (0, 0)))
    rows = samples * depth * height * width
    classes = parity_view(extended)
    cols = im2col(classes, depth, height, width).reshape(rows, -1)
    kernel_mat = kernel_full.reshape(-1, filters)
    total = lax.dot_general(
        kernel_mat, cols, (((0,), (1,)), ((), ())), preferred_element_type=jnp.float32
    )
    n_sx = lax.axis_size("sx")
    conv_t = total.astype(jnp.bfloat16).reshape(n_sy, n_af, per_dev, depth, height, width)
    by_af = flat_all_to_all(conv_t.transpose(1, 0, 2, 3, 4, 5), "af")
    by_region = by_af.reshape(n_sx * n_sy, per_dev, depth, height, width)
    gathered = flat_all_to_all(by_region, ("sx", "sy"))
    own_samples = cotangent.shape[0]
    features = (
        gathered.reshape(n_sx, n_sy, per_dev, depth, height, width)
        .transpose(2, 0, 3, 1, 4, 5)
        .reshape(cotangent.shape)
    )
    grad_blocks = (
        cotangent.reshape(per_dev, n_sx, depth, n_sy, height, width)
        .transpose(1, 3, 0, 2, 4, 5)
        .reshape(n_sx * n_sy, per_dev, depth, height, width)
    )
    grad_region = flat_all_to_all(grad_blocks, ("sx", "sy"))
    grad_region = grad_region.reshape(n_sx * own_samples, n_sy, per_dev, depth, height, width)
    grad_back = flat_all_to_all(grad_region, "af")
    grad_t = grad_back.transpose(1, 0, 2, 3, 4, 5).reshape(filters, rows)
    by_parity = grad_t.reshape(n_sy * n_af // 2, 2, per_dev, rows).transpose(1, 0, 2, 3)
    kernel_terms = lax.dot_general(
        by_parity.reshape(filters, rows), cols, (((1,), (0,)), ((), ())),
        preferred_element_type=jnp.float32,
    )
    channels = kernel_full.shape[3]
    own_ch = channels // n_sx
    by_filter = reduce_filters(kernel_terms)
    by_filter = by_filter.reshape(per_dev, 27, n_sx, own_ch).transpose(2, 1, 3, 0)
    kernel_grad = lax.all_to_all(by_filter, "sx", 0, 0, tiled=True).sum(axis=0)
    kernel_grad = kernel_grad.reshape(3, 3, 3, own_ch, per_dev)
    partial_grad = spread_back(grad_t, kernel_full, samples, depth, height, width)
    from_above = from_behind(partial_grad[:, 0:1], "sx", -1)
    own_depth = partial_grad[:, 1:]
    own_depth = jnp.concatenate([own_depth[:, :-1], own_depth[:, -1:] + from_above], axis=1)
    from_right = from_behind(own_depth[:, :, 0:1].astype(jnp.bfloat16), "sy", -1).astype(
        jnp.float32
    )
    own_height = own_depth[:, :, 1:]
    own_height = jnp.concatenate(
        [own_height[:, :, :-1], own_height[:, :, -1:] + from_right], axis=2
    )
    volume_grad = own_height[:, :, :, 1:]
    return (features, volume_grad.astype(jnp.bfloat16), kernel_grad)


def solution(mesh):
    return jax.shard_map(
        on_device,
        mesh=mesh,
        in_specs=(
            P("af", "sx", "sy", None, None),
            P(None, None, None, "sx", ("sy", "af")),
            P("sx", ("sy", "af"), None, None),
        ),
        out_specs=(
            P("sx", ("sy", "af"), None, None),
            P("af", "sx", "sy", None, None),
            P(None, None, None, "sx", ("sy", "af")),
        ),
        check_vma=False,
    )
```

```python
import functools

import jax
import jax.numpy as jnp
from jax import lax
from jax.experimental import pallas as pl
from jax.experimental.pallas import tpu as pltpu
from jax.sharding import PartitionSpec as P


def _gather_body(n_sy, n_af, block_ref, out_ref, send_sem, recv_sem):
    group = n_sy * n_af
    sx = lax.axis_index("sx")
    me = lax.axis_index("sy") * n_af + lax.axis_index("af")
    barrier = pltpu.get_barrier_semaphore()
    for step in range(1, group):
        peer = lax.rem(me + step, group)
        pl.semaphore_signal(
            barrier,
            inc=1,
            device_id=(sx, peer // n_af, lax.rem(peer, n_af)),
            device_id_type=pl.DeviceIdType.MESH,
        )
    pl.semaphore_wait(barrier, group - 1)
    copies = []
    for step in range(1, group):
        peer = lax.rem(me + step, group)
        copy = pltpu.make_async_remote_copy(
            src_ref=block_ref,
            dst_ref=out_ref.at[me],
            send_sem=send_sem.at[step - 1],
            recv_sem=recv_sem.at[step - 1],
            device_id=(sx, peer // n_af, lax.rem(peer, n_af)),
            device_id_type=pl.DeviceIdType.MESH,
        )
        copy.start()
        copies.append(copy)
    out_ref[me] = block_ref[...]
    for copy in copies:
        copy.wait_send()
    for step in range(1, group):
        source = lax.rem(me + group - step, group)
        incoming = pltpu.make_async_remote_copy(
            src_ref=block_ref,
            dst_ref=out_ref.at[source],
            send_sem=send_sem.at[step - 1],
            recv_sem=recv_sem.at[step - 1],
            device_id=(sx, source // n_af, lax.rem(source, n_af)),
            device_id_type=pl.DeviceIdType.MESH,
        )
        incoming.wait_recv()


def _reduce_body(n_sy, n_af, terms_ref, out_ref, from_sib, mine, held, sib_send, sib_recv, send_sem, recv_sem):
    half = n_sy * n_af // 2
    rows = out_ref.shape[0]
    span = half * rows
    sx = lax.axis_index("sx")
    sy = lax.axis_index("sy")
    af = lax.axis_index("af")
    parity = lax.rem(af, 2)
    sib_af = af + 1 - 2 * parity
    me = sy * (n_af // 2) + af // 2

    def peer_of(index):
        block = 2 * index + parity
        return (sx, block // n_af, lax.rem(block, n_af))

    barrier = pltpu.get_barrier_semaphore()
    pl.semaphore_signal(barrier, inc=1, device_id=(sx, sy, sib_af), device_id_type=pl.DeviceIdType.MESH)
    for step in range(1, half):
        pl.semaphore_signal(
            barrier,
            inc=1,
            device_id=peer_of(lax.rem(me + step, half)),
            device_id_type=pl.DeviceIdType.MESH,
        )
    pl.semaphore_wait(barrier, half)
    to_sib = pltpu.make_async_remote_copy(
        src_ref=terms_ref.at[pl.ds(pl.multiple_of((1 - parity) * span, span), span)],
        dst_ref=from_sib,
        send_sem=sib_send,
        recv_sem=sib_recv,
        device_id=(sx, sy, sib_af),
        device_id_type=pl.DeviceIdType.MESH,
    )
    to_sib.start()
    to_sib.wait_send()
    to_sib.wait_recv()
    mine[...] = terms_ref[pl.ds(pl.multiple_of(parity * span, span), span), :] + from_sib[...]
    copies = []
    for step in range(1, half):
        peer = lax.rem(me + step, half)
        copy = pltpu.make_async_remote_copy(
            src_ref=mine.at[pl.ds(pl.multiple_of(peer * rows, rows), rows)],
            dst_ref=held.at[me],
            send_sem=send_sem.at[step - 1],
            recv_sem=recv_sem.at[step - 1],
            device_id=peer_of(peer),
            device_id_type=pl.DeviceIdType.MESH,
        )
        copy.start()
        copies.append(copy)
    total = mine[pl.ds(pl.multiple_of(me * rows, rows), rows), :]
    for copy in copies:
        copy.wait_send()
    for step in range(1, half):
        source = lax.rem(me + half - step, half)
        incoming = pltpu.make_async_remote_copy(
            src_ref=mine.at[pl.ds(0, rows)],
            dst_ref=held.at[source],
            send_sem=send_sem.at[step - 1],
            recv_sem=recv_sem.at[step - 1],
            device_id=peer_of(source),
            device_id_type=pl.DeviceIdType.MESH,
        )
        incoming.wait_recv()
        total = total + held[source]
    out_ref[...] = total


def reduce_filters(terms):
    n_sy = lax.axis_size("sy")
    n_af = lax.axis_size("af")
    group = n_sy * n_af
    rows = terms.shape[0] // group
    return pl.pallas_call(
        functools.partial(_reduce_body, n_sy, n_af),
        out_shape=jax.ShapeDtypeStruct((rows, terms.shape[1]), terms.dtype),
        in_specs=[pl.BlockSpec(memory_space=pltpu.VMEM)],
        out_specs=pl.BlockSpec(memory_space=pltpu.VMEM),
        scratch_shapes=[
            pltpu.VMEM((group // 2 * rows, terms.shape[1]), terms.dtype),
            pltpu.VMEM((group // 2 * rows, terms.shape[1]), terms.dtype),
            pltpu.VMEM((group // 2, rows, terms.shape[1]), terms.dtype),
            pltpu.SemaphoreType.DMA(()),
            pltpu.SemaphoreType.DMA(()),
            pltpu.SemaphoreType.DMA((group // 2 - 1,)),
            pltpu.SemaphoreType.DMA((group // 2 - 1,)),
        ],
        compiler_params=pltpu.CompilerParams(collective_id=1, has_side_effects=True),
        cost_estimate=pl.CostEstimate(
            flops=terms.size, bytes_accessed=2 * terms.size * 4, transcendentals=0
        ),
    )(terms)


def gather_filters(kernel):
    n_sy = lax.axis_size("sy")
    n_af = lax.axis_size("af")
    group = n_sy * n_af
    taps, channels, per_dev = kernel.shape[0] * kernel.shape[1] * kernel.shape[2], kernel.shape[3], kernel.shape[4]
    block = kernel.reshape(-1, 128)
    gathered = pl.pallas_call(
        functools.partial(_gather_body, n_sy, n_af),
        out_shape=jax.ShapeDtypeStruct((group,) + block.shape, block.dtype),
        in_specs=[pl.BlockSpec(memory_space=pltpu.VMEM)],
        out_specs=pl.BlockSpec(memory_space=pltpu.VMEM),
        scratch_shapes=[
            pltpu.SemaphoreType.DMA((group - 1,)),
            pltpu.SemaphoreType.DMA((group - 1,)),
        ],
        compiler_params=pltpu.CompilerParams(collective_id=0, has_side_effects=True),
    )(block)
    gathered = gathered.reshape(group, taps, channels, per_dev).transpose(1, 2, 0, 3)
    return gathered.reshape(kernel.shape[:4] + (group * per_dev,))


def flat_all_to_all(x, axes):
    moved = lax.all_to_all(x.reshape(x.shape[0], 2, -1), axes, 0, 0, tiled=True)
    return moved.reshape(x.shape)


def from_behind(value, axis, steps):
    count = lax.axis_size(axis)
    leading, last = (max(0, -steps), min(count, count - steps))
    return lax.ppermute(value, axis, [(source, source + steps) for source in range(leading, last)])


def strided_patch(extended, tap_d, tap_h, tap_w, depth, height, width):
    return extended[
        :,
        tap_d : tap_d + 2 * depth : 2,
        tap_h : tap_h + 2 * height : 2,
        tap_w : tap_w + 2 * width : 2,
        :,
    ]


def parity_view(extended):
    samples, d_ext, h_ext, w_ext, channels = extended.shape
    pads = [(0, 0)] + [(0, n % 2) for n in (d_ext, h_ext, w_ext)] + [(0, 0)]
    even = jnp.pad(extended, pads)
    _, d2, h2, w2, _ = even.shape
    return even.reshape(samples, d2 // 2, 2, h2 // 2, 2, w2, channels)


def _im2col_body(depth, height, width, x_ref, out_ref):
    channels = x_ref.shape[-1]
    tap = 0
    for tap_d in range(3):
        for tap_h in range(3):
            for tap_w in range(3):
                od, oh = tap_d // 2, tap_h // 2
                for p in range(depth):
                    for q in range(height):
                        row = x_ref[0, od + p, tap_d % 2, oh + q, tap_h % 2, pl.ds(tap_w, width, stride=2), :]
                        out_ref[p, q, :, tap * channels : (tap + 1) * channels] = row.astype(out_ref.dtype)
                tap += 1


def im2col(classes, depth, height, width):
    channels = classes.shape[-1]
    return pl.pallas_call(
        functools.partial(_im2col_body, depth, height, width),
        out_shape=jax.ShapeDtypeStruct((depth, height, width, 27 * channels), classes.dtype),
        in_specs=[pl.BlockSpec(memory_space=pltpu.VMEM)],
        out_specs=pl.BlockSpec(memory_space=pltpu.VMEM),
    )(classes.astype(jnp.float32))


def weave(even_part, odd_part, axis):
    stacked = jnp.stack([even_part, odd_part], axis=axis + 1)
    shape = list(even_part.shape)
    shape[axis] = shape[axis] * 2
    return stacked.reshape(shape)


def spread_back(grad_t, kernel_full, samples, depth, height, width):
    filters = grad_t.shape[0]
    channels = kernel_full.shape[3]
    spread = lax.dot_general(
        grad_t,
        kernel_full.reshape(-1, channels, filters),
        (((0,), (2,)), ((), ())),
        preferred_element_type=jnp.float32,
    ).reshape(samples, depth, height, width, 27, channels)
    classes = {}
    for tap_d in range(3):
        for tap_h in range(3):
            for tap_w in range(3):
                term = spread[:, :, :, :, tap_d * 9 + tap_h * 3 + tap_w]
                pads = [(0, 0)]
                for tap in (tap_d, tap_h, tap_w):
                    pads.append((1, 0) if tap == 2 else (0, 1))
                pads.append((0, 0))
                term = jnp.pad(term, pads)
                key_name = (tap_d % 2, tap_h % 2, tap_w % 2)
                classes[key_name] = classes[key_name] + term if key_name in classes else term
    planes = []
    for parity_d in range(2):
        rows_h = []
        for parity_h in range(2):
            rows_h.append(weave(classes[parity_d, parity_h, 0], classes[parity_d, parity_h, 1], 3))
        planes.append(weave(rows_h[0], rows_h[1], 2))
    whole = weave(planes[0], planes[1], 1)
    return whole[:, : 2 * depth + 1, : 2 * height + 1, : 2 * width + 1, :]


def on_device(volume, kernel, cotangent):
    samples = volume.shape[0]
    depth = volume.shape[1] // 2
    height = volume.shape[2] // 2
    width = volume.shape[3] // 2
    n_sy = lax.axis_size("sy")
    n_af = lax.axis_size("af")
    kernel_part = gather_filters(kernel)
    kernel_full = lax.all_gather(kernel_part, "sx", axis=3, tiled=True)
    filters = kernel_full.shape[4]
    per_dev = filters // (n_sy * n_af)
    below = from_behind(volume[:, -1:], "sx", 1)
    n_sx_axis = lax.axis_size("sx")
    corner = lax.ppermute(
        volume[:, -1:, -1:],
        ("sx", "sy"),
        [
            (i * n_sy + j, (i + 1) * n_sy + j + 1)
            for i in range(n_sx_axis - 1)
            for j in range(n_sy - 1)
        ],
    )
    beside = jnp.concatenate([corner, from_behind(volume[:, :, -1:], "sy", 1)], axis=1)
    extended = jnp.concatenate([below, volume], axis=1)
    extended = jnp.concatenate([beside, extended], axis=2)
    extended = jnp.pad(extended, ((0, 0), (0, 0), (0, 0), (1, 0), (0, 0)))
    rows = samples * depth * height * width
    classes = parity_view(extended)
    cols = im2col(classes, depth, height, width).reshape(rows, -1)
    kernel_mat = kernel_full.reshape(-1, filters)
    total = lax.dot_general(
        kernel_mat, cols, (((0,), (1,)), ((), ())), preferred_element_type=jnp.float32
    )
    n_sx = lax.axis_size("sx")
    conv_t = total.astype(jnp.bfloat16).reshape(n_sy, n_af, per_dev, depth, height, width)
    by_af = flat_all_to_all(conv_t.transpose(1, 0, 2, 3, 4, 5), "af")
    by_region = by_af.reshape(n_sx * n_sy, per_dev, depth, height, width)
    gathered = flat_all_to_all(by_region, ("sx", "sy"))
    own_samples = cotangent.shape[0]
    features = (
        gathered.reshape(n_sx, n_sy, per_dev, depth, height, width)
        .transpose(2, 0, 3, 1, 4, 5)
        .reshape(cotangent.shape)
    )
    grad_blocks = (
        cotangent.reshape(per_dev, n_sx, depth, n_sy, height, width)
        .transpose(1, 3, 0, 2, 4, 5)
        .reshape(n_sx * n_sy, per_dev, depth, height, width)
    )
    grad_region = flat_all_to_all(grad_blocks, ("sx", "sy"))
    grad_region = grad_region.reshape(n_sx * own_samples, n_sy, per_dev, depth, height, width)
    grad_back = flat_all_to_all(grad_region, "af")
    grad_t = grad_back.transpose(1, 0, 2, 3, 4, 5).reshape(filters, rows)
    by_parity = grad_t.reshape(n_sy * n_af // 2, 2, per_dev, rows).transpose(1, 0, 2, 3)
    kernel_terms = lax.dot_general(
        by_parity.reshape(filters, rows), cols, (((1,), (0,)), ((), ())),
        preferred_element_type=jnp.float32,
    )
    channels = kernel_full.shape[3]
    own_ch = channels // n_sx
    by_filter = reduce_filters(kernel_terms)
    by_filter = by_filter.reshape(per_dev, 27, n_sx, own_ch).transpose(2, 1, 3, 0)
    kernel_grad = lax.all_to_all(by_filter, "sx", 0, 0, tiled=True).sum(axis=0)
    kernel_grad = kernel_grad.reshape(3, 3, 3, own_ch, per_dev)
    partial_grad = spread_back(grad_t, kernel_full, samples, depth, height, width)
    from_above = from_behind(partial_grad[:, 0:1], "sx", -1)
    own_depth = partial_grad[:, 1:]
    own_depth = jnp.concatenate([own_depth[:, :-1], own_depth[:, -1:] + from_above], axis=1)
    from_right = from_behind(own_depth[:, :, 0:1].astype(jnp.bfloat16), "sy", -1).astype(
        jnp.float32
    )
    own_height = own_depth[:, :, 1:]
    own_height = jnp.concatenate(
        [own_height[:, :, :-1], own_height[:, :, -1:] + from_right], axis=2
    )
    volume_grad = own_height[:, :, :, 1:]
    return (features, volume_grad.astype(jnp.bfloat16), kernel_grad)


def solution(mesh):
    return jax.shard_map(
        on_device,
        mesh=mesh,
        in_specs=(
            P("af", "sx", "sy", None, None),
            P(None, None, None, "sx", ("sy", "af")),
            P("sx", ("sy", "af"), None, None),
        ),
        out_specs=(
            P("sx", ("sy", "af"), None, None),
            P("af", "sx", "sy", None, None),
            P(None, None, None, "sx", ("sy", "af")),
        ),
        check_vma=False,
    )
```

```python
import functools

import jax
import jax.numpy as jnp
from jax import lax
from jax.experimental import pallas as pl
from jax.experimental.pallas import tpu as pltpu
from jax.sharding import PartitionSpec as P


def _gather_body(n_sy, n_af, block_ref, out_ref, send_sem, recv_sem):
    group = n_sy * n_af
    sx = lax.axis_index("sx")
    me = lax.axis_index("sy") * n_af + lax.axis_index("af")
    barrier = pltpu.get_barrier_semaphore()
    for step in range(1, group):
        peer = lax.rem(me + step, group)
        pl.semaphore_signal(
            barrier,
            inc=1,
            device_id=(sx, peer // n_af, lax.rem(peer, n_af)),
            device_id_type=pl.DeviceIdType.MESH,
        )
    pl.semaphore_wait(barrier, group - 1)
    copies = []
    for step in range(1, group):
        peer = lax.rem(me + step, group)
        copy = pltpu.make_async_remote_copy(
            src_ref=block_ref,
            dst_ref=out_ref.at[me],
            send_sem=send_sem.at[step - 1],
            recv_sem=recv_sem.at[step - 1],
            device_id=(sx, peer // n_af, lax.rem(peer, n_af)),
            device_id_type=pl.DeviceIdType.MESH,
        )
        copy.start()
        copies.append(copy)
    out_ref[me] = block_ref[...]
    for copy in copies:
        copy.wait_send()
    for step in range(1, group):
        source = lax.rem(me + group - step, group)
        incoming = pltpu.make_async_remote_copy(
            src_ref=block_ref,
            dst_ref=out_ref.at[source],
            send_sem=send_sem.at[step - 1],
            recv_sem=recv_sem.at[step - 1],
            device_id=(sx, source // n_af, lax.rem(source, n_af)),
            device_id_type=pl.DeviceIdType.MESH,
        )
        incoming.wait_recv()


def _reduce_body(n_sy, n_af, terms_ref, out_ref, from_sib, mine, held, sib_send, sib_recv, send_sem, recv_sem):
    half = n_sy * n_af // 2
    rows = out_ref.shape[0]
    span = half * rows
    sx = lax.axis_index("sx")
    sy = lax.axis_index("sy")
    af = lax.axis_index("af")
    parity = lax.rem(af, 2)
    sib_af = af + 1 - 2 * parity
    me = sy * (n_af // 2) + af // 2

    def peer_of(index):
        block = 2 * index + parity
        return (sx, block // n_af, lax.rem(block, n_af))

    barrier = pltpu.get_barrier_semaphore()
    pl.semaphore_signal(barrier, inc=1, device_id=(sx, sy, sib_af), device_id_type=pl.DeviceIdType.MESH)
    for step in range(1, half):
        pl.semaphore_signal(
            barrier,
            inc=1,
            device_id=peer_of(lax.rem(me + step, half)),
            device_id_type=pl.DeviceIdType.MESH,
        )
    pl.semaphore_wait(barrier, half)
    to_sib = pltpu.make_async_remote_copy(
        src_ref=terms_ref.at[pl.ds(pl.multiple_of((1 - parity) * span, span), span)],
        dst_ref=from_sib,
        send_sem=sib_send,
        recv_sem=sib_recv,
        device_id=(sx, sy, sib_af),
        device_id_type=pl.DeviceIdType.MESH,
    )
    to_sib.start()
    to_sib.wait_send()
    to_sib.wait_recv()
    mine[...] = terms_ref[pl.ds(pl.multiple_of(parity * span, span), span), :] + from_sib[...]
    copies = []
    for step in range(1, half):
        peer = lax.rem(me + step, half)
        copy = pltpu.make_async_remote_copy(
            src_ref=mine.at[pl.ds(pl.multiple_of(peer * rows, rows), rows)],
            dst_ref=held.at[me],
            send_sem=send_sem.at[step - 1],
            recv_sem=recv_sem.at[step - 1],
            device_id=peer_of(peer),
            device_id_type=pl.DeviceIdType.MESH,
        )
        copy.start()
        copies.append(copy)
    total = mine[pl.ds(pl.multiple_of(me * rows, rows), rows), :]
    for copy in copies:
        copy.wait_send()
    for step in range(1, half):
        source = lax.rem(me + half - step, half)
        incoming = pltpu.make_async_remote_copy(
            src_ref=mine.at[pl.ds(0, rows)],
            dst_ref=held.at[source],
            send_sem=send_sem.at[step - 1],
            recv_sem=recv_sem.at[step - 1],
            device_id=peer_of(source),
            device_id_type=pl.DeviceIdType.MESH,
        )
        incoming.wait_recv()
        total = total + held[source]
    out_ref[...] = total


def reduce_filters(terms):
    n_sy = lax.axis_size("sy")
    n_af = lax.axis_size("af")
    group = n_sy * n_af
    rows = terms.shape[0] // group
    return pl.pallas_call(
        functools.partial(_reduce_body, n_sy, n_af),
        out_shape=jax.ShapeDtypeStruct((rows, terms.shape[1]), terms.dtype),
        in_specs=[pl.BlockSpec(memory_space=pltpu.VMEM)],
        out_specs=pl.BlockSpec(memory_space=pltpu.VMEM),
        scratch_shapes=[
            pltpu.VMEM((group // 2 * rows, terms.shape[1]), terms.dtype),
            pltpu.VMEM((group // 2 * rows, terms.shape[1]), terms.dtype),
            pltpu.VMEM((group // 2, rows, terms.shape[1]), terms.dtype),
            pltpu.SemaphoreType.DMA(()),
            pltpu.SemaphoreType.DMA(()),
            pltpu.SemaphoreType.DMA((group // 2 - 1,)),
            pltpu.SemaphoreType.DMA((group // 2 - 1,)),
        ],
        compiler_params=pltpu.CompilerParams(collective_id=1, has_side_effects=True),
        cost_estimate=pl.CostEstimate(
            flops=terms.size, bytes_accessed=2 * terms.size * 4, transcendentals=0
        ),
    )(terms)


def gather_filters(kernel):
    n_sy = lax.axis_size("sy")
    n_af = lax.axis_size("af")
    group = n_sy * n_af
    taps, channels, per_dev = kernel.shape[0] * kernel.shape[1] * kernel.shape[2], kernel.shape[3], kernel.shape[4]
    block = kernel.reshape(-1, 128)
    gathered = pl.pallas_call(
        functools.partial(_gather_body, n_sy, n_af),
        out_shape=jax.ShapeDtypeStruct((group,) + block.shape, block.dtype),
        in_specs=[pl.BlockSpec(memory_space=pltpu.VMEM)],
        out_specs=pl.BlockSpec(memory_space=pltpu.VMEM),
        scratch_shapes=[
            pltpu.SemaphoreType.DMA((group - 1,)),
            pltpu.SemaphoreType.DMA((group - 1,)),
        ],
        compiler_params=pltpu.CompilerParams(collective_id=0, has_side_effects=True),
    )(block)
    gathered = gathered.reshape(group, taps, channels, per_dev).transpose(1, 2, 0, 3)
    return gathered.reshape(kernel.shape[:4] + (group * per_dev,))


def flat_all_to_all(x, axes):
    moved = lax.all_to_all(x.reshape(x.shape[0], 2, -1), axes, 0, 0, tiled=True)
    return moved.reshape(x.shape)


def from_behind(value, axis, steps):
    count = lax.axis_size(axis)
    leading, last = (max(0, -steps), min(count, count - steps))
    return lax.ppermute(value, axis, [(source, source + steps) for source in range(leading, last)])


def strided_patch(extended, tap_d, tap_h, tap_w, depth, height, width):
    return extended[
        :,
        tap_d : tap_d + 2 * depth : 2,
        tap_h : tap_h + 2 * height : 2,
        tap_w : tap_w + 2 * width : 2,
        :,
    ]


def parity_view(extended):
    samples, d_ext, h_ext, w_ext, channels = extended.shape
    pads = [(0, 0)] + [(0, n % 2) for n in (d_ext, h_ext, w_ext)] + [(0, 0)]
    even = jnp.pad(extended, pads)
    _, d2, h2, w2, _ = even.shape
    return even.reshape(samples, d2 // 2, 2, h2 // 2, 2, w2, channels)


def _im2col_body(depth, height, width, x_ref, out_ref):
    channels = x_ref.shape[-1]
    tap = 0
    for tap_d in range(3):
        for tap_h in range(3):
            for tap_w in range(3):
                od, oh = tap_d // 2, tap_h // 2
                for p in range(depth):
                    for q in range(height):
                        row = x_ref[0, od + p, tap_d % 2, oh + q, tap_h % 2, pl.ds(tap_w, width, stride=2), :]
                        out_ref[p, q, :, tap * channels : (tap + 1) * channels] = row.astype(out_ref.dtype)
                tap += 1


def im2col(classes, depth, height, width):
    channels = classes.shape[-1]
    return pl.pallas_call(
        functools.partial(_im2col_body, depth, height, width),
        out_shape=jax.ShapeDtypeStruct((depth, height, width, 27 * channels), classes.dtype),
        in_specs=[pl.BlockSpec(memory_space=pltpu.VMEM)],
        out_specs=pl.BlockSpec(memory_space=pltpu.VMEM),
    )(classes)


def weave(even_part, odd_part, axis):
    stacked = jnp.stack([even_part, odd_part], axis=axis + 1)
    shape = list(even_part.shape)
    shape[axis] = shape[axis] * 2
    return stacked.reshape(shape)


def spread_back(grad_t, kernel_full, samples, depth, height, width):
    filters = grad_t.shape[0]
    channels = kernel_full.shape[3]
    spread = lax.dot_general(
        grad_t,
        kernel_full.reshape(-1, channels, filters),
        (((0,), (2,)), ((), ())),
        preferred_element_type=jnp.float32,
    ).reshape(samples, depth, height, width, 27, channels)
    classes = {}
    for tap_d in range(3):
        for tap_h in range(3):
            for tap_w in range(3):
                term = spread[:, :, :, :, tap_d * 9 + tap_h * 3 + tap_w]
                pads = [(0, 0)]
                for tap in (tap_d, tap_h, tap_w):
                    pads.append((1, 0) if tap == 2 else (0, 1))
                pads.append((0, 0))
                term = jnp.pad(term, pads)
                key_name = (tap_d % 2, tap_h % 2, tap_w % 2)
                classes[key_name] = classes[key_name] + term if key_name in classes else term
    planes = []
    for parity_d in range(2):
        rows_h = []
        for parity_h in range(2):
            rows_h.append(weave(classes[parity_d, parity_h, 0], classes[parity_d, parity_h, 1], 3))
        planes.append(weave(rows_h[0], rows_h[1], 2))
    whole = weave(planes[0], planes[1], 1)
    return whole[:, : 2 * depth + 1, : 2 * height + 1, : 2 * width + 1, :]


def on_device(volume, kernel, cotangent):
    samples = volume.shape[0]
    depth = volume.shape[1] // 2
    height = volume.shape[2] // 2
    width = volume.shape[3] // 2
    n_sy = lax.axis_size("sy")
    n_af = lax.axis_size("af")
    kernel_part = gather_filters(kernel)
    kernel_full = lax.all_gather(kernel_part, "sx", axis=3, tiled=True)
    filters = kernel_full.shape[4]
    per_dev = filters // (n_sy * n_af)
    below = from_behind(volume[:, -1:], "sx", 1)
    n_sx_axis = lax.axis_size("sx")
    corner = lax.ppermute(
        volume[:, -1:, -1:],
        ("sx", "sy"),
        [
            (i * n_sy + j, (i + 1) * n_sy + j + 1)
            for i in range(n_sx_axis - 1)
            for j in range(n_sy - 1)
        ],
    )
    beside = jnp.concatenate([corner, from_behind(volume[:, :, -1:], "sy", 1)], axis=1)
    extended = jnp.concatenate([below, volume], axis=1)
    extended = jnp.concatenate([beside, extended], axis=2)
    extended = jnp.pad(extended, ((0, 0), (0, 0), (0, 0), (1, 0), (0, 0)))
    rows = samples * depth * height * width
    classes = parity_view(extended)
    cols = im2col(classes, depth, height, width).reshape(rows, -1)
    kernel_mat = kernel_full.reshape(-1, filters)
    total = lax.dot_general(
        kernel_mat, cols, (((0,), (1,)), ((), ())), preferred_element_type=jnp.float32
    )
    n_sx = lax.axis_size("sx")
    conv_t = total.astype(jnp.bfloat16).reshape(n_sy, n_af, per_dev, depth, height, width)
    by_af = flat_all_to_all(conv_t.transpose(1, 0, 2, 3, 4, 5), "af")
    by_region = by_af.reshape(n_sx * n_sy, per_dev, depth, height, width)
    gathered = flat_all_to_all(by_region, ("sx", "sy"))
    own_samples = cotangent.shape[0]
    features = (
        gathered.reshape(n_sx, n_sy, per_dev, depth, height, width)
        .transpose(2, 0, 3, 1, 4, 5)
        .reshape(cotangent.shape)
    )
    grad_blocks = (
        cotangent.reshape(per_dev, n_sx, depth, n_sy, height, width)
        .transpose(1, 3, 0, 2, 4, 5)
        .reshape(n_sx * n_sy, per_dev, depth, height, width)
    )
    grad_region = flat_all_to_all(grad_blocks, ("sx", "sy"))
    grad_region = grad_region.reshape(n_sx * own_samples, n_sy, per_dev, depth, height, width)
    grad_back = flat_all_to_all(grad_region, "af")
    grad_t = grad_back.transpose(1, 0, 2, 3, 4, 5).reshape(filters, rows)
    by_parity = grad_t.reshape(n_sy * n_af // 2, 2, per_dev, rows).transpose(1, 0, 2, 3)
    kernel_terms = lax.dot_general(
        by_parity.reshape(filters, rows), cols, (((1,), (0,)), ((), ())),
        preferred_element_type=jnp.float32,
    )
    channels = kernel_full.shape[3]
    own_ch = channels // n_sx
    by_filter = reduce_filters(kernel_terms)
    by_filter = by_filter.reshape(per_dev, 27, n_sx, own_ch).transpose(2, 1, 3, 0)
    kernel_grad = lax.all_to_all(by_filter, "sx", 0, 0, tiled=True).sum(axis=0)
    kernel_grad = kernel_grad.reshape(3, 3, 3, own_ch, per_dev)
    partial_grad = spread_back(grad_t, kernel_full, samples, depth, height, width)
    from_above = from_behind(partial_grad[:, 0:1], "sx", -1)
    own_depth = partial_grad[:, 1:]
    own_depth = jnp.concatenate([own_depth[:, :-1], own_depth[:, -1:] + from_above], axis=1)
    from_right = from_behind(own_depth[:, :, 0:1].astype(jnp.bfloat16), "sy", -1).astype(
        jnp.float32
    )
    own_height = own_depth[:, :, 1:]
    own_height = jnp.concatenate(
        [own_height[:, :, :-1], own_height[:, :, -1:] + from_right], axis=2
    )
    volume_grad = own_height[:, :, :, 1:]
    return (features, volume_grad.astype(jnp.bfloat16), kernel_grad)


def solution(mesh):
    return jax.shard_map(
        on_device,
        mesh=mesh,
        in_specs=(
            P("af", "sx", "sy", None, None),
            P(None, None, None, "sx", ("sy", "af")),
            P("sx", ("sy", "af"), None, None),
        ),
        out_specs=(
            P("sx", ("sy", "af"), None, None),
            P("af", "sx", "sy", None, None),
            P(None, None, None, "sx", ("sy", "af")),
        ),
        check_vma=False,
    )
```
